32 devices in a mesh: wide: 8 (over z, x), narrow: 4 (over y, core).
Axes of the slice: x: 2, y: 2, z: 4, core: 2. Of those that a mesh axis runs over, the one named last changes fastest.
Arguments:
- latents: bfloat16 [128, 32, 32, 384], P('wide', 'narrow'), may hold values from -6 to 6
- timesteps: int32 [128], P('wide'), may hold values from 0 to 999
- out_grad: bfloat16 [128, 16, 16, 768], P(('wide', 'narrow')), may hold values from -6 to 6
- ada_weight: bfloat16 [256, 2304], replicated, may hold values from -1 to 1
- ada_bias: bfloat16 [2304], replicated, may hold values from -4 to 4
- conv_attn: bfloat16 [3, 3, 384], replicated, may hold values from -2 to 2
- qkv_weight: bfloat16 [384, 1152], replicated, may hold values from -0.3125 to 0.3125
- proj_weight: bfloat16 [384, 384], replicated, may hold values from -1.25 to 1.25
- fc1_weight: bfloat16 [384, 1536], replicated, may hold values from -0.3125 to 0.3125
- fc1_bias: bfloat16 [1536], replicated, may hold values from -6 to 6
- conv_ffn: bfloat16 [3, 3, 1536], replicated, may hold values from -2 to 2
- fc2_weight: bfloat16 [1536, 384], replicated, may hold values from -0.15625 to 0.15625
- fc2_bias: bfloat16 [384], replicated, may hold values from -4 to 4
- down_weight: bfloat16 [1536, 768], replicated, may hold values from -0.15625 to 0.15625
- down_bias: bfloat16 [768], replicated, may hold values from -4 to 4
Outputs:
- result: bfloat16 [128, 16, 16, 768], P(('wide', 'narrow'))
- grad_latents: float32 [128, 32, 32, 384], P('wide', 'narrow')
- grad_ada_weight: float32 [256, 2304], replicated
- grad_ada_bias: float32 [2304], replicated
- grad_conv_attn: float32 [3, 3, 384], replicated
- grad_qkv_weight: float32 [384, 1152], replicated
- grad_proj_weight: float32 [384, 384], replicated
- grad_fc1_weight: float32 [384, 1536], replicated
- grad_fc1_bias: float32 [1536], replicated
- grad_conv_ffn: float32 [3, 3, 1536], replicated
- grad_fc2_weight: float32 [1536, 384], replicated
- grad_fc2_bias: float32 [384], replicated
- grad_down_weight: float32 [1536, 768], replicated
- grad_down_bias: float32 [768], replicated
The draws below stay inside these ranges and needn't reach their ends.
All inputs are finite; a program needn't handle non-finite values.
Results may differ from the reference program's by a relative error of at most 0.018.
The reference program's roundings to bfloat16 on the way count: a program that leaves them out, or rounds other values in their place, can miss the bound.
Values may be sent and summed in bfloat16 or wider, within the bound.
No kernel may reach another device: no remote copies, remote signals or barrier semaphores. Data moves between devices by JAX's collectives and lax.ppermute only.
A program may use at most 384 MiB of HBM per device.

```python
import math
import jax
import jax.numpy as jnp
import numpy as np
from jax import lax

D = 384
HEADS = 6
HEAD = 64
FF = 1536
OUT = 768
FREQ = 256
H = 32
W = 32
STEPS = 1000
BATCH = 128


def with_ends(values, stream_key, smallest, high):
    longest = values.shape.index(max(values.shape))
    spots = []
    for shift in (0, 1):
        where = [jax.random.randint(jax.random.fold_in(stream_key, axis), (), 0, length) for axis, length in enumerate(values.shape)]
        where[longest] = (where[longest] + shift) % values.shape[longest]
        spots.append(tuple(where))
    return values.at[spots[0]].set(smallest).at[spots[1]].set(high)


def level_of(rng, shape, cuts, low, high):
    factor_of, own = 1.0, jax.random.fold_in(rng, 6)
    for axis_at, blocks in cuts:
        steps = jnp.exp(jax.random.uniform(jax.random.fold_in(own, axis_at), (blocks,), jnp.float32, low / len(cuts), high / len(cuts)))
        factor_of = factor_of * jnp.repeat(steps, shape[axis_at] // blocks).reshape([-1 if axis == axis_at else 1 for axis in range(len(shape))])
    return factor_of


def rank_table(count, skew):
    weights = [(1 << 20) // math.isqrt(grade ** skew) + 1 for grade in range(1, count + 1)]
    scale = 1 + sum(weights) // (1 << 30)
    return np.cumsum(np.array([max(1, weight // scale) for weight in weights]))


def ranked(key, dims, count, slope):
    table = rank_table(count, slope)
    pick = jax.random.randint(jax.random.fold_in(key, 1), dims, 0, int(table[count - 1]))
    standing = jnp.searchsorted(jnp.asarray(table, jnp.int32), pick, side="right")
    return jax.random.permutation(jax.random.fold_in(key, 2), count)[standing].astype(jnp.int32)


def normal_values(own_key, extent, scale, limit, split=(), kind=jnp.bfloat16):
    values = scale * jax.random.normal(own_key, extent, jnp.float32)
    if split:
        values = values * level_of(own_key, extent, split, -0.22, 0.18)
    return jnp.clip(values, -limit, limit).astype(kind)


def setup_inputs(seed: int = 0) -> dict:
    key_of = jax.random.split(jax.random.key(seed), 16)
    latents = normal_values(key_of[0], (BATCH, H, W, D), 1.0, 6.0, ((0, 8), (1, 4)))
    timesteps = with_ends(ranked(key_of[1], (BATCH,), STEPS, 2), jax.random.fold_in(key_of[1], 3), 0, STEPS - 1).astype(jnp.int32)
    out_grad = normal_values(key_of[2], (BATCH, H // 2, W // 2, OUT), 1.0, 6.0, ((0, 32),))
    ada_weight = normal_values(key_of[3], (FREQ, 6 * D), (FREQ // 8) ** -0.5, 1.0)
    ada_bias = normal_values(key_of[4], (6 * D,), 0.3, 4.0)
    conv_attn = normal_values(key_of[5], (3, 3, D), 9 ** -0.5, 2.0)
    qkv_weight = normal_values(key_of[6], (D, 3 * D), D ** -0.5, 0.3125)
    proj_weight = normal_values(key_of[7], (D, D), (D // 16) ** -0.5, 1.25)
    fc1_weight = normal_values(key_of[8], (D, FF), D ** -0.5, 0.3125)
    fc1_bias = normal_values(key_of[9], (FF,), 0.5, 6.0)
    conv_ffn = normal_values(key_of[10], (3, 3, FF), 9 ** -0.5, 2.0)
    fc2_weight = normal_values(key_of[11], (FF, D), FF ** -0.5, 0.15625)
    fc2_bias = normal_values(key_of[12], (D,), 0.3, 4.0)
    down_weight = normal_values(key_of[13], (4 * D, OUT), (4 * D) ** -0.5, 0.15625)
    down_bias = normal_values(key_of[14], (OUT,), 0.3, 4.0)
    return {"latents": latents, "timesteps": timesteps, "out_grad": out_grad, "ada_weight": ada_weight, "ada_bias": ada_bias, "conv_attn": conv_attn, "qkv_weight": qkv_weight, "proj_weight": proj_weight, "fc1_weight": fc1_weight, "fc1_bias": fc1_bias, "conv_ffn": conv_ffn, "fc2_weight": fc2_weight, "fc2_bias": fc2_bias, "down_weight": down_weight, "down_bias": down_bias}


EPSILON = 1e-06
HIGH = lax.Precision.HIGHEST

@jax.custom_vjp
def low(v):
    return lax.optimization_barrier(v.astype(jnp.bfloat16)).astype(jnp.float32)

@jax.custom_vjp
def low_back(v):
    return v

def low_keep(v):
    return (low(v), None)

def low_pass(kept, grad):
    return (grad,)

def back_keep(v):
    return (v, None)

def back_low(kept, grad):
    return (low(grad),)
low.defvjp(low_keep, low_pass)
low_back.defvjp(back_keep, back_low)

def timestep_features(steps_in, feature_count):
    half_count = feature_count // 2
    freq_table = jnp.exp(-math.log(10000.0) * jnp.arange(half_count, dtype=jnp.float32) / half_count)
    angles = steps_in.astype(jnp.float32)[:, None] * freq_table[None, :]
    return jnp.concatenate([jnp.cos(angles), jnp.sin(angles)], axis=1)

def layer_norm(values):
    center = values - lax.optimization_barrier(jnp.mean(values, axis=-1, keepdims=True))
    spread = lax.optimization_barrier(jnp.mean(center * center, axis=-1, keepdims=True))
    return center * lax.rsqrt(spread + EPSILON)

def modulate_norm(values, shift_part, scale_part):
    return layer_norm(values) * (1.0 + scale_part) + shift_part

def gelu_tanh(values):
    return jax.nn.gelu(values, approximate=True)

def pad_rows(values):
    return jnp.pad(values, ((0, 0), (1, 1), (0, 0), (0, 0)))

def depth_conv(row_padded, kernel):
    row_count = row_padded.shape[1] - 2
    col_count = row_padded.shape[2]
    padded = jnp.pad(row_padded, ((0, 0), (0, 0), (1, 1), (0, 0)))
    total = jnp.zeros((row_padded.shape[0], row_count, col_count, row_padded.shape[3]), jnp.float32)
    for row_tap in range(3):
        for col_tap in range(3):
            window = padded[:, row_tap:row_tap + row_count, col_tap:col_tap + col_count, :].astype(jnp.float32)
            total = total + window * kernel[row_tap, col_tap].astype(jnp.float32)
    return total

def to_groups(values, head_count):
    batch_size, row_count, col_count, channels = values.shape
    head_size = channels // head_count
    shaped = values.reshape(batch_size, row_count // 2, 2, col_count // 2, 2, head_count, head_size)
    shaped = shaped.transpose(0, 2, 4, 5, 1, 3, 6)
    return shaped.reshape(batch_size, 4, head_count, row_count // 2 * (col_count // 2), head_size)

def from_groups(values, row_count, col_count):
    batch_size = values.shape[0]
    head_count = values.shape[2]
    head_size = values.shape[4]
    shaped = values.reshape(batch_size, 2, 2, head_count, row_count // 2, col_count // 2, head_size)
    shaped = shaped.transpose(0, 4, 1, 5, 2, 3, 6)
    return shaped.reshape(batch_size, row_count, col_count, head_count * head_size)

def unshuffle(values):
    batch_size, row_count, col_count, channels = values.shape
    shaped = values.reshape(batch_size, row_count // 2, 2, col_count // 2, 2, channels)
    return shaped.transpose(0, 1, 3, 2, 4, 5).reshape(batch_size, row_count // 2, col_count // 2, 4 * channels)

def matmul(left_side, right_side):
    return jnp.einsum('...i,ij->...j', left_side, right_side, precision=HIGH)

def block_forward(params, tokens, cond_rows):
    ada_weight, ada_bias, conv_attn, qkv_weight, proj_weight, fc1_weight, fc1_bias, conv_ffn, fc2_weight, fc2_bias, down_weight, down_bias = params
    channels = tokens.shape[3]
    row_count = tokens.shape[1]
    col_count = tokens.shape[2]
    modulation = jnp.dot(cond_rows, ada_weight, precision=HIGH) + ada_bias
    pieces = [modulation[:, None, None, part_index * channels:(part_index + 1) * channels] for part_index in range(6)]
    shift_one, scale_one, gate_one, shift_two, scale_two, gate_two = pieces
    hidden_in = low(modulate_norm(tokens, shift_one, scale_one))
    conv_out = low(low_back(depth_conv(pad_rows(hidden_in), conv_attn)))
    qkv_all = matmul(conv_out, qkv_weight)
    queries = low(low_back(qkv_all[..., :channels]))
    keys_part = low(low_back(qkv_all[..., channels:2 * channels]))
    values_part = low(low_back(qkv_all[..., 2 * channels:]))
    factor = HEAD ** (-0.5)
    q_groups = to_groups(queries, HEADS)
    k_groups = to_groups(keys_part, HEADS)
    v_groups = to_groups(values_part, HEADS)
    scores = low_back(jnp.einsum('bghqe,bghke->bghqk', q_groups, k_groups, precision=HIGH) * factor)
    top_score = lax.optimization_barrier(jnp.max(scores, axis=-1, keepdims=True))
    log_total = top_score + jnp.log(lax.optimization_barrier(jnp.sum(jnp.exp(scores - top_score), axis=-1, keepdims=True)))
    probs = low(jnp.exp(scores - log_total))
    mixed_groups = jnp.einsum('bghqk,bghke->bghqe', probs, v_groups, precision=HIGH)
    mixed = low(low_back(from_groups(mixed_groups, row_count, col_count)))
    attn_out = low_back(matmul(mixed, proj_weight))
    after_attn = tokens + gate_one * attn_out
    hidden_two = low(modulate_norm(after_attn, shift_two, scale_two))
    ffn_pre = low(low_back(matmul(hidden_two, fc1_weight) + fc1_bias))
    ffn_conv = low_back(depth_conv(pad_rows(ffn_pre), conv_ffn))
    activated = low(gelu_tanh(ffn_conv))
    ffn_out = low_back(matmul(activated, fc2_weight) + fc2_bias)
    after_ffn = after_attn + gate_two * ffn_out
    low_res = low(unshuffle(after_ffn))
    return matmul(low_res, down_weight) + down_bias

def reference(latents, timesteps, out_grad, ada_weight, ada_bias, conv_attn, qkv_weight, proj_weight, fc1_weight, fc1_bias, conv_ffn, fc2_weight, fc2_bias, down_weight, down_bias):
    params = tuple((tensor.astype(jnp.float32) for tensor in (ada_weight, ada_bias, conv_attn, qkv_weight, proj_weight, fc1_weight, fc1_bias, conv_ffn, fc2_weight, fc2_bias, down_weight, down_bias)))
    cond_all = low(jax.nn.silu(timestep_features(timesteps, FREQ)))
    block_images = math.gcd(BATCH, 4)
    block_count = BATCH // block_images
    token_blocks = latents.astype(jnp.float32).reshape(block_count, block_images, H, W, D)
    cond_blocks = cond_all.reshape(block_count, block_images, FREQ)
    grad_blocks = out_grad.astype(jnp.float32).reshape(block_count, block_images, H // 2, W // 2, OUT)

    def accumulate(totals, pieces):
        tokens_blk, cond_blk, grad_blk = pieces
        result_blk, back_fn = jax.vjp(lambda params_in, values_in: block_forward(params_in, values_in, cond_blk), params, tokens_blk)
        grad_params, grad_tokens = back_fn(grad_blk)
        totals = jax.tree.map(lambda running, adding: running + adding, totals, grad_params)
        return (totals, (result_blk, grad_tokens))
    initial = tuple((jnp.zeros_like(tensor) for tensor in params))
    totals, (results, grad_all) = lax.scan(accumulate, initial, (token_blocks, cond_blocks, grad_blocks))
    result = results.reshape(BATCH, H // 2, W // 2, OUT).astype(jnp.bfloat16)
    grad_latents = grad_all.reshape(BATCH, H, W, D)
    return (result, grad_latents, totals[0], totals[1], totals[2], totals[3], totals[4], totals[5], totals[6], totals[7], totals[8], totals[9], totals[10], totals[11])
```

```python
import functools
import math

import jax
import jax.numpy as jnp
from jax import lax
from jax.experimental import pallas as pl
from jax.experimental.pallas import tpu as pltpu
from jax.sharding import PartitionSpec as P

HEADS = 6
EPSILON = 1e-06
HIGH = lax.Precision.HIGHEST
BF = jnp.bfloat16
F32 = jnp.float32
NN = ((1,), (0,))
NT = ((1,), (1,))
TN = ((0,), (0,))
LANES = 128
CHUNK = 256
GELU_A = math.sqrt(2.0 / math.pi)
GELU_B = 0.044715
AXES = ("wide", "narrow")


def mm(left, right, dims=NN):
    return lax.dot_general(left, right, (dims, ((), ())), preferred_element_type=F32)


def col_sum(values):
    return jnp.sum(values, axis=0, keepdims=True)


def row_mean(values):
    return jnp.mean(values, axis=1, keepdims=True)


def normed(values):
    center = values - row_mean(values)
    spread = row_mean(center * center)
    inverse = lax.rsqrt(spread + EPSILON)
    return center * inverse, inverse


def norm_back(grad_normed, normed_values, inverse):
    return inverse * (
        grad_normed - row_mean(grad_normed) - normed_values * row_mean(grad_normed * normed_values)
    )


def tap_source(phase, tap):
    distance = phase + tap - 1
    return distance % 2, distance // 2


def tap_ref(plain, moved, row_phase, col_phase, row_tap, col_tap, cols, start, size, lanes):
    source_row, row_move = tap_source(row_phase, row_tap)
    source_col, col_move = tap_source(col_phase, col_tap)
    held = plain if col_move == 0 else moved
    return held[2 * source_row + source_col, pl.ds(cols + cols * row_move + start, size), lanes]


def fill_planes(plain, moved, plane, col_phase_matrix, values_low, cols, lanes):
    tokens = values_low.shape[0]
    plain[plane, pl.ds(cols, tokens), lanes] = values_low.astype(F32)
    moved[plane, pl.ds(cols, tokens), lanes] = mm(col_phase_matrix, values_low)


def conv_tile(plain, moved, weight, row_phase, col_phase, cols, start, size, lanes, lanes_weight):
    total = None
    for row_tap in range(3):
        for col_tap in range(3):
            window = tap_ref(
                plain, moved, row_phase, col_phase, row_tap, col_tap, cols, start, size, lanes
            )
            part = window * weight[pl.ds(row_tap * 3 + col_tap, 1), lanes_weight]
            total = part if total is None else total + part
    return total


def conv_back_tile(
    plain, moved, weight, inputs, kernel_grad, row_phase, col_phase, cols, start, size, lanes, lanes_weight
):
    total = None
    for row_tap in range(3):
        for col_tap in range(3):
            window = tap_ref(
                plain, moved, row_phase, col_phase, row_tap, col_tap, cols, start, size, lanes
            )
            mirror = (2 - row_tap) * 3 + (2 - col_tap)
            part = window * weight[pl.ds(mirror, 1), lanes_weight]
            total = part if total is None else total + part
            product = jnp.sum((window * inputs).reshape(size // 8, 8, LANES), axis=0)
            kernel_grad[mirror, :, lanes_weight] += product
    return total


def zero_pads(buffer, cols):
    planes, padded, width = buffer.shape
    edge = jnp.zeros((planes, cols, width), F32)
    buffer[:, pl.ds(0, cols), :] = edge
    buffer[:, pl.ds(padded - cols, cols), :] = edge


def forward_kernel(
    x_ref,
    mod_ref,
    og_ref,
    qkv_w,
    proj_w,
    fc1_w,
    fc1_b,
    fc2_w,
    fc2_b,
    down_w,
    down_b,
    conv_a,
    conv_f,
    perm,
    moves,
    res_ref,
    gmid_ref,
    xp_ref,
    co_ref,
    qkv_ref,
    mix_ref,
    stat_ref,
    gmod_ref,
    d_fc1,
    d_fc2t,
    d_downt,
    d_conv,
    d_fc1b,
    d_fc2b,
    d_downb,
    plain_h,
    moved_h,
    plain_g,
    moved_g,
    attn_s,
    gaft_s,
    gffn_s,
    hid_s,
    act_s,
    gpre_s,
    gact_s,
    gconv_s,
    low_s,
    fout_s,
    dconv_s,
):
    image = pl.program_id(0)
    tokens = perm.shape[0]
    cols = (stat_ref.shape[3] // 16)
    width = x_ref.shape[2]
    hidden = fc1_w.shape[1]
    quarter = tokens // 4
    blocks = x_ref.shape[1] // tokens
    all_lanes = pl.ds(0, width)

    @pl.when(image == 0)
    def _():
        for ref in (d_fc1, d_fc2t, d_downt, d_conv, d_fc1b, d_fc2b, d_downb):
            ref[...] = jnp.zeros(ref.shape, F32)
        dconv_s[...] = jnp.zeros(dconv_s.shape, F32)
        for ref in (plain_h, moved_h, plain_g, moved_g):
            zero_pads(ref, cols)

    gmod_ref[...] = jnp.zeros(gmod_ref.shape, F32)
    shift_one, scale_one, gate_one, shift_two, scale_two, gate_two = (
        mod_ref[0, pl.ds(part, 1), :] for part in range(6)
    )

    for block in range(blocks):
        moved_block = mm(perm[...], x_ref[0, pl.ds(block * tokens, tokens), :]).astype(BF)
        for plane in range(4):
            xp_ref[0, pl.ds(plane * tokens + block * quarter, quarter), :] = moved_block[
                plane * quarter : (plane + 1) * quarter
            ]

    for plane in range(4):
        unit, _ = normed(xp_ref[0, pl.ds(plane * tokens, tokens), :].astype(F32))
        low = (unit * (1.0 + scale_one) + shift_one).astype(BF)
        fill_planes(plain_h, moved_h, plane, moves[plane % 2], low, cols, all_lanes)
    for plane in range(4):
        for lane in range(0, width, LANES):
            for start in range(0, tokens, 128):
                lanes = pl.ds(lane, LANES)
                total = conv_tile(
                    plain_h, moved_h, conv_a, plane // 2, plane % 2, cols, start, 128, lanes, lanes
                )
                co_ref[0, pl.ds(plane * tokens + start, 128), lanes] = total.astype(BF)

    head_size = width // HEADS
    factor = head_size ** (-0.5)

    def attend(plane, carry):
        rows = pl.ds(pl.multiple_of(plane * tokens, tokens), tokens)
        qkv_ref[0, rows, :] = mm(co_ref[0, rows, :], qkv_w[...]).astype(BF)
        even = lax.broadcasted_iota(jnp.int32, (tokens, LANES), 1) < head_size
        for pair in range(width // LANES):
            lane = pair * LANES
            query = qkv_ref[0, rows, pl.ds(lane, LANES)]
            key = qkv_ref[0, rows, pl.ds(width + lane, LANES)] * jnp.asarray(factor, BF)
            value_t = qkv_ref[0, rows, pl.ds(2 * width + lane, LANES)].T
            parts = []
            for half in range(2):
                mine = even if half == 0 else ~even
                key_head = jnp.where(mine, key, jnp.zeros_like(key))
                scores = mm(key_head, query, NT)
                top = jnp.max(scores, axis=0, keepdims=True)
                grown = jnp.exp(scores - top)
                total = col_sum(grown)
                stat_ref[0, plane, pl.ds(2 * pair + half, 1), :] = top + jnp.log(total)
                probs = (grown * (1.0 / total)).astype(BF)
                parts.append(mm(value_t[half * head_size : (half + 1) * head_size], probs))
            mixed_t = jnp.concatenate(parts, axis=0).astype(BF)
            mix_ref[0, rows, pl.ds(lane, LANES)] = mixed_t.T
        attn_s[rows, :] = mm(mix_ref[0, rows, :], proj_w[...])
        return carry

    lax.fori_loop(0, 4, attend, 0)

    grad_low = og_ref[0]
    d_downb[...] += col_sum(grad_low.astype(F32))
    for plane in range(4):
        rows = pl.ds(plane * tokens, tokens)
        grad_after = mm(grad_low, down_w[pl.ds(plane * width, width), :], NT)
        gaft_s[rows, :] = grad_after
        grad_out = (gate_two * grad_after).astype(BF)
        gffn_s[rows, :] = grad_out
        d_fc2b[...] += col_sum(grad_out.astype(F32))
        after = xp_ref[0, rows, :].astype(F32) + gate_one * attn_s[rows, :]
        unit, _ = normed(after)
        hid_s[rows, :] = (unit * (1.0 + scale_two) + shift_two).astype(BF)

    chunk_lanes = pl.ds(0, CHUNK)

    def feed(chunk, carry):
        offset = pl.multiple_of(chunk * CHUNK, CHUNK)
        units = pl.ds(offset, CHUNK)
        for plane in range(4):
            rows = pl.ds(plane * tokens, tokens)
            pre = (mm(hid_s[rows, :], fc1_w[:, units]) + fc1_b[:, units]).astype(BF)
            fill_planes(plain_h, moved_h, plane, moves[plane % 2], pre, cols, chunk_lanes)
            gact_s[rows, :] = mm(gffn_s[rows, :], fc2_w[units, :], NT)
        for plane in range(4):
            for lane in range(0, CHUNK, LANES):
                lanes = pl.ds(lane, LANES)
                here = pl.ds(pl.multiple_of(offset + lane, LANES), LANES)
                for start in range(0, tokens, 128):
                    rows = pl.ds(plane * tokens + start, 128)
                    value = conv_tile(
                        plain_h, moved_h, conv_f, plane // 2, plane % 2, cols, start, 128, lanes, here
                    )
                    square = value * value
                    bent = jnp.tanh(value * (GELU_A + (GELU_A * GELU_B) * square))
                    halved = 0.5 * value
                    act_s[rows, here] = (halved + halved * bent).astype(BF)
                    slope = 0.5 + 0.5 * bent + halved * (1.0 - bent * bent) * (
                        GELU_A + (3.0 * GELU_A * GELU_B) * square
                    )
                    gconv_s[rows, lanes] = (slope * gact_s[rows, lanes]).astype(BF)
        for plane in range(4):
            fill_planes(
                plain_g,
                moved_g,
                plane,
                moves[plane % 2],
                gconv_s[pl.ds(plane * tokens, tokens), :],
                cols,
                chunk_lanes,
            )
        for plane in range(4):
            for lane in range(0, CHUNK, LANES):
                lanes = pl.ds(lane, LANES)
                here = pl.ds(pl.multiple_of(offset + lane, LANES), LANES)
                for start in range(0, tokens, 128):
                    rows = pl.ds(plane * tokens + start, 128)
                    inputs = plain_h[plane, pl.ds(cols + start, 128), lanes]
                    total = conv_back_tile(
                        plain_g,
                        moved_g,
                        conv_f,
                        inputs,
                        dconv_s,
                        plane // 2,
                        plane % 2,
                        cols,
                        start,
                        128,
                        lanes,
                        here,
                    )
                    low = total.astype(BF)
                    gpre_s[rows, here] = low
                    d_fc1b[:, here] += col_sum(low.astype(F32))
        return carry

    lax.fori_loop(0, hidden // CHUNK, feed, 0)

    hid_t = hid_s[...].T
    gffn_t = gffn_s[...].T

    def weights(chunk, carry):
        units = pl.ds(pl.multiple_of(chunk * CHUNK, CHUNK), CHUNK)
        d_fc1[:, units] += mm(hid_t, gpre_s[:, units])
        d_fc2t[:, units] += mm(gffn_t, act_s[:, units])
        return carry

    lax.fori_loop(0, hidden // CHUNK, weights, 0)

    grad_gate_one = grad_shift_two = grad_scale_two = grad_gate_two = jnp.zeros((1, width), F32)
    for plane in range(4):
        rows = pl.ds(plane * tokens, tokens)
        attn = attn_s[rows, :]
        after = xp_ref[0, rows, :].astype(F32) + gate_one * attn
        grad_after = gaft_s[rows, :]
        out = mm(act_s[rows, :], fc2_w[...]) + fc2_b[...]
        grad_gate_two += col_sum(out * grad_after)
        low_s[:, pl.ds(plane * width, width)] = (after + gate_two * out).astype(BF)
        grad_hid = mm(gpre_s[rows, :], fc1_w[...], NT)
        unit, inverse = normed(after)
        grad_shift_two += col_sum(grad_hid)
        grad_scale_two += col_sum(grad_hid * unit)
        grad_mid = grad_after + norm_back(grad_hid * (1.0 + scale_two), unit, inverse)
        gmid_ref[0, rows, :] = grad_mid
        grad_gate_one += col_sum(attn * grad_mid)
    gmod_ref[0, pl.ds(0, 1), :] = grad_gate_one
    gmod_ref[0, pl.ds(1, 1), :] = grad_shift_two
    gmod_ref[0, pl.ds(2, 1), :] = grad_scale_two
    gmod_ref[0, pl.ds(3, 1), :] = grad_gate_two

    res_ref[0] = (mm(low_s[...], down_w[...]) + down_b[...]).astype(BF)
    grad_low_t = grad_low.T

    def down_weights(chunk, carry):
        units = pl.ds(pl.multiple_of(chunk * CHUNK, CHUNK), CHUNK)
        d_downt[:, units] += mm(grad_low_t, low_s[:, units])
        return carry

    lax.fori_loop(0, low_s.shape[1] // CHUNK, down_weights, 0)

    @pl.when(image == pl.num_programs(0) - 1)
    def _():
        for tap in range(9):
            d_conv[pl.ds(tap, 1), :] = col_sum(dconv_s[tap])


def backward_kernel(
    xp_ref,
    mod_ref,
    gmid_ref,
    co_ref,
    qkv_ref,
    mix_ref,
    stat_ref,
    qkv_w,
    proj_w,
    conv_a,
    perm_back,
    moves,
    out_ref,
    gmod_ref,
    d_qkv,
    d_proj,
    d_conv,
    plain_h,
    plain_g,
    moved_g,
    gout_s,
    gmix_s,
    gqkv_s,
    glat_s,
    dconv_s,
):
    image = pl.program_id(0)
    tokens = perm_back.shape[0]
    cols = stat_ref.shape[3] // 16
    width = mix_ref.shape[2]
    quarter = tokens // 4
    blocks = mix_ref.shape[1] // tokens
    all_lanes = pl.ds(0, width)

    @pl.when(image == 0)
    def _():
        for ref in (d_qkv, d_proj, d_conv):
            ref[...] = jnp.zeros(ref.shape, F32)
        dconv_s[...] = jnp.zeros(dconv_s.shape, F32)
        for ref in (plain_g, moved_g):
            zero_pads(ref, cols)

    gmod_ref[...] = jnp.zeros(gmod_ref.shape, F32)
    shift_one, scale_one, gate_one = (mod_ref[0, pl.ds(part, 1), :] for part in range(3))
    head_size = width // HEADS
    factor = jnp.asarray(head_size ** (-0.5), BF)

    def attend(plane, carry):
        rows = pl.ds(pl.multiple_of(plane * tokens, tokens), tokens)
        grad_out = (gate_one * gmid_ref[0, rows, :]).astype(BF)
        gout_s[rows, :] = grad_out
        gmix_s[...] = mm(grad_out, proj_w[...], NT).astype(BF)
        even = lax.broadcasted_iota(jnp.int32, (tokens, LANES), 1) < head_size
        for pair in range(width // LANES):
            lane = pair * LANES
            query = qkv_ref[0, rows, pl.ds(lane, LANES)]
            key = qkv_ref[0, rows, pl.ds(width + lane, LANES)] * factor
            value = qkv_ref[0, rows, pl.ds(2 * width + lane, LANES)]
            query_low = query * factor
            key_t = key.T
            grad_mixed = gmix_s[:, pl.ds(lane, LANES)]
            zero = jnp.zeros_like(key)
            grad_value = grad_key = None
            parts = []
            for half in range(2):
                mine = even if half == 0 else ~even
                scores = mm(jnp.where(mine, key, zero), query, NT)
                probs = jnp.exp(scores - stat_ref[0, plane, pl.ds(2 * pair + half, 1), :])
                grad_probs = mm(jnp.where(mine, value, zero), grad_mixed, NT)
                weighted = probs * grad_probs
                grad_scores = (weighted - probs * col_sum(weighted)).astype(BF)
                one = mm(probs.astype(BF), jnp.where(mine, grad_mixed, zero))
                two = mm(grad_scores, jnp.where(mine, query_low, zero))
                grad_value = one if half == 0 else grad_value + one
                grad_key = two if half == 0 else grad_key + two
                parts.append(mm(key_t[half * head_size : (half + 1) * head_size], grad_scores))
            gqkv_s[rows, pl.ds(lane, LANES)] = jnp.concatenate(parts, axis=0).astype(BF).T
            gqkv_s[rows, pl.ds(width + lane, LANES)] = grad_key.astype(BF)
            gqkv_s[rows, pl.ds(2 * width + lane, LANES)] = grad_value.astype(BF)
        return carry

    lax.fori_loop(0, 4, attend, 0)

    d_proj[...] += mm(mix_ref[0].T, gout_s[...])
    conv_t = co_ref[0].T
    for part in range(3):
        lanes = pl.ds(part * width, width)
        d_qkv[:, lanes] += mm(conv_t, gqkv_s[:, lanes])
    for plane in range(4):
        rows = pl.ds(plane * tokens, tokens)
        grad_conv = mm(gqkv_s[rows, :], qkv_w[...], NT).astype(BF)
        fill_planes(plain_g, moved_g, plane, moves[plane % 2], grad_conv, cols, all_lanes)
        unit, _ = normed(xp_ref[0, rows, :].astype(F32))
        low = (unit * (1.0 + scale_one) + shift_one).astype(BF)
        plain_h[rows, :] = low.astype(F32)
    for plane in range(4):
        for lane in range(0, width, LANES):
            for start in range(0, tokens, 128):
                lanes = pl.ds(lane, LANES)
                rows = pl.ds(plane * tokens + start, 128)
                total = conv_back_tile(
                    plain_g,
                    moved_g,
                    conv_a,
                    plain_h[rows, lanes],
                    dconv_s,
                    plane // 2,
                    plane % 2,
                    cols,
                    start,
                    128,
                    lanes,
                    lanes,
                )
                glat_s[rows, lanes] = total
    grad_shift = grad_scale = jnp.zeros((1, width), F32)
    for plane in range(4):
        rows = pl.ds(plane * tokens, tokens)
        grad_hid = glat_s[rows, :]
        unit, inverse = normed(xp_ref[0, rows, :].astype(F32))
        grad_shift += col_sum(grad_hid)
        grad_scale += col_sum(grad_hid * unit)
        gout_s[rows, :] = (
            gmid_ref[0, rows, :] + norm_back(grad_hid * (1.0 + scale_one), unit, inverse)
        ).astype(BF)
    gmod_ref[0, pl.ds(0, 1), :] = grad_shift
    gmod_ref[0, pl.ds(1, 1), :] = grad_scale
    for block in range(blocks):
        gathered = jnp.concatenate(
            [gout_s[pl.ds(plane * tokens + block * quarter, quarter), :] for plane in range(4)], axis=0
        )
        out_ref[0, pl.ds(block * tokens, tokens), :] = mm(perm_back[...], gathered).astype(BF)

    @pl.when(image == pl.num_programs(0) - 1)
    def _():
        for tap in range(9):
            d_conv[pl.ds(tap, 1), :] = col_sum(dconv_s[tap])


def per_image(shape):
    rest = len(shape) - 1
    return pl.BlockSpec((1,) + tuple(shape[1:]), lambda b: (b,) + (0,) * rest)


def resident(shape):
    rank = len(shape)
    return pl.BlockSpec(tuple(shape), lambda b: (0,) * rank, pipeline_mode=pl.Buffered(1))


def out_of(shape, dtype):
    return jax.ShapeDtypeStruct(shape, dtype)


PARAMS = pltpu.CompilerParams(
    dimension_semantics=("arbitrary",), vmem_limit_bytes=63 * 1024 * 1024
)


def token_tables(cols):
    tokens = (cols // 2) ** 2
    half = cols // 2
    spot = jnp.arange(tokens)
    from_row, from_col = spot // cols, spot % cols
    quarter = tokens // 4
    target = ((from_row % 2) * 2 + from_col % 2) * quarter + (from_row // 2) * half + from_col // 2
    perm_back = (target[:, None] == spot[None, :]).astype(BF)
    perm = (spot[:, None] == target[None, :]).astype(BF)
    ahead = ((spot[None, :] == spot[:, None] + 1) & (spot[:, None] % half != half - 1)).astype(BF)
    behind = ((spot[None, :] == spot[:, None] - 1) & (spot[:, None] % half != 0)).astype(BF)
    return perm, perm_back, jnp.stack([ahead, behind])


def forward_call(x, mod, og, weights, perm, moves):
    qkv_w, proj_w, fc1_w, fc1_b, fc2_w, fc2_b, down_w, down_b, conv_a, conv_f = weights
    images, all_tokens, width = x.shape
    tokens = perm.shape[0]
    cols = 16
    hidden = fc1_w.shape[1]
    padded = tokens + 2 * cols
    shared = (qkv_w, proj_w, fc1_w, fc1_b, fc2_w, fc2_b, down_w, down_b, conv_a, conv_f, perm, moves)
    outs = [
        (og.shape[:2] + (down_w.shape[1],), BF),
        (x.shape, F32),
        (x.shape, BF),
        (x.shape, BF),
        (x.shape[:2] + (3 * width,), BF),
        (x.shape, BF),
        ((images, 4, 8, tokens), F32),
        ((images, 8, width), F32),
    ]
    sums = [
        (width, hidden),
        (width, hidden),
        (down_w.shape[1], down_w.shape[0]),
        (16, hidden),
        (1, hidden),
        (1, width),
        (1, down_w.shape[1]),
    ]
    return pl.pallas_call(
        forward_kernel,
        grid=(images,),
        in_specs=[per_image(x.shape), per_image(mod.shape), per_image(og.shape)]
        + [resident(w.shape) for w in shared],
        out_specs=[per_image(s) for s, _ in outs] + [resident(s) for s in sums],
        out_shape=[out_of(s, d) for s, d in outs] + [out_of(s, F32) for s in sums],
        scratch_shapes=[
            pltpu.VMEM((4, padded, width), F32),
            pltpu.VMEM((4, padded, width), F32),
            pltpu.VMEM((4, padded, CHUNK), F32),
            pltpu.VMEM((4, padded, CHUNK), F32),
            pltpu.VMEM((all_tokens, width), F32),
            pltpu.VMEM((all_tokens, width), F32),
            pltpu.VMEM((all_tokens, width), BF),
            pltpu.VMEM((all_tokens, width), BF),
            pltpu.VMEM((all_tokens, hidden), BF),
            pltpu.VMEM((all_tokens, hidden), BF),
            pltpu.VMEM((all_tokens, CHUNK), F32),
            pltpu.VMEM((all_tokens, CHUNK), BF),
            pltpu.VMEM((tokens, 4 * width), BF),
            pltpu.VMEM((8, LANES), F32),
            pltpu.VMEM((9, 8, hidden), F32),
        ],
        compiler_params=PARAMS,
        name="block_forward",
    )(x, mod, og, *shared)


def backward_call(xp, mod, gmid, co, qkv, mix, stat, weights, perm_back, moves):
    qkv_w, proj_w, conv_a = weights
    images, all_tokens, width = xp.shape
    tokens = perm_back.shape[0]
    padded = tokens + 2 * 16
    shared = (qkv_w, proj_w, conv_a, perm_back, moves)
    per = (xp, mod, gmid, co, qkv, mix, stat)
    outs = [(xp.shape, BF), ((images, 8, width), F32)]
    sums = [(width, 3 * width), (width, width), (16, width)]
    return pl.pallas_call(
        backward_kernel,
        grid=(images,),
        in_specs=[per_image(v.shape) for v in per] + [resident(w.shape) for w in shared],
        out_specs=[per_image(s) for s, _ in outs] + [resident(s) for s in sums],
        out_shape=[out_of(s, d) for s, d in outs] + [out_of(s, F32) for s in sums],
        scratch_shapes=[
            pltpu.VMEM((all_tokens, width), F32),
            pltpu.VMEM((4, padded, width), F32),
            pltpu.VMEM((4, padded, width), F32),
            pltpu.VMEM((all_tokens, width), BF),
            pltpu.VMEM((tokens, width), BF),
            pltpu.VMEM((all_tokens, 3 * width), BF),
            pltpu.VMEM((all_tokens, width), F32),
            pltpu.VMEM((9, 8, width), F32),
        ],
        compiler_params=PARAMS,
        name="block_backward",
    )(*per, *shared)


def exchange(values, axis, step):
    count = lax.axis_size(axis)
    return lax.ppermute(values, axis, [(i, i ^ step) for i in range(count)])


def upper(axis, step):
    return (lax.axis_index(axis) // step) % 2 == 1


def stages():
    found = []
    for axis in ("narrow", "wide"):
        step = 1
        while step < lax.axis_size(axis):
            found.append((axis, step))
            step *= 2
    return found


def scatter_sum(values, order):
    for axis, step in order:
        half = values.shape[0] // 2
        low, high = values[:half], values[half:]
        top = upper(axis, step)
        sent = jnp.where(top, low, high).astype(BF)
        values = jnp.where(top, high, low).astype(F32) + exchange(sent, axis, step).astype(F32)
    return values


def gather_back(values, order):
    for axis, step in reversed(order):
        other = exchange(values, axis, step)
        top = upper(axis, step)
        values = jnp.concatenate(
            [jnp.where(top, other, values), jnp.where(top, values, other)], axis=0
        )
    return values


def total_of(parts):
    order = stages()
    devices = lax.axis_size("wide") * lax.axis_size("narrow")
    row = 1024
    flat = jnp.concatenate([p.reshape(-1) for p in parts])
    count = flat.shape[0]
    unit = devices * row * 8
    padded = -(-count // unit) * unit
    flat = jnp.pad(flat, (0, padded - count)).reshape(-1, row)
    flat = gather_back(scatter_sum(flat, order).astype(BF), order).reshape(-1).astype(F32)
    found, at = [], 0
    for p in parts:
        found.append(flat[at : at + p.size].reshape(p.shape))
        at += p.size
    return found


def shards(
    latents,
    timesteps,
    out_grad,
    ada_weight,
    ada_bias,
    conv_attn,
    qkv_weight,
    proj_weight,
    fc1_weight,
    fc1_bias,
    conv_ffn,
    fc2_weight,
    fc2_bias,
    down_weight,
    down_bias,
):
    images, height, cols, width = out_grad.shape[0], *latents.shape[1:3], latents.shape[3]
    height = height * lax.axis_size("narrow")
    x = lax.all_to_all(latents, "narrow", split_axis=0, concat_axis=1, tiled=True)
    x = x.reshape(images, height * cols, width)
    own_steps = lax.dynamic_slice_in_dim(timesteps, lax.axis_index("narrow") * images, images)
    half_count = ada_weight.shape[0] // 2
    freq = jnp.exp(-math.log(10000.0) * jnp.arange(half_count, dtype=F32) / half_count)
    angles = own_steps.astype(F32)[:, None] * freq[None, :]
    features = jnp.concatenate([jnp.cos(angles), jnp.sin(angles)], axis=1)
    cond = jax.nn.silu(features).astype(BF)
    mod = jnp.dot(cond, ada_weight, preferred_element_type=F32) + ada_bias.astype(F32)
    mod = jnp.pad(mod.reshape(images, 6, width), ((0, 0), (0, 2), (0, 0)))
    perm, perm_back, moves = token_tables(cols)
    conv_a = jnp.pad(conv_attn.reshape(9, width).astype(F32), ((0, 7), (0, 0)))
    hidden = fc1_weight.shape[1]
    conv_f = jnp.pad(conv_ffn.reshape(9, hidden).astype(F32), ((0, 7), (0, 0)))
    low = out_grad.reshape(images, height * cols // 4, out_grad.shape[3])
    res, gmid, xp, co, qkv, mix, stat, gmod_two, d_fc1, d_fc2t, d_downt, d_cf, d_fc1b, d_fc2b, d_downb = forward_call(
        x,
        mod,
        low,
        (
            qkv_weight,
            proj_weight,
            fc1_weight,
            fc1_bias.astype(F32)[None],
            fc2_weight,
            fc2_bias.astype(F32)[None],
            down_weight,
            down_bias.astype(F32)[None],
            conv_a,
            conv_f,
        ),
        perm,
        moves,
    )
    first = total_of([d_fc1, d_fc2t, d_downt, d_cf[:9], d_fc1b, d_fc2b, d_downb])
    glat, gmod_one, d_qkv, d_proj, d_ca = backward_call(
        xp, mod, gmid, co, qkv, mix, stat, (qkv_weight, proj_weight, conv_a), perm_back, moves
    )
    grad_latents = lax.all_to_all(
        glat.reshape(images, height, cols, width), "narrow", split_axis=1, concat_axis=0, tiled=True
    ).astype(F32)
    grad_mod = jnp.concatenate([gmod_one[:, :2], gmod_two[:, :4]], axis=1).reshape(images, 6 * width)
    grad_ada = jnp.dot(cond.astype(F32).T, grad_mod, precision=HIGH)
    second = total_of([d_qkv, d_proj, d_ca[:9], grad_ada, jnp.sum(grad_mod, axis=0)])
    return (
        res.reshape(out_grad.shape),
        grad_latents,
        second[3],
        second[4],
        second[2].reshape(conv_attn.shape),
        second[0],
        second[1],
        first[0],
        first[4][0],
        first[3].reshape(conv_ffn.shape),
        first[1].T,
        first[5][0],
        first[2].T,
        first[6][0],
    )


def solution(mesh):
    strip = P("wide", "narrow", None, None)
    image = P(AXES, None, None, None)
    in_specs = (strip, P("wide"), image) + (P(),) * 12
    out_specs = (image, strip) + (P(),) * 12
    return jax.shard_map(shards, mesh=mesh, in_specs=in_specs, out_specs=out_specs, check_vma=False)
```

```python
import functools
import math

import jax
import jax.numpy as jnp
from jax import lax
from jax.experimental import pallas as pl
from jax.experimental.pallas import tpu as pltpu
from jax.sharding import PartitionSpec as P

HEADS = 6
EPSILON = 1e-06
HIGH = lax.Precision.HIGHEST
BF = jnp.bfloat16
F32 = jnp.float32
NN = ((1,), (0,))
NT = ((1,), (1,))
TN = ((0,), (0,))
LANES = 128
CHUNK = 256
TILE = 64
GELU_A = math.sqrt(2.0 / math.pi)
GELU_B = 0.044715
AXES = ("wide", "narrow")


def mm(left, right, dims=NN):
    return lax.dot_general(left, right, (dims, ((), ())), preferred_element_type=F32)


def col_sum(values):
    return jnp.sum(values, axis=0, keepdims=True)


def row_mean(values):
    return jnp.mean(values, axis=1, keepdims=True)


def normed(values):
    center = values - row_mean(values)
    spread = row_mean(center * center)
    inverse = lax.rsqrt(spread + EPSILON)
    return center * inverse, inverse


def norm_back(grad_normed, normed_values, inverse):
    return inverse * (
        grad_normed - row_mean(grad_normed) - normed_values * row_mean(grad_normed * normed_values)
    )


def tap_source(phase, tap):
    distance = phase + tap - 1
    return distance % 2, distance // 2


def tap_ref(plain, moved, row_phase, col_phase, row_tap, col_tap, cols, start, size, lanes):
    source_row, row_move = tap_source(row_phase, row_tap)
    source_col, col_move = tap_source(col_phase, col_tap)
    held = plain if col_move == 0 else moved
    return held[2 * source_row + source_col, pl.ds(cols + cols * row_move + start, size), lanes]


def fill_planes(plain, moved, plane, col_phase_matrix, values_low, cols, lanes):
    tokens = values_low.shape[0]
    plain[plane, pl.ds(cols, tokens), lanes] = values_low.astype(F32)
    moved[plane, pl.ds(cols, tokens), lanes] = mm(col_phase_matrix, values_low)


def conv_tile(plain, moved, weight, row_phase, col_phase, cols, start, size, lanes, lanes_weight):
    total = None
    for row_tap in range(3):
        for col_tap in range(3):
            window = tap_ref(
                plain, moved, row_phase, col_phase, row_tap, col_tap, cols, start, size, lanes
            )
            part = window * weight[pl.ds(row_tap * 3 + col_tap, 1), lanes_weight]
            total = part if total is None else total + part
    return total


def conv_back_tile(
    plain, moved, weight, inputs, kernel_grad, row_phase, col_phase, cols, start, size, lanes, lanes_weight
):
    total = None
    for row_tap in range(3):
        for col_tap in range(3):
            window = tap_ref(
                plain, moved, row_phase, col_phase, row_tap, col_tap, cols, start, size, lanes
            )
            mirror = (2 - row_tap) * 3 + (2 - col_tap)
            part = window * weight[pl.ds(mirror, 1), lanes_weight]
            total = part if total is None else total + part
            product = jnp.sum((window * inputs).reshape(size // 8, 8, LANES), axis=0)
            kernel_grad[mirror, :, lanes_weight] += product
    return total


def packed(values):
    return values.reshape(values.shape[0] // 8, 8, values.shape[1])


def kernel_rows(weight, lanes):
    return [jnp.broadcast_to(weight[pl.ds(tap, 1), lanes], (8, lanes.size)) for tap in range(9)]


def conv_packed(plain, moved, taps, row_phase, col_phase, cols, start, lanes):
    total = None
    for row_tap in range(3):
        for col_tap in range(3):
            window = packed(
                tap_ref(plain, moved, row_phase, col_phase, row_tap, col_tap, cols, start, TILE, lanes)
            )
            part = window * taps[row_tap * 3 + col_tap]
            total = part if total is None else total + part
    return total


def conv_back_packed(plain, moved, taps, inputs, row_phase, col_phase, cols, start, lanes):
    total = None
    sums = [None] * 9
    for row_tap in range(3):
        for col_tap in range(3):
            window = packed(
                tap_ref(plain, moved, row_phase, col_phase, row_tap, col_tap, cols, start, TILE, lanes)
            )
            mirror = (2 - row_tap) * 3 + (2 - col_tap)
            part = window * taps[mirror]
            total = part if total is None else total + part
            product = window * inputs
            count = product.shape[0]
            while count > 1:
                count //= 2
                product = product[:count] + product[count:]
            sums[mirror] = product[0].astype(F32)
    return total, sums


def fill_packed(plain, moved, plane, matrix, values_low, cols):
    tokens = values_low.shape[0]
    plain[plane, pl.ds(cols, tokens), :] = values_low
    moved[plane, pl.ds(cols, tokens), :] = mm(matrix, values_low).astype(BF)


def place_rows(ref, values, first_row, rank, parts):
    share = ref.shape[0] // parts
    step = math.gcd(math.gcd(share, values.shape[0]), first_row)
    for at in range(0, values.shape[0], step):
        part, rest = divmod(first_row + at, share)
        row = pl.multiple_of((part ^ rank) * share + rest, step)
        ref[pl.ds(row, step), :] = values[at : at + step]


def zero_pads(buffer, cols):
    planes, padded, width = buffer.shape
    edge = jnp.zeros((planes, cols, width), buffer.dtype)
    buffer[:, pl.ds(0, cols), :] = edge
    buffer[:, pl.ds(padded - cols, cols), :] = edge


def attention_forward_kernel(strips, begin, rank_ref, *refs):
    pieces, refs = refs[:strips], refs[strips:]
    mod_ref, qkv_w, conv_a, perm, moves = refs[:5]
    refs = refs[5:] if begin else refs[10:]
    xp_ref, co_ref, qkv_ref, mix_ref, stat_ref, plain_h, moved_h = refs
    tokens = moves.shape[1]
    cols = tokens // 16
    width = xp_ref.shape[2]
    quarter = perm.shape[0] // 4
    all_lanes = pl.ds(0, width)
    for ref in (plain_h, moved_h):
        zero_pads(ref, cols)
    shift_one, scale_one = (mod_ref[0, pl.ds(part, 1), :] for part in range(2))

    for at, piece in enumerate(pieces):
        strip = at ^ rank_ref[1]
        moved_piece = mm(perm[...], piece[...]).astype(BF)
        for plane in range(4):
            row = pl.multiple_of(plane * tokens + strip * quarter, quarter)
            xp_ref[0, pl.ds(row, quarter), :] = moved_piece[plane * quarter : (plane + 1) * quarter]

    for plane in range(4):
        unit, _ = normed(xp_ref[0, pl.ds(plane * tokens, tokens), :].astype(F32))
        low = (unit * (1.0 + scale_one) + shift_one).astype(BF)
        fill_planes(plain_h, moved_h, plane, moves[plane % 2], low, cols, all_lanes)
    for plane in range(4):
        for lane in range(0, width, LANES):
            for start in range(0, tokens, 128):
                lanes = pl.ds(lane, LANES)
                total = conv_tile(
                    plain_h, moved_h, conv_a, plane // 2, plane % 2, cols, start, 128, lanes, lanes
                )
                co_ref[0, pl.ds(plane * tokens + start, 128), lanes] = total.astype(BF)

    head_size = width // HEADS
    factor = head_size ** (-0.5)

    def attend(plane, carry):
        rows = pl.ds(pl.multiple_of(plane * tokens, tokens), tokens)
        qkv_ref[0, rows, :] = mm(co_ref[0, rows, :], qkv_w[...]).astype(BF)
        even = lax.broadcasted_iota(jnp.int32, (tokens, LANES), 1) < head_size
        scores = []
        for pair in range(width // LANES):
            query = qkv_ref[0, rows, pl.ds(pair * LANES, LANES)]
            key = qkv_ref[0, rows, pl.ds(width + pair * LANES, LANES)] * jnp.asarray(factor, BF)
            for mine in (even, ~even):
                scores.append(mm(jnp.where(mine, key, jnp.zeros_like(key)), query, NT))
        tops = [jnp.max(score, axis=0, keepdims=True) for score in scores]
        grown = [jnp.exp(score - top) for score, top in zip(scores, tops)]
        totals = [col_sum(values) for values in grown]
        probs = [(values * (1.0 / total)).astype(BF) for values, total in zip(grown, totals)]
        for pair in range(width // LANES):
            value_t = qkv_ref[0, rows, pl.ds(2 * width + pair * LANES, LANES)].T
            mixed_t = jnp.concatenate(
                [
                    mm(value_t[half * head_size : (half + 1) * head_size], probs[2 * pair + half])
                    for half in range(2)
                ],
                axis=0,
            )
            mix_ref[0, rows, pl.ds(pair * LANES, LANES)] = mixed_t.astype(BF).T
        for head in range(HEADS):
            stat_ref[0, plane, pl.ds(head, 1), :] = tops[head] + jnp.log(totals[head])
        return carry

    lax.fori_loop(0, 4, attend, 0)


def feed_forward_kernel(
    rank_ref,
    xp_ref,
    mix_ref,
    mod_ref,
    og_ref,
    proj_w,
    fc1_w,
    fc1_b,
    fc2_w,
    fc2_b,
    down_w,
    down_b,
    conv_f,
    moves,
    res_ref,
    gmid_ref,
    gmod_ref,
    big_ref,
    small_ref,
    fout_s,
    ghid_s,
    plain_p,
    moved_p,
    plain_g,
    moved_g,
    attn_s,
    gffn_s,
    hid_s,
    act_s,
    gpre_s,
    gact_s,
    hid_t,
    gffn_t,
    low_s,
    dconv_s,
    fc1_sum,
    fc2_sum,
    down_sum,
    *,
    parts,
):
    image = pl.program_id(0)
    tokens = moves.shape[1]
    cols = tokens // 16
    width = xp_ref.shape[2]
    hidden = fc1_w.shape[1]

    @pl.when(image == 0)
    def _():
        for ref in (fc1_sum, fc2_sum, down_sum, small_ref, dconv_s):
            ref[...] = jnp.zeros(ref.shape, F32)
        for ref in (plain_g, moved_g):
            zero_pads(ref, cols)
        for ref in (plain_p, moved_p):
            for slot in range(2):
                zero_pads(ref.at[slot], cols)

    gmod_ref[...] = jnp.zeros(gmod_ref.shape, F32)
    gate_one, shift_two, scale_two, gate_two = (mod_ref[0, pl.ds(part, 1), :] for part in range(2, 6))
    attn_s[...] = mm(mix_ref[0], proj_w[...])

    grad_low = og_ref[0]
    small_ref[pl.ds(10, 1), pl.ds(width, 2 * width)] += col_sum(grad_low.astype(F32))
    for plane in range(4):
        rows = pl.ds(plane * tokens, tokens)
        grad_after = mm(grad_low, down_w[pl.ds(plane * width, width), :], NT)
        gmid_ref[0, rows, :] = grad_after
        grad_out = (gate_two * grad_after).astype(BF)
        gffn_s[rows, :] = grad_out
        small_ref[pl.ds(10, 1), pl.ds(0, width)] += col_sum(grad_out.astype(F32))
        after = xp_ref[0, rows, :].astype(F32) + gate_one * attn_s[rows, :]
        unit, _ = normed(after)
        hid_s[rows, :] = (unit * (1.0 + scale_two) + shift_two).astype(BF)

    hid_t[...] = hid_s[...].T
    gffn_t[...] = gffn_s[...].T
    chunks = hidden // CHUNK

    def units_of(chunk):
        return pl.ds(pl.multiple_of(chunk * CHUNK, CHUNK), CHUNK)

    def prepare(chunk, slot):
        units = units_of(chunk)
        pre = (mm(hid_s[...], fc1_w[:, units]) + fc1_b[:, units]).astype(BF)
        for plane in range(4):
            fill_packed(
                plain_p.at[slot],
                moved_p.at[slot],
                plane,
                moves[plane % 2],
                pre[plane * tokens : (plane + 1) * tokens],
                cols,
            )
        gact_s[slot] = mm(gffn_s[...], fc2_w[units, :], NT).astype(gact_s.dtype)

    def collect(chunk, slot):
        units = units_of(chunk)
        ones = jnp.ones((16, act_s.shape[1]), BF)
        grad_pre = gpre_s[slot]
        active = act_s[slot]
        fc1_sum[:, units] += mm(hid_t[...], grad_pre)
        small_ref[pl.ds(9, 1), units] += mm(ones, grad_pre)[:1]
        fc2_sum[:, units] += mm(gffn_t[...], active)
        out = mm(active, fc2_w[units, :])
        grad_hid = mm(grad_pre, fc1_w[:, units], NT)
        for plane in range(4):
            part = slice(plane * tokens, (plane + 1) * tokens)
            fout_s[plane] += out[part]
            ghid_s[plane] += grad_hid[part]

    def convolve(chunk, slot):
        units = units_of(chunk)
        taps = kernel_rows(conv_f, units)
        chunk_lanes = pl.ds(0, CHUNK)
        plain, moved = plain_p.at[slot], moved_p.at[slot]
        for plane in range(4):
            for start in range(0, tokens, TILE):
                rows = pl.ds(plane * tokens + start, TILE)
                value = conv_packed(plain, moved, taps, plane // 2, plane % 2, cols, start, chunk_lanes)
                value_low = value.reshape(TILE, CHUNK)
                value = value_low.astype(F32)
                square = value * value
                half = 0.5 * jnp.tanh(value * (GELU_A + (GELU_A * GELU_B) * square))
                gate = 0.5 + half
                act_s[slot, rows, :] = (value * gate).astype(BF)
                gate_low = gate.astype(BF)
                bend = (value_low * (0.5 - half).astype(BF)) * (
                    jnp.asarray(2.0 * GELU_A, BF)
                    + (value_low * value_low) * jnp.asarray(6.0 * GELU_A * GELU_B, BF)
                )
                slope = gate_low + gate_low * bend
                plain_g[plane, pl.ds(cols + start, TILE), :] = slope * gact_s[slot, rows, :]
            rows = pl.ds(cols, tokens)
            moved_g[plane, rows, :] = mm(moves[plane % 2], plain_g[plane, rows, :]).astype(BF)
        kernel_grads = None
        for plane in range(4):
            for start in range(0, tokens, TILE):
                inputs = packed(plain[plane, pl.ds(cols + start, TILE), :])
                total, sums = conv_back_packed(
                    plain_g, moved_g, taps, inputs, plane // 2, plane % 2, cols, start, chunk_lanes
                )
                gpre_s[slot, pl.ds(plane * tokens + start, TILE), :] = total.reshape(TILE, CHUNK)
                kernel_grads = (
                    sums if kernel_grads is None else [a + b for a, b in zip(kernel_grads, sums)]
                )
        for tap in range(9):
            dconv_s[tap, :, units] += kernel_grads[tap]

    for ref in (fout_s, ghid_s):
        ref[...] = jnp.zeros(ref.shape, F32)
    for ref in (act_s, gpre_s):
        ref[1] = jnp.zeros(ref.shape[1:], BF)
    prepare(0, 0)

    def feed(step, carry):
        chunk = 2 * step
        prepare(chunk + 1, 1)
        collect(jnp.maximum(chunk - 1, 0), 1)
        convolve(chunk, 0)
        prepare(jnp.minimum(chunk + 2, chunks - 1), 0)
        collect(chunk, 0)
        convolve(chunk + 1, 1)
        return carry

    lax.fori_loop(0, chunks // 2, feed, 0)
    collect(chunks - 1, 1)

    grad_gate_one = grad_shift_two = grad_scale_two = grad_gate_two = jnp.zeros((1, width), F32)
    for plane in range(4):
        rows = pl.ds(plane * tokens, tokens)
        attn = attn_s[rows, :]
        after = xp_ref[0, rows, :].astype(F32) + gate_one * attn
        grad_after = gmid_ref[0, rows, :]
        out = fout_s[plane] + fc2_b[...]
        grad_gate_two += col_sum(out * grad_after)
        low_s[:, pl.ds(plane * width, width)] = (after + gate_two * out).astype(BF)
        grad_hid = ghid_s[plane]
        unit, inverse = normed(after)
        grad_shift_two += col_sum(grad_hid)
        grad_scale_two += col_sum(grad_hid * unit)
        grad_mid = grad_after + norm_back(grad_hid * (1.0 + scale_two), unit, inverse)
        gmid_ref[0, rows, :] = grad_mid
        grad_gate_one += col_sum(attn * grad_mid)
    gmod_ref[0, pl.ds(0, 1), :] = grad_gate_one
    gmod_ref[0, pl.ds(1, 1), :] = grad_shift_two
    gmod_ref[0, pl.ds(2, 1), :] = grad_scale_two
    gmod_ref[0, pl.ds(3, 1), :] = grad_gate_two

    res_ref[0] = (mm(low_s[...], down_w[...]) + down_b[...]).astype(BF)
    grad_low_t = grad_low.T

    def down_weights(chunk, carry):
        units = pl.ds(pl.multiple_of(chunk * CHUNK, CHUNK), CHUNK)
        down_sum[:, units] += mm(grad_low_t, low_s[:, units])
        return carry

    lax.fori_loop(0, low_s.shape[1] // CHUNK, down_weights, 0)

    @pl.when(image == pl.num_programs(0) - 1)
    def _():
        for tap in range(9):
            small_ref[pl.ds(tap, 1), :] = col_sum(dconv_s[tap])

        rank = rank_ref[0]
        for chunk in range(hidden // CHUNK):
            units = pl.ds(chunk * CHUNK, CHUNK)
            place_rows(big_ref, fc2_sum[:, units].T.astype(BF), chunk * CHUNK, rank, parts)
            down = down_sum[:, units].T.astype(BF)
            for half in range(2):
                place_rows(
                    big_ref,
                    down[:, half * width : (half + 1) * width],
                    (1 + half) * hidden + chunk * CHUNK,
                    rank,
                    parts,
                )
        for part in range(hidden // width):
            block = fc1_sum[:, pl.ds(part * width, width)].astype(BF)
            place_rows(big_ref, block, 3 * hidden + part * width, rank, parts)


def attention_back_kernel(
    rank_ref,
    mod_ref,
    gmid_ref,
    co_ref,
    qkv_ref,
    mix_ref,
    stat_ref,
    proj_w,
    small_ref,
    *rest,
    parts,
    begin,
    fresh,
    last,
):
    image = pl.program_id(0)
    width = mix_ref.shape[2]
    tokens = mix_ref.shape[1] // 4
    rest = list(rest)
    before_ref = None if begin else rest.pop(0)
    if not fresh:
        rest.pop(0)
    gqkv_ref = rest.pop(0)
    sum_ref = rest.pop(0)
    rows_ref = rest.pop(0) if last else None
    gout_s, gmix_s = rest

    @pl.when(image == 0)
    def _():
        sum_ref[...] = jnp.zeros(sum_ref.shape, F32) if begin else before_ref[...]

    gate_one = mod_ref[0, pl.ds(2, 1), :]
    head_size = width // HEADS
    factor = jnp.asarray(head_size ** (-0.5), BF)

    def attend(plane, carry):
        rows = pl.ds(pl.multiple_of(plane * tokens, tokens), tokens)
        grad_out = (gate_one * gmid_ref[0, rows, :]).astype(BF)
        gout_s[rows, :] = grad_out
        gmix_s[...] = mm(grad_out, proj_w[...], NT).astype(BF)
        even = lax.broadcasted_iota(jnp.int32, (tokens, LANES), 1) < head_size
        zero = jnp.zeros((tokens, LANES), BF)
        for pair in range(width // LANES):
            lane = pair * LANES
            query = qkv_ref[0, rows, pl.ds(lane, LANES)]
            key = qkv_ref[0, rows, pl.ds(width + lane, LANES)] * factor
            value = qkv_ref[0, rows, pl.ds(2 * width + lane, LANES)]
            query_low = query * factor
            key_t = key.T
            grad_mixed = gmix_s[:, pl.ds(lane, LANES)]
            masks = (even, ~even)
            scores = [mm(jnp.where(mine, key, zero), query, NT) for mine in masks]
            grad_probs = [mm(jnp.where(mine, value, zero), grad_mixed, NT) for mine in masks]
            probs = [
                jnp.exp(score - stat_ref[0, plane, pl.ds(2 * pair + half, 1), :])
                for half, score in enumerate(scores)
            ]
            weighted = [a * b for a, b in zip(probs, grad_probs)]
            inner = [col_sum(values) for values in weighted]
            grad_scores = [
                (values - prob * total).astype(BF)
                for values, prob, total in zip(weighted, probs, inner)
            ]
            grad_value = sum(
                mm(prob.astype(BF), jnp.where(mine, grad_mixed, zero))
                for prob, mine in zip(probs, masks)
            )
            grad_key = sum(
                mm(values, jnp.where(mine, query_low, zero)) for values, mine in zip(grad_scores, masks)
            )
            grad_query_t = jnp.concatenate(
                [
                    mm(key_t[half * head_size : (half + 1) * head_size], grad_scores[half])
                    for half in range(2)
                ],
                axis=0,
            )
            gqkv_ref[0, rows, pl.ds(lane, LANES)] = grad_query_t.astype(BF).T
            gqkv_ref[0, rows, pl.ds(width + lane, LANES)] = grad_key.astype(BF)
            gqkv_ref[0, rows, pl.ds(2 * width + lane, LANES)] = grad_value.astype(BF)
        return carry

    lax.fori_loop(0, 4, attend, 0)

    sum_ref[:, pl.ds(3 * width, width)] += mm(mix_ref[0].T, gout_s[...])
    conv_t = co_ref[0].T
    for part in range(3):
        lanes = pl.ds(part * width, width)
        sum_ref[:, lanes] += mm(conv_t, gqkv_ref[0, :, lanes])

    if last:

        @pl.when(image == pl.num_programs(0) - 1)
        def _():
            rank = rank_ref[0]
            rows_ref[...] = jnp.zeros(rows_ref.shape, BF)
            for part in range(4):
                lanes = pl.ds(part * width, width)
                place_rows(rows_ref, sum_ref[:, lanes].astype(BF), part * width, rank, parts)
            for part in range(4):
                lanes = pl.ds(part * width, width)
                place_rows(rows_ref, small_ref[:, lanes].astype(BF), 4 * width + part * 16, rank, parts)


def conv_attn_back_kernel(
    strips,
    rank_ref,
    xp_ref,
    mod_ref,
    gmid_ref,
    gqkv_ref,
    qkv_w,
    conv_a,
    perm_back,
    moves,
    *refs,
):
    pieces, refs = refs[:strips], refs[strips:]
    gmod_ref, d_conv, plain_h, plain_g, moved_g, gout_s, glat_s, dconv_s = refs
    image = pl.program_id(0)
    tokens = moves.shape[1]
    cols = tokens // 16
    width = xp_ref.shape[2]
    quarter = perm_back.shape[0] // 4
    all_lanes = pl.ds(0, width)

    @pl.when(image == 0)
    def _():
        d_conv[...] = jnp.zeros(d_conv.shape, F32)
        dconv_s[...] = jnp.zeros(dconv_s.shape, F32)
        for ref in (plain_g, moved_g):
            zero_pads(ref, cols)

    gmod_ref[...] = jnp.zeros(gmod_ref.shape, F32)
    shift_one, scale_one = (mod_ref[0, pl.ds(part, 1), :] for part in range(2))
    for plane in range(4):
        rows = pl.ds(plane * tokens, tokens)
        grad_conv = mm(gqkv_ref[0, rows, :], qkv_w[...], NT).astype(BF)
        fill_planes(plain_g, moved_g, plane, moves[plane % 2], grad_conv, cols, all_lanes)
        unit, _ = normed(xp_ref[0, rows, :].astype(F32))
        low = (unit * (1.0 + scale_one) + shift_one).astype(BF)
        plain_h[rows, :] = low.astype(F32)
    for plane in range(4):
        for lane in range(0, width, LANES):
            for start in range(0, tokens, 128):
                lanes = pl.ds(lane, LANES)
                rows = pl.ds(plane * tokens + start, 128)
                total = conv_back_tile(
                    plain_g,
                    moved_g,
                    conv_a,
                    plain_h[rows, lanes],
                    dconv_s,
                    plane // 2,
                    plane % 2,
                    cols,
                    start,
                    128,
                    lanes,
                    lanes,
                )
                glat_s[rows, lanes] = total
    grad_shift = grad_scale = jnp.zeros((1, width), F32)
    for plane in range(4):
        rows = pl.ds(plane * tokens, tokens)
        grad_hid = glat_s[rows, :]
        unit, inverse = normed(xp_ref[0, rows, :].astype(F32))
        grad_shift += col_sum(grad_hid)
        grad_scale += col_sum(grad_hid * unit)
        gout_s[rows, :] = (
            gmid_ref[0, rows, :] + norm_back(grad_hid * (1.0 + scale_one), unit, inverse)
        ).astype(BF)
    gmod_ref[0, pl.ds(0, 1), :] = grad_shift
    gmod_ref[0, pl.ds(1, 1), :] = grad_scale
    for at, piece in enumerate(pieces):
        strip = at ^ rank_ref[1]
        gathered = jnp.concatenate(
            [
                gout_s[pl.ds(pl.multiple_of(plane * tokens + strip * quarter, quarter), quarter), :]
                for plane in range(4)
            ],
            axis=0,
        )
        piece[0] = mm(perm_back[...], gathered).astype(BF)

    @pl.when(image == pl.num_programs(0) - 1)
    def _():
        for tap in range(9):
            d_conv[pl.ds(tap, 1), :] = col_sum(dconv_s[tap])


FINISH_STEPS = 8


def finish_big_kernel(rank_ref, rows_ref, fc1_ref, fc2_ref, down_ref):
    step = pl.program_id(0)
    count, share, width = rows_ref.shape
    inner = rank_ref[0] % count

    def write(ref, flat):
        for at in range(count):
            values = rows_ref[at ^ inner].astype(F32)
            if flat:
                ref[pl.ds(at * share, share), :] = values
            else:
                block, row = divmod(at * share, width)
                ref[pl.ds(row, share), pl.ds(block * width, width)] = values

    @pl.when(step < 2)
    def _():
        write(fc2_ref, True)

    @pl.when((step >= 2) & (step < 6))
    def _():
        write(down_ref, True)

    @pl.when(step >= 6)
    def _():
        write(fc1_ref, False)


def finish_rest_kernel(rank_ref, rows_ref, qkv_ref, proj_ref, small_ref, *, share):
    width = proj_ref.shape[0]
    rank = rank_ref[0]
    for part in range(rows_ref.shape[0]):
        values = rows_ref[part ^ rank, pl.ds(0, share), :].astype(F32)
        block, row = divmod(part * share, width)
        if block < 3:
            qkv_ref[pl.ds(row, share), pl.ds(block * width, width)] = values
        elif block == 3:
            proj_ref[pl.ds(row, share), :] = values
        elif block == 4 and row < 64:
            small = min(share, 16)
            for at in range(0, share, small):
                lanes = pl.ds((row + at) // 16 * width, width)
                small_ref[:, lanes] = values[at : at + small]


def per_image(shape, first=0):
    rest = len(shape) - 1
    return pl.BlockSpec((1,) + tuple(shape[1:]), lambda b, *_: (b + first,) + (0,) * rest)


def resident(shape):
    rank = len(shape)
    return pl.BlockSpec(tuple(shape), lambda b, *_: (0,) * rank, pipeline_mode=pl.Buffered(1))


def out_of(shape, dtype):
    return jax.ShapeDtypeStruct(shape, dtype)


PARAMS = pltpu.CompilerParams(
    dimension_semantics=("arbitrary",), vmem_limit_bytes=63 * 1024 * 1024
)


def token_tables(cols, strip):
    half = cols // 2
    spot = jnp.arange(strip)
    from_row, from_col = spot // cols, spot % cols
    target = ((from_row % 2) * 2 + from_col % 2) * (strip // 4) + (from_row // 2) * half + from_col // 2
    perm_back = (target[:, None] == spot[None, :]).astype(BF)
    perm = (spot[:, None] == target[None, :]).astype(BF)
    spot = jnp.arange(half * half)
    ahead = ((spot[None, :] == spot[:, None] + 1) & (spot[:, None] % half != half - 1)).astype(BF)
    behind = ((spot[None, :] == spot[:, None] - 1) & (spot[:, None] % half != 0)).astype(BF)
    return perm, perm_back, jnp.stack([ahead, behind])


def attention_forward_call(rank, image, images, pieces, mod, qkv_w, conv_a, perm, moves, held):
    strips = len(pieces)
    width = pieces[0].shape[1]
    tokens = moves.shape[1]
    shared = (qkv_w, conv_a, perm, moves)
    rows = 4 * tokens
    outs = [
        ((images, rows, width), BF),
        ((images, rows, width), BF),
        ((images, rows, 3 * width), BF),
        ((images, rows, width), BF),
        ((images, 4, 8, tokens), F32),
    ]
    begin = held is None
    held = () if begin else tuple(held)
    grid = pltpu.PrefetchScalarGridSpec(
        num_scalar_prefetch=1,
        grid=(1,),
        in_specs=[resident(piece.shape) for piece in pieces]
        + [per_image(mod.shape, image)]
        + [resident(w.shape) for w in shared]
        + [pl.BlockSpec(memory_space=pl.ANY)] * len(held),
        out_specs=[per_image(shape, image) for shape, _ in outs],
        scratch_shapes=[pltpu.VMEM((4, tokens + 32, width), F32)] * 2,
    )
    return pl.pallas_call(
        functools.partial(attention_forward_kernel, strips, begin),
        grid_spec=grid,
        out_shape=[out_of(shape, dtype) for shape, dtype in outs],
        input_output_aliases={} if begin else {strips + 6 + at: at for at in range(5)},
        compiler_params=PARAMS,
        cost_estimate=cost(1, 5e9, 8e6),
        name="attention_forward",
    )(rank, *pieces, mod, *shared, *held)


def feed_forward_call(rank, parts, xp, mix, mod, og, weights, moves):
    proj_w, fc1_w, fc1_b, fc2_w, fc2_b, down_w, down_b, conv_f = weights
    images, all_tokens, width = xp.shape
    tokens = moves.shape[1]
    hidden = fc1_w.shape[1]
    padded = tokens + 32
    per = (xp, mix, mod, og)
    shared = (*weights, moves)
    outs = [
        (og.shape[:2] + (down_w.shape[1],), BF),
        (xp.shape, F32),
        ((images, 8, width), F32),
    ]
    sums = [((4 * hidden, width), BF), ((16, hidden), F32)]
    grid = pltpu.PrefetchScalarGridSpec(
        num_scalar_prefetch=1,
        grid=(images,),
        in_specs=[per_image(v.shape) for v in per] + [resident(w.shape) for w in shared],
        out_specs=[per_image(s) for s, _ in outs] + [resident(s) for s, _ in sums],
        scratch_shapes=[
            pltpu.VMEM((4, tokens, width), F32),
            pltpu.VMEM((4, tokens, width), F32),
            pltpu.VMEM((2, 4, padded, CHUNK), BF),
            pltpu.VMEM((2, 4, padded, CHUNK), BF),
            pltpu.VMEM((4, padded, CHUNK), BF),
            pltpu.VMEM((4, padded, CHUNK), BF),
            pltpu.VMEM((all_tokens, width), F32),
            pltpu.VMEM((all_tokens, width), BF),
            pltpu.VMEM((all_tokens, width), BF),
            pltpu.VMEM((2, all_tokens, CHUNK), BF),
            pltpu.VMEM((2, all_tokens, CHUNK), BF),
            pltpu.VMEM((2, all_tokens, CHUNK), BF),
            pltpu.VMEM((width, all_tokens), BF),
            pltpu.VMEM((width, all_tokens), BF),
            pltpu.VMEM((tokens, 4 * width), BF),
            pltpu.VMEM((9, 8, hidden), F32),
            pltpu.VMEM((width, hidden), F32),
            pltpu.VMEM((width, hidden), F32),
            pltpu.VMEM((down_w.shape[1], hidden), F32),
        ],
    )
    return pl.pallas_call(
        functools.partial(feed_forward_kernel, parts=parts),
        grid_spec=grid,
        out_shape=[out_of(s, d) for s, d in outs + sums],
        compiler_params=PARAMS,
        cost_estimate=cost(images, 14e9, 20e6),
        name="feed_forward",
    )(rank, *per, *shared)


def cost(images, flops, moved):
    return pl.CostEstimate(
        flops=int(images * flops), bytes_accessed=int(images * moved), transcendentals=0
    )


def attention_back_call(rank, parts, image, last, group, mod, gmid, co, qkv, mix, stat, proj_w, small, before, held):
    width = mix.shape[2]
    all_tokens = mix.shape[1]
    first, count = group
    begin = before is None
    fresh = held is None
    per = (mod, gmid, co, qkv, mix, stat)
    shared = (proj_w, small) + (() if begin else (before,))
    aliased = () if fresh else (held,)
    outs = [((count,) + qkv.shape[1:], BF)]
    share = 64 if parts <= 32 else 16
    sums = [((width, 4 * width), F32)] + ([((share * parts, width), BF)] if last else [])
    grid = pltpu.PrefetchScalarGridSpec(
        num_scalar_prefetch=1,
        grid=(1,),
        in_specs=[per_image(v.shape, image) for v in per]
        + [resident(w.shape) for w in shared]
        + [pl.BlockSpec(memory_space=pl.ANY)] * len(aliased),
        out_specs=[per_image(s, image - first) for s, _ in outs] + [resident(s) for s, _ in sums],
        scratch_shapes=[
            pltpu.VMEM((all_tokens, width), BF),
            pltpu.VMEM((all_tokens // 4, width), BF),
        ],
    )
    return pl.pallas_call(
        functools.partial(attention_back_kernel, parts=parts, begin=begin, fresh=fresh, last=last),
        grid_spec=grid,
        out_shape=[out_of(s, d) for s, d in outs + sums],
        input_output_aliases={} if fresh else {1 + len(per) + len(shared): 0},
        compiler_params=PARAMS,
        cost_estimate=cost(1, 8e9, 10e6),
        name="attention_back",
    )(rank, *per, *shared, *aliased)


def conv_attn_back_call(rank, strips, first, xp, mod, gmid, gqkv, weights, perm_back, moves):
    qkv_w, conv_a = weights
    images, all_tokens, width = gqkv.shape[0], xp.shape[1], xp.shape[2]
    tokens = moves.shape[1]
    padded = tokens + 32
    shared = (qkv_w, conv_a, perm_back, moves)
    outs = [((images, all_tokens // strips, width), BF)] * strips + [((images, 8, width), F32)]
    sums = [(16, width)]
    grid = pltpu.PrefetchScalarGridSpec(
        num_scalar_prefetch=1,
        grid=(images,),
        in_specs=[per_image(v.shape, first) for v in (xp, mod, gmid)]
        + [per_image(gqkv.shape)]
        + [resident(w.shape) for w in shared],
        out_specs=[per_image(s) for s, _ in outs] + [resident(s) for s in sums],
        scratch_shapes=[
            pltpu.VMEM((all_tokens, width), F32),
            pltpu.VMEM((4, padded, width), F32),
            pltpu.VMEM((4, padded, width), F32),
            pltpu.VMEM((all_tokens, width), BF),
            pltpu.VMEM((all_tokens, width), F32),
            pltpu.VMEM((9, 8, width), F32),
        ],
    )
    return pl.pallas_call(
        functools.partial(conv_attn_back_kernel, strips),
        grid_spec=grid,
        out_shape=[out_of(s, d) for s, d in outs] + [out_of(s, F32) for s in sums],
        compiler_params=PARAMS,
        cost_estimate=cost(images, 4e9, 8e6),
        name="conv_attn_back",
    )(rank, xp, mod, gmid, gqkv, *shared)


def finish_latents_kernel(strips, rank_ref, *refs):
    out_ref = refs[-1]
    for at in range(strips):
        out_ref[at ^ rank_ref[1], 0] = refs[at][0].astype(F32)


def finish_latents_call(rank, images, first, pieces, held):
    strips = len(pieces)
    count, tokens, width = pieces[0].shape
    shape = (strips, images, tokens, width)
    held = () if held is None else (held,)
    grid = pltpu.PrefetchScalarGridSpec(
        num_scalar_prefetch=1,
        grid=(count,),
        in_specs=[per_image(piece.shape) for piece in pieces]
        + [pl.BlockSpec(memory_space=pl.ANY)] * len(held),
        out_specs=pl.BlockSpec((strips, 1, tokens, width), lambda b, *_: (0, b + first, 0, 0)),
    )
    return pl.pallas_call(
        functools.partial(finish_latents_kernel, strips),
        grid_spec=grid,
        out_shape=out_of(shape, F32),
        input_output_aliases={strips + 1: 0} if held else {},
        compiler_params=PARAMS,
        cost_estimate=cost(count, 0, 3e6),
        name="finish_latents",
    )(rank, *pieces, *held)


def finish_big_call(rank, rows, hidden, width):
    parts, share, _ = rows.shape
    count = parts // FINISH_STEPS
    deep = count * share
    grid = pltpu.PrefetchScalarGridSpec(
        num_scalar_prefetch=1,
        grid=(FINISH_STEPS,),
        in_specs=[pl.BlockSpec((count, share, width), lambda i, rank: (i ^ (rank[0] // count), 0, 0))],
        out_specs=[
            pl.BlockSpec((width, deep), lambda i, rank: (0, jnp.maximum(i - 6, 0))),
            pl.BlockSpec((deep, width), lambda i, rank: (jnp.minimum(i, 1), 0)),
            pl.BlockSpec(
                (deep, width), lambda i, rank: (jnp.clip(i - 2, 0, 3) % 2, jnp.clip(i - 2, 0, 3) // 2)
            ),
        ],
    )
    return pl.pallas_call(
        finish_big_kernel,
        grid_spec=grid,
        out_shape=[out_of((width, hidden), F32), out_of((hidden, width), F32), out_of((hidden, 2 * width), F32)],
        compiler_params=PARAMS,
        cost_estimate=cost(1, 0, 15e6),
        name="finish_big",
    )(rank, rows)


def finish_rest_call(rank, rows, share, width):
    shapes = [(width, 3 * width), (width, width), (16, 4 * width)]
    grid = pltpu.PrefetchScalarGridSpec(
        num_scalar_prefetch=1,
        grid=(1,),
        in_specs=[resident(rows.shape)],
        out_specs=[resident(shape) for shape in shapes],
    )
    return pl.pallas_call(
        functools.partial(finish_rest_kernel, share=share),
        grid_spec=grid,
        out_shape=[out_of(shape, F32) for shape in shapes],
        compiler_params=PARAMS,
        cost_estimate=cost(1, 0, 5e6),
        name="finish_rest",
    )(rank, rows)


def stages(devices):
    bits = devices.bit_length() - 1
    found = [[1]]
    for at in range(1, bits, 2):
        group = [1 << b for b in range(at, min(at + 2, bits))]
        found.append(group)
    return found


def group_masks(group):
    if len(group) == 1:
        return [0, group[0]]
    return [0, group[1], group[0], group[0] | group[1]]


def exchange(values, mask, devices):
    return lax.ppermute(values, AXES, [(i, i ^ mask) for i in range(devices)])


def swap_strips(values, mask):
    count = lax.axis_size("narrow")
    return lax.ppermute(values, "narrow", [(i, i ^ mask) for i in range(count)])


def sent_strips(pieces):
    return [piece if at == 0 else swap_strips(piece, at) for at, piece in enumerate(pieces)]


def scatter_stage(values, group, devices):
    masks = group_masks(group)
    size = values.shape[0] // len(masks)
    total = values[:size].astype(F32)
    for at, mask in enumerate(masks[1:], 1):
        total = total + exchange(values[at * size : (at + 1) * size], mask, devices).astype(F32)
    return total.astype(BF)


def gather_stage(values, group, devices):
    masks = group_masks(group)
    return jnp.concatenate(
        [values] + [exchange(values, mask, devices) for mask in masks[1:]], axis=0
    )


def flat_rank(devices):
    index = lax.axis_index("wide") * lax.axis_size("narrow") + lax.axis_index("narrow")
    rank = jnp.zeros((), jnp.int32)
    bits = devices.bit_length() - 1
    for bit in range(bits):
        rank = rank | (((index >> bit) & 1) << (bits - 1 - bit))
    return jnp.stack([rank, lax.axis_index("narrow")])


def shards(
    latents,
    timesteps,
    out_grad,
    ada_weight,
    ada_bias,
    conv_attn,
    qkv_weight,
    proj_weight,
    fc1_weight,
    fc1_bias,
    conv_ffn,
    fc2_weight,
    fc2_bias,
    down_weight,
    down_bias,
):
    images, cols, width = out_grad.shape[0], latents.shape[2], latents.shape[3]
    height = latents.shape[1] * lax.axis_size("narrow")
    hidden = fc1_weight.shape[1]
    devices = lax.axis_size("wide") * lax.axis_size("narrow")
    rank = flat_rank(devices)
    steps = stages(devices)
    strips = lax.axis_size("narrow")
    strip_tokens = latents.shape[1] * cols
    place = lax.axis_index("narrow")
    sources = latents.reshape(strips, images, strip_tokens, width)
    own_steps = lax.dynamic_slice_in_dim(timesteps, lax.axis_index("narrow") * images, images)
    half_count = ada_weight.shape[0] // 2
    freq = jnp.exp(-math.log(10000.0) * jnp.arange(half_count, dtype=F32) / half_count)
    angles = own_steps.astype(F32)[:, None] * freq[None, :]
    features = jnp.concatenate([jnp.cos(angles), jnp.sin(angles)], axis=1)
    cond = jax.nn.silu(features).astype(BF)
    mod = jnp.dot(cond, ada_weight, preferred_element_type=F32) + ada_bias.astype(F32)
    mod = jnp.pad(mod.reshape(images, 6, width), ((0, 0), (0, 2), (0, 0)))
    perm, perm_back, moves = token_tables(cols, strip_tokens)
    conv_a = jnp.pad(conv_attn.reshape(9, width).astype(F32), ((0, 7), (0, 0)))
    conv_f = jnp.pad(conv_ffn.reshape(9, hidden), ((0, 7), (0, 0)))
    low = out_grad.reshape(images, height * cols // 4, out_grad.shape[3])
    held = None
    behind = None
    for image in range(images):
        pieces = [
            lax.dynamic_slice(sources, (place ^ at, image, 0, 0), (1, 1, strip_tokens, width)).reshape(
                strip_tokens, width
            )
            for at in range(strips)
        ]
        if behind is not None:
            behind, *pieces = lax.optimization_barrier((behind, *pieces))
            held = attention_forward_call(
                rank, image - 1, images, behind, mod, qkv_weight, conv_a, perm, moves, held
            )
        behind = tuple(
            piece if at == 0 else swap_strips(piece, at) for at, piece in enumerate(pieces)
        )
    xp, co, qkv, mix, stat = attention_forward_call(
        rank, images - 1, images, behind, mod, qkv_weight, conv_a, perm, moves, held
    )
    res, gmid, gmod_two, big, small = feed_forward_call(
        rank,
        devices,
        xp,
        mix,
        mod,
        low,
        (
            proj_weight,
            fc1_weight,
            fc1_bias.astype(F32)[None],
            fc2_weight,
            fc2_bias.astype(F32)[None],
            down_weight,
            down_bias.astype(F32)[None],
            conv_f,
        ),
        moves,
    )
    halves = [(0, images)] if images == 1 else [(0, images // 2), (images // 2, images - images // 2)]
    calls = images + len(halves)
    plan = [(0, 0), (1, 0), (1, 0), (2, 0), (3, 0), (4, 1)] if calls == 6 else [(min(at, 3), 0) for at in range(calls)]
    large = [functools.partial(scatter_stage, group=group, devices=devices) for group in steps]
    large += [functools.partial(gather_stage, group=group, devices=devices) for group in reversed(steps)]
    little = [functools.partial(scatter_stage, group=group, devices=devices) for group in steps]
    large_at = little_at = 0
    rest = before = None
    gqkv_parts = []

    def advance(call):
        nonlocal large_at, little_at, big, rest, mod
        while large_at < plan[call][0]:
            big = large[large_at](big)
            large_at += 1
        while little_at < plan[call][1]:
            rest = little[little_at](rest)
            little_at += 1
        if large_at:
            mod, big, rest = lax.optimization_barrier((mod, big, rest))

    for group in halves:
        gqkv = None
        for image in range(group[0], sum(group)):
            advance(image)
            gqkv, before, *final = attention_back_call(
                rank,
                devices,
                image,
                image == images - 1,
                group,
                mod,
                gmid,
                co,
                qkv,
                mix,
                stat,
                proj_weight,
                small,
                before,
                gqkv,
            )
        gqkv_parts.append(gqkv)
    rest = final[0]
    outs, mods, convs = [], [], []
    made = ()
    for at, ((first, count), gqkv) in enumerate(zip(halves, gqkv_parts)):
        advance(images + at)
        if at:
            mod, big, rest, made = lax.optimization_barrier((mod, big, rest, made))
            outs.append(sent_strips(made))
        *made, gmod_one, d_ca = conv_attn_back_call(
            rank, strips, first, xp, mod, gmid, gqkv, (qkv_weight, conv_a), perm_back, moves
        )
        mods.append(gmod_one)
        convs.append(d_ca)
    arrived = outs
    while large_at < len(large) or little_at < len(little):
        if large_at < len(large):
            big = large[large_at](big)
            large_at += 1
        if little_at < len(little):
            rest = little[little_at](rest)
            little_at += 1
        if made is not None:
            big, rest, made = lax.optimization_barrier((big, rest, made))
            sent, made = sent_strips(made), None
        else:
            big, rest, arrived = lax.optimization_barrier((big, rest, arrived))
    outs = [*arrived, sent]
    grad_mod = jnp.concatenate([jnp.concatenate(mods, axis=0)[:, :2], gmod_two[:, :4]], axis=1)
    late = jnp.concatenate(
        [
            sum(convs),
            grad_mod.reshape(images * 6, width),
            jnp.pad(cond.astype(F32), ((0, 0), (0, width - cond.shape[1]))),
        ],
        axis=0,
    )
    late = jnp.pad(late, ((0, -late.shape[0] % 16), (0, 0))).astype(BF)
    share = rest.shape[0]
    rest = jnp.concatenate([rest, late], axis=0)
    finished = None
    for at, group in enumerate(reversed(steps)):
        rest = gather_stage(rest, group, devices)
        if at == 0:
            rest, outs = lax.optimization_barrier((rest, outs))
        if at == 1:
            finished = finish_big_call(rank, big.reshape(devices, -1, width), hidden, width)
            rest, finished = lax.optimization_barrier((rest, finished))
    grad_fc1, grad_fc2, grad_down = finished
    grad_latents = None
    for (first, count), pieces in zip(halves, outs):
        grad_latents = finish_latents_call(rank, images, first, pieces, grad_latents)
    rest = rest.reshape(devices, -1, width)
    rest, grad_latents = lax.optimization_barrier((rest, grad_latents))
    grad_qkv, grad_proj, small = finish_rest_call(rank, rest, share, width)
    late = rest[:, share:]
    grad_conv_attn = jnp.sum(late[:, :9].astype(F32), axis=0)
    all_mod = late[:, 16 : 16 + 6 * images].reshape(devices * images, 6 * width)
    all_cond = late[:, 16 + 6 * images : 16 + 7 * images, : cond.shape[1]]
    all_cond = all_cond.reshape(devices * images, cond.shape[1])
    grad_ada = lax.dot_general(all_cond, all_mod, (TN, ((), ())), preferred_element_type=F32)
    grad_ada_bias = jnp.sum(all_mod.astype(F32), axis=0)
    return (
        res.reshape(out_grad.shape),
        grad_latents.reshape(latents.shape),
        grad_ada,
        grad_ada_bias,
        grad_conv_attn.reshape(conv_attn.shape),
        grad_qkv,
        grad_proj,
        grad_fc1,
        small[9],
        small[:9].reshape(conv_ffn.shape),
        grad_fc2,
        small[10, :width],
        grad_down,
        small[10, width : 3 * width],
    )


def solution(mesh):
    strip = P("wide", "narrow", None, None)
    image = P(AXES, None, None, None)
    in_specs = (strip, P("wide"), image) + (P(),) * 12
    out_specs = (image, strip) + (P(),) * 12
    return jax.shard_map(shards, mesh=mesh, in_specs=in_specs, out_specs=out_specs, check_vma=False)
```

```python
import functools
import math

import jax
import jax.numpy as jnp
from jax import lax
from jax.experimental import pallas as pl
from jax.experimental.pallas import tpu as pltpu
from jax.sharding import PartitionSpec as P

HEADS = 6
EPSILON = 1e-06
HIGH = lax.Precision.HIGHEST
BF = jnp.bfloat16
F32 = jnp.float32
NN = ((1,), (0,))
NT = ((1,), (1,))
TN = ((0,), (0,))
LANES = 128
CHUNK = 256
TILE = 64
GELU_A = math.sqrt(2.0 / math.pi)
GELU_B = 0.044715
AXES = ("wide", "narrow")


def mm(left, right, dims=NN):
    return lax.dot_general(left, right, (dims, ((), ())), preferred_element_type=F32)


def col_sum(values):
    return jnp.sum(values, axis=0, keepdims=True)


def row_mean(values):
    return jnp.mean(values, axis=1, keepdims=True)


def normed(values):
    center = values - row_mean(values)
    spread = row_mean(center * center)
    inverse = lax.rsqrt(spread + EPSILON)
    return center * inverse, inverse


def norm_back(grad_normed, normed_values, inverse):
    return inverse * (
        grad_normed - row_mean(grad_normed) - normed_values * row_mean(grad_normed * normed_values)
    )


def tap_source(phase, tap):
    distance = phase + tap - 1
    return distance % 2, distance // 2


def tap_ref(plain, moved, row_phase, col_phase, row_tap, col_tap, cols, start, size, lanes):
    source_row, row_move = tap_source(row_phase, row_tap)
    source_col, col_move = tap_source(col_phase, col_tap)
    held = plain if col_move == 0 else moved
    return held[2 * source_row + source_col, pl.ds(cols + cols * row_move + start, size), lanes]


def fill_planes(plain, moved, plane, col_phase_matrix, values_low, cols, lanes):
    tokens = values_low.shape[0]
    plain[plane, pl.ds(cols, tokens), lanes] = values_low.astype(F32)
    moved[plane, pl.ds(cols, tokens), lanes] = mm(col_phase_matrix, values_low)


def conv_tile(plain, moved, weight, row_phase, col_phase, cols, start, size, lanes, lanes_weight):
    total = None
    for row_tap in range(3):
        for col_tap in range(3):
            window = tap_ref(
                plain, moved, row_phase, col_phase, row_tap, col_tap, cols, start, size, lanes
            )
            part = window * weight[pl.ds(row_tap * 3 + col_tap, 1), lanes_weight]
            total = part if total is None else total + part
    return total


def conv_back_tile(
    plain, moved, weight, inputs, kernel_grad, row_phase, col_phase, cols, start, size, lanes, lanes_weight
):
    total = None
    for row_tap in range(3):
        for col_tap in range(3):
            window = tap_ref(
                plain, moved, row_phase, col_phase, row_tap, col_tap, cols, start, size, lanes
            )
            mirror = (2 - row_tap) * 3 + (2 - col_tap)
            part = window * weight[pl.ds(mirror, 1), lanes_weight]
            total = part if total is None else total + part
            product = jnp.sum((window * inputs).reshape(size // 8, 8, LANES), axis=0)
            kernel_grad[mirror, :, lanes_weight] += product
    return total


def packed(values):
    return values.reshape(values.shape[0] // 8, 8, values.shape[1])


def kernel_rows(weight, lanes):
    return [jnp.broadcast_to(weight[pl.ds(tap, 1), lanes], (8, lanes.size)) for tap in range(9)]


def conv_packed(plain, moved, taps, row_phase, col_phase, cols, start, lanes):
    total = None
    for row_tap in range(3):
        for col_tap in range(3):
            window = packed(
                tap_ref(plain, moved, row_phase, col_phase, row_tap, col_tap, cols, start, TILE, lanes)
            )
            part = window * taps[row_tap * 3 + col_tap]
            total = part if total is None else total + part
    return total


def conv_back_packed(plain, moved, taps, inputs, row_phase, col_phase, cols, start, lanes):
    total = None
    sums = [None] * 9
    for row_tap in range(3):
        for col_tap in range(3):
            window = packed(
                tap_ref(plain, moved, row_phase, col_phase, row_tap, col_tap, cols, start, TILE, lanes)
            )
            mirror = (2 - row_tap) * 3 + (2 - col_tap)
            part = window * taps[mirror]
            total = part if total is None else total + part
            product = window * inputs
            count = product.shape[0]
            while count > 1:
                count //= 2
                product = product[:count] + product[count:]
            sums[mirror] = product[0].astype(F32)
    return total, sums


def fill_packed(plain, moved, plane, matrix, values_low, cols):
    tokens = values_low.shape[0]
    plain[plane, pl.ds(cols, tokens), :] = values_low
    moved[plane, pl.ds(cols, tokens), :] = mm(matrix, values_low).astype(BF)


def place_rows(ref, values, first_row, rank, parts):
    share = ref.shape[0] // parts
    step = math.gcd(math.gcd(share, values.shape[0]), first_row)
    for at in range(0, values.shape[0], step):
        part, rest = divmod(first_row + at, share)
        row = pl.multiple_of((part ^ rank) * share + rest, step)
        ref[pl.ds(row, step), :] = values[at : at + step]


def zero_pads(buffer, cols):
    planes, padded, width = buffer.shape
    edge = jnp.zeros((planes, cols, width), buffer.dtype)
    buffer[:, pl.ds(0, cols), :] = edge
    buffer[:, pl.ds(padded - cols, cols), :] = edge


def attention_forward_kernel(strips, begin, rank_ref, *refs):
    pieces, refs = refs[:strips], refs[strips:]
    mod_ref, qkv_w, conv_a, perm, moves = refs[:5]
    refs = refs[5:] if begin else refs[10:]
    xp_ref, co_ref, qkv_ref, mix_ref, stat_ref, plain_h, moved_h = refs
    tokens = moves.shape[1]
    cols = tokens // 16
    width = xp_ref.shape[2]
    quarter = perm.shape[0] // 4
    for ref in (plain_h, moved_h):
        zero_pads(ref, cols)
    shift_one, scale_one = (mod_ref[0, pl.ds(part, 1), :] for part in range(2))

    for at, piece in enumerate(pieces):
        strip = at ^ rank_ref[1]
        moved_piece = mm(perm[...], piece[...]).astype(BF)
        for plane in range(4):
            row = pl.multiple_of(plane * tokens + strip * quarter, quarter)
            xp_ref[0, pl.ds(row, quarter), :] = moved_piece[plane * quarter : (plane + 1) * quarter]

    for plane in range(4):
        unit, _ = normed(xp_ref[0, pl.ds(plane * tokens, tokens), :].astype(F32))
        low = (unit * (1.0 + scale_one) + shift_one).astype(BF)
        fill_planes(plain_h, moved_h, plane, moves[plane % 2], low, cols, pl.ds(0, width))
    for plane in range(4):
        for lane in range(0, width, LANES):
            for start in range(0, tokens, 128):
                lanes = pl.ds(lane, LANES)
                total = conv_tile(
                    plain_h, moved_h, conv_a, plane // 2, plane % 2, cols, start, 128, lanes, lanes
                )
                co_ref[0, pl.ds(plane * tokens + start, 128), lanes] = total.astype(BF)

    head_size = width // HEADS
    factor = head_size ** (-0.5)

    def attend(plane, carry):
        rows = pl.ds(pl.multiple_of(plane * tokens, tokens), tokens)
        qkv_ref[0, rows, :] = mm(co_ref[0, rows, :], qkv_w[...]).astype(BF)
        even = lax.broadcasted_iota(jnp.int32, (tokens, LANES), 1) < head_size
        scores = []
        zero = jnp.zeros((tokens, LANES), BF)
        for pair in range(width // LANES):
            query = qkv_ref[0, rows, pl.ds(pair * LANES, LANES)]
            key = qkv_ref[0, rows, pl.ds(width + pair * LANES, LANES)] * jnp.asarray(factor, BF)
            both = mm(jnp.concatenate([jnp.where(even, key, zero), jnp.where(even, zero, key)], axis=0), query, NT)
            scores += [both[:tokens], both[tokens:]]
        tops = [jnp.max(score, axis=0, keepdims=True) for score in scores]
        grown = [jnp.exp(score - top) for score, top in zip(scores, tops)]
        totals = [col_sum(values) for values in grown]
        probs = [(values * (1.0 / total)).astype(BF) for values, total in zip(grown, totals)]
        for pair in range(width // LANES):
            value_t = qkv_ref[0, rows, pl.ds(2 * width + pair * LANES, LANES)].T
            mixed_t = jnp.concatenate(
                [
                    mm(value_t[half * head_size : (half + 1) * head_size], probs[2 * pair + half])
                    for half in range(2)
                ],
                axis=0,
            )
            mix_ref[0, rows, pl.ds(pair * LANES, LANES)] = mixed_t.astype(BF).T
        for head in range(HEADS):
            stat_ref[0, plane, pl.ds(head, 1), :] = tops[head] + jnp.log(totals[head])
        return carry

    lax.fori_loop(0, 4, attend, 0)


def feed_forward_kernel(
    rank_ref,
    xp_ref,
    mix_ref,
    mod_ref,
    og_ref,
    proj_w,
    fc1_w,
    fc1_b,
    fc2_w,
    fc2_b,
    down_w,
    down_b,
    conv_f,
    moves,
    res_ref,
    gmid_ref,
    gmod_ref,
    big_ref,
    small_ref,
    fout_s,
    ghid_s,
    plain_p,
    moved_p,
    plain_g,
    moved_g,
    attn_s,
    gffn_s,
    hid_s,
    act_s,
    gpre_s,
    gact_s,
    hid_t,
    gffn_t,
    low_s,
    dconv_s,
    fc1_sum,
    fc2_sum,
    down_sum,
    *,
    parts,
):
    image = pl.program_id(0)
    tokens = moves.shape[1]
    cols = tokens // 16
    width = xp_ref.shape[2]
    hidden = fc1_w.shape[1]

    @pl.when(image == 0)
    def _():
        for ref in (fc1_sum, fc2_sum, down_sum, small_ref, dconv_s):
            ref[...] = jnp.zeros(ref.shape, F32)
        for ref in (plain_g, moved_g):
            zero_pads(ref, cols)
        for ref in (plain_p, moved_p):
            for slot in range(2):
                zero_pads(ref.at[slot], cols)

    gmod_ref[...] = jnp.zeros(gmod_ref.shape, F32)
    gate_one, shift_two, scale_two, gate_two = (mod_ref[0, pl.ds(part, 1), :] for part in range(2, 6))
    attn_s[...] = mm(mix_ref[0], proj_w[...])

    grad_low = og_ref[0]
    small_ref[pl.ds(10, 1), pl.ds(width, 2 * width)] += col_sum(grad_low.astype(F32))
    for plane in range(4):
        rows = pl.ds(plane * tokens, tokens)
        grad_after = mm(grad_low, down_w[pl.ds(plane * width, width), :], NT)
        gmid_ref[0, rows, :] = grad_after
        grad_out = (gate_two * grad_after).astype(BF)
        gffn_s[rows, :] = grad_out
        small_ref[pl.ds(10, 1), pl.ds(0, width)] += col_sum(grad_out.astype(F32))
        after = xp_ref[0, rows, :].astype(F32) + gate_one * attn_s[rows, :]
        unit, _ = normed(after)
        hid_s[rows, :] = (unit * (1.0 + scale_two) + shift_two).astype(BF)

    hid_t[...] = hid_s[...].T
    gffn_t[...] = gffn_s[...].T
    chunks = hidden // CHUNK

    def units_of(chunk):
        return pl.ds(pl.multiple_of(chunk * CHUNK, CHUNK), CHUNK)

    def prepare(chunk, slot):
        units = units_of(chunk)
        pre = (mm(hid_s[...], fc1_w[:, units]) + fc1_b[:, units]).astype(BF)
        for plane in range(4):
            fill_packed(
                plain_p.at[slot],
                moved_p.at[slot],
                plane,
                moves[plane % 2],
                pre[plane * tokens : (plane + 1) * tokens],
                cols,
            )
        gact_s[slot] = mm(gffn_s[...], fc2_w[units, :], NT).astype(gact_s.dtype)

    def collect(chunk, slot):
        units = units_of(chunk)
        ones = jnp.ones((16, act_s.shape[1]), BF)
        grad_pre = gpre_s[slot]
        active = act_s[slot]
        fc1_sum[:, units] += mm(hid_t[...], grad_pre)
        small_ref[pl.ds(9, 1), units] += mm(ones, grad_pre)[:1]
        fc2_sum[:, units] += mm(gffn_t[...], active)
        out = mm(active, fc2_w[units, :])
        grad_hid = mm(grad_pre, fc1_w[:, units], NT)
        for plane in range(4):
            part = slice(plane * tokens, (plane + 1) * tokens)
            fout_s[plane] += out[part]
            ghid_s[plane] += grad_hid[part]

    def convolve(chunk, slot):
        units = units_of(chunk)
        taps = kernel_rows(conv_f, units)
        chunk_lanes = pl.ds(0, CHUNK)
        plain, moved = plain_p.at[slot], moved_p.at[slot]
        for plane in range(4):
            for start in range(0, tokens, TILE):
                rows = pl.ds(plane * tokens + start, TILE)
                value = conv_packed(plain, moved, taps, plane // 2, plane % 2, cols, start, chunk_lanes)
                value_low = value.reshape(TILE, CHUNK)
                value = value_low.astype(F32)
                square = value * value
                half = 0.5 * jnp.tanh(value * (GELU_A + (GELU_A * GELU_B) * square))
                gate = 0.5 + half
                act_s[slot, rows, :] = (value * gate).astype(BF)
                gate_low = gate.astype(BF)
                bend = (value_low * (0.5 - half).astype(BF)) * (
                    jnp.asarray(2.0 * GELU_A, BF)
                    + (value_low * value_low) * jnp.asarray(6.0 * GELU_A * GELU_B, BF)
                )
                slope = gate_low + gate_low * bend
                plain_g[plane, pl.ds(cols + start, TILE), :] = slope * gact_s[slot, rows, :]
            rows = pl.ds(cols, tokens)
            moved_g[plane, rows, :] = mm(moves[plane % 2], plain_g[plane, rows, :]).astype(BF)
        kernel_grads = None
        for plane in range(4):
            for start in range(0, tokens, TILE):
                inputs = packed(plain[plane, pl.ds(cols + start, TILE), :])
                total, sums = conv_back_packed(
                    plain_g, moved_g, taps, inputs, plane // 2, plane % 2, cols, start, chunk_lanes
                )
                gpre_s[slot, pl.ds(plane * tokens + start, TILE), :] = total.reshape(TILE, CHUNK)
                kernel_grads = (
                    sums if kernel_grads is None else [a + b for a, b in zip(kernel_grads, sums)]
                )
        for tap in range(9):
            dconv_s[tap, :, units] += kernel_grads[tap]

    for ref in (fout_s, ghid_s):
        ref[...] = jnp.zeros(ref.shape, F32)
    for ref in (act_s, gpre_s):
        ref[1] = jnp.zeros(ref.shape[1:], BF)
    prepare(0, 0)

    def feed(step, carry):
        chunk = 2 * step
        prepare(chunk + 1, 1)
        collect(jnp.maximum(chunk - 1, 0), 1)
        convolve(chunk, 0)
        prepare(jnp.minimum(chunk + 2, chunks - 1), 0)
        collect(chunk, 0)
        convolve(chunk + 1, 1)
        return carry

    lax.fori_loop(0, chunks // 2, feed, 0)
    collect(chunks - 1, 1)

    grad_gate_one = grad_shift_two = grad_scale_two = grad_gate_two = jnp.zeros((1, width), F32)
    for plane in range(4):
        rows = pl.ds(plane * tokens, tokens)
        attn = attn_s[rows, :]
        after = xp_ref[0, rows, :].astype(F32) + gate_one * attn
        grad_after = gmid_ref[0, rows, :]
        out = fout_s[plane] + fc2_b[...]
        grad_gate_two += col_sum(out * grad_after)
        low_s[:, pl.ds(plane * width, width)] = (after + gate_two * out).astype(BF)
        grad_hid = ghid_s[plane]
        unit, inverse = normed(after)
        grad_shift_two += col_sum(grad_hid)
        grad_scale_two += col_sum(grad_hid * unit)
        grad_mid = grad_after + norm_back(grad_hid * (1.0 + scale_two), unit, inverse)
        gmid_ref[0, rows, :] = grad_mid
        grad_gate_one += col_sum(attn * grad_mid)
    gmod_ref[0, pl.ds(0, 1), :] = grad_gate_one
    gmod_ref[0, pl.ds(1, 1), :] = grad_shift_two
    gmod_ref[0, pl.ds(2, 1), :] = grad_scale_two
    gmod_ref[0, pl.ds(3, 1), :] = grad_gate_two

    res_ref[0] = (mm(low_s[...], down_w[...]) + down_b[...]).astype(BF)
    grad_low_t = grad_low.T

    def down_weights(chunk, carry):
        units = pl.ds(pl.multiple_of(chunk * CHUNK, CHUNK), CHUNK)
        down_sum[:, units] += mm(grad_low_t, low_s[:, units])
        return carry

    lax.fori_loop(0, low_s.shape[1] // CHUNK, down_weights, 0)

    @pl.when(image == pl.num_programs(0) - 1)
    def _():
        for tap in range(9):
            small_ref[pl.ds(tap, 1), :] = col_sum(dconv_s[tap])

        rank = rank_ref[0]
        for chunk in range(hidden // CHUNK):
            units = pl.ds(chunk * CHUNK, CHUNK)
            place_rows(big_ref, fc2_sum[:, units].T.astype(BF), chunk * CHUNK, rank, parts)
            down = down_sum[:, units].T.astype(BF)
            for half in range(2):
                place_rows(
                    big_ref,
                    down[:, half * width : (half + 1) * width],
                    (1 + half) * hidden + chunk * CHUNK,
                    rank,
                    parts,
                )
        for part in range(hidden // width):
            block = fc1_sum[:, pl.ds(part * width, width)].astype(BF)
            place_rows(big_ref, block, 3 * hidden + part * width, rank, parts)


def attention_back_kernel(
    rank_ref,
    mod_ref,
    gmid_ref,
    co_ref,
    qkv_ref,
    mix_ref,
    stat_ref,
    proj_w,
    small_ref,
    *rest,
    parts,
    begin,
    last,
):
    image = pl.program_id(0)
    width = mix_ref.shape[2]
    tokens = mix_ref.shape[1] // 4
    before_ref = None if begin else rest[0]
    gqkv_ref, sum_ref = rest[0 if begin else 1 :][:2]
    rows_ref = rest[-3] if last else None
    gout_s, gmix_s = rest[-2:]

    @pl.when(image == 0)
    def _():
        sum_ref[...] = jnp.zeros(sum_ref.shape, F32) if begin else before_ref[...]

    gate_one = mod_ref[0, pl.ds(2, 1), :]
    head_size = width // HEADS
    factor = jnp.asarray(head_size ** (-0.5), BF)

    def attend(plane, carry):
        rows = pl.ds(pl.multiple_of(plane * tokens, tokens), tokens)
        grad_out = (gate_one * gmid_ref[0, rows, :]).astype(BF)
        gout_s[rows, :] = grad_out
        gmix_s[...] = mm(grad_out, proj_w[...], NT).astype(BF)
        even = lax.broadcasted_iota(jnp.int32, (tokens, LANES), 1) < head_size
        zero = jnp.zeros((tokens, LANES), BF)
        for pair in range(width // LANES):
            lane = pair * LANES
            query = qkv_ref[0, rows, pl.ds(lane, LANES)]
            key = qkv_ref[0, rows, pl.ds(width + lane, LANES)] * factor
            value = qkv_ref[0, rows, pl.ds(2 * width + lane, LANES)]
            query_low = query * factor
            key_t = key.T
            grad_mixed = gmix_s[:, pl.ds(lane, LANES)]

            def heads(values):
                return jnp.concatenate([jnp.where(even, values, zero), jnp.where(even, zero, values)], axis=0)

            def joined(values):
                return jnp.where(even, values[:tokens], values[tokens:])

            scores = mm(heads(key), query, NT)
            grad_probs = mm(heads(value), grad_mixed, NT)
            probs, grad_scores = [], []
            for half in range(2):
                part = slice(half * tokens, (half + 1) * tokens)
                prob = jnp.exp(scores[part] - stat_ref[0, plane, pl.ds(2 * pair + half, 1), :])
                weighted = prob * grad_probs[part]
                probs.append(prob.astype(BF))
                grad_scores.append((weighted - prob * col_sum(weighted)).astype(BF))
            grad_value = joined(mm(jnp.concatenate(probs, axis=0), grad_mixed))
            grad_key = joined(mm(jnp.concatenate(grad_scores, axis=0), query_low))
            grad_query_t = jnp.concatenate(
                [
                    mm(key_t[half * head_size : (half + 1) * head_size], grad_scores[half])
                    for half in range(2)
                ],
                axis=0,
            )
            gqkv_ref[0, rows, pl.ds(lane, LANES)] = grad_query_t.astype(BF).T
            gqkv_ref[0, rows, pl.ds(width + lane, LANES)] = grad_key.astype(BF)
            gqkv_ref[0, rows, pl.ds(2 * width + lane, LANES)] = grad_value.astype(BF)
        return carry

    lax.fori_loop(0, 4, attend, 0)

    sum_ref[:, pl.ds(3 * width, width)] += mm(mix_ref[0].T, gout_s[...])
    conv_t = co_ref[0].T
    for part in range(3):
        lanes = pl.ds(part * width, width)
        sum_ref[:, lanes] += mm(conv_t, gqkv_ref[0, :, lanes])

    if not last:
        return

    @pl.when(image == pl.num_programs(0) - 1)
    def _():
        rank = rank_ref[0]
        rows_ref[...] = jnp.zeros(rows_ref.shape, BF)
        for part in range(4):
            lanes = pl.ds(part * width, width)
            place_rows(rows_ref, sum_ref[:, lanes].astype(BF), part * width, rank, parts)
        for part in range(4):
            lanes = pl.ds(part * width, width)
            place_rows(rows_ref, small_ref[:, lanes].astype(BF), 4 * width + part * 16, rank, parts)


def conv_attn_back_kernel(
    strips,
    rank_ref,
    xp_ref,
    mod_ref,
    gmid_ref,
    gqkv_ref,
    qkv_w,
    conv_a,
    perm_back,
    moves,
    *refs,
):
    pieces, refs = refs[:strips], refs[strips:]
    gmod_ref, d_conv, plain_h, plain_g, moved_g, gout_s, glat_s, dconv_s = refs
    image = pl.program_id(0)
    tokens = moves.shape[1]
    cols = tokens // 16
    width = xp_ref.shape[2]
    quarter = perm_back.shape[0] // 4

    @pl.when(image == 0)
    def _():
        d_conv[...] = jnp.zeros(d_conv.shape, F32)
        dconv_s[...] = jnp.zeros(dconv_s.shape, F32)
        for ref in (plain_g, moved_g):
            zero_pads(ref, cols)

    gmod_ref[...] = jnp.zeros(gmod_ref.shape, F32)
    shift_one, scale_one = (mod_ref[0, pl.ds(part, 1), :] for part in range(2))
    for plane in range(4):
        rows = pl.ds(plane * tokens, tokens)
        grad_conv = mm(gqkv_ref[0, rows, :], qkv_w[...], NT).astype(BF)
        fill_planes(plain_g, moved_g, plane, moves[plane % 2], grad_conv, cols, pl.ds(0, width))
        unit, _ = normed(xp_ref[0, rows, :].astype(F32))
        low = (unit * (1.0 + scale_one) + shift_one).astype(BF)
        plain_h[rows, :] = low.astype(F32)
    for plane in range(4):
        for lane in range(0, width, LANES):
            for start in range(0, tokens, 128):
                lanes = pl.ds(lane, LANES)
                rows = pl.ds(plane * tokens + start, 128)
                total = conv_back_tile(
                    plain_g,
                    moved_g,
                    conv_a,
                    plain_h[rows, lanes],
                    dconv_s,
                    plane // 2,
                    plane % 2,
                    cols,
                    start,
                    128,
                    lanes,
                    lanes,
                )
                glat_s[rows, lanes] = total
    grad_shift = grad_scale = jnp.zeros((1, width), F32)
    for plane in range(4):
        rows = pl.ds(plane * tokens, tokens)
        grad_hid = glat_s[rows, :]
        unit, inverse = normed(xp_ref[0, rows, :].astype(F32))
        grad_shift += col_sum(grad_hid)
        grad_scale += col_sum(grad_hid * unit)
        gout_s[rows, :] = (
            gmid_ref[0, rows, :] + norm_back(grad_hid * (1.0 + scale_one), unit, inverse)
        ).astype(BF)
    gmod_ref[0, pl.ds(0, 1), :] = grad_shift
    gmod_ref[0, pl.ds(1, 1), :] = grad_scale
    for at, piece in enumerate(pieces):
        strip = at ^ rank_ref[1]
        gathered = jnp.concatenate(
            [
                gout_s[pl.ds(pl.multiple_of(plane * tokens + strip * quarter, quarter), quarter), :]
                for plane in range(4)
            ],
            axis=0,
        )
        piece[0] = mm(perm_back[...], gathered).astype(BF)

    @pl.when(image == pl.num_programs(0) - 1)
    def _():
        for tap in range(9):
            d_conv[pl.ds(tap, 1), :] = col_sum(dconv_s[tap])


FINISH_STEPS = 8


def finish_big_kernel(*refs):
    rows, (fc1_ref, fc2_ref, down_ref) = refs[:-3], refs[-3:]
    step = pl.program_id(0)
    share, width = rows[0].shape

    def write(ref, flat):
        for at, rows_ref in enumerate(rows):
            block, row = (0, at * share) if flat else divmod(at * share, width)
            ref[pl.ds(row, share), pl.ds(block * width, width)] = rows_ref[...].astype(F32)

    @pl.when(step < 2)
    def _():
        write(fc2_ref, True)

    @pl.when((step >= 2) & (step < 6))
    def _():
        write(down_ref, True)

    @pl.when(step >= 6)
    def _():
        write(fc1_ref, False)


def finish_rest_kernel(
    rank_ref,
    own_ref,
    other_ref,
    qkv_ref,
    proj_ref,
    conv_ffn_ref,
    fc1b_ref,
    fc2b_ref,
    downb_ref,
    conv_ref,
    ada_ref,
    bias_ref,
    *,
    share,
    images,
    features,
):
    width = proj_ref.shape[0]
    rank = rank_ref[0]
    half = own_ref.shape[0]
    near = rank < half
    for part in range(2 * half):
        at = (part ^ rank) % half
        rows = pl.ds(0, share)
        own, other = own_ref[at, rows, :], other_ref[at, rows, :]
        is_own = near if part < half else ~near
        values = jnp.where(is_own, own.astype(F32), other.astype(F32))
        block, row = divmod(part * share, width)
        if block < 3:
            qkv_ref[pl.ds(row, share), pl.ds(block * width, width)] = values
        elif block == 3:
            proj_ref[pl.ds(row, share), :] = values
        elif block == 4 and row < 64:
            small = min(share, 16)
            for first in range(0, share, small):
                block = (row + first) // 16
                lanes = pl.ds(block * width, width)
                for tap in range(9):
                    conv_ffn_ref[tap // 3, pl.ds(tap % 3, 1), lanes] = values[first + tap : first + tap + 1]
                fc1b_ref[lanes] = values[first + 9]
                if block == 0:
                    fc2b_ref[...] = values[first + 10]
                elif block < 3:
                    downb_ref[pl.ds((block - 1) * width, width)] = values[first + 10]
    conv = jnp.zeros((16, width), F32)
    for ref in (own_ref, other_ref):
        for at in range(half):
            conv += ref[at, pl.ds(share, 16), :].astype(F32)
    for tap in range(9):
        conv_ref[tap // 3, pl.ds(tap % 3, 1), :] = conv[tap : tap + 1]
    per_tile = 8 // images
    tiles = -(-6 // per_tile)

    def tile(index, lanes):
        rows = pl.ds(share + 16 + 8 * index, 8)
        return jnp.concatenate(
            [ref[:, rows, lanes].reshape(8 * half, lanes.size) for ref in (own_ref, other_ref)], axis=0
        )

    cond = tile(tiles, pl.ds(0, features))
    slot = lax.broadcasted_iota(jnp.int32, cond.shape, 0) % 8 // images
    for part in range(6):
        chosen = jnp.where(slot == part % per_tile, cond, jnp.zeros_like(cond))
        ones = jnp.where(slot == part % per_tile, jnp.ones_like(cond), jnp.zeros_like(cond))[:, :LANES]
        grads = tile(part // per_tile, pl.ds(0, width))
        lanes = pl.ds(part * width, width)
        ada_ref[:, lanes] = mm(chosen, grads, TN)
        bias_ref[lanes] = mm(ones, grads, TN)[0]


def per_image(shape, first=0):
    rest = len(shape) - 1
    return pl.BlockSpec((1,) + tuple(shape[1:]), lambda b, *_: (b + first,) + (0,) * rest)


def resident(shape):
    rank = len(shape)
    return pl.BlockSpec(tuple(shape), lambda b, *_: (0,) * rank, pipeline_mode=pl.Buffered(1))


def out_of(shape, dtype):
    return jax.ShapeDtypeStruct(shape, dtype)


PARAMS = pltpu.CompilerParams(
    dimension_semantics=("arbitrary",), vmem_limit_bytes=63 * 1024 * 1024
)


def token_tables(cols, strip):
    half = cols // 2
    spot = jnp.arange(strip)
    from_row, from_col = spot // cols, spot % cols
    target = ((from_row % 2) * 2 + from_col % 2) * (strip // 4) + (from_row // 2) * half + from_col // 2
    perm_back = (target[:, None] == spot[None, :]).astype(BF)
    perm = (spot[:, None] == target[None, :]).astype(BF)
    spot = jnp.arange(half * half)
    ahead = ((spot[None, :] == spot[:, None] + 1) & (spot[:, None] % half != half - 1)).astype(BF)
    behind = ((spot[None, :] == spot[:, None] - 1) & (spot[:, None] % half != 0)).astype(BF)
    return perm, perm_back, jnp.stack([ahead, behind])


def attention_forward_call(rank, image, images, pieces, mod, qkv_w, conv_a, perm, moves, held):
    strips = len(pieces)
    width = pieces[0].shape[1]
    tokens = moves.shape[1]
    shared = (qkv_w, conv_a, perm, moves)
    rows = 4 * tokens
    outs = [
        ((images, rows, width), BF),
        ((images, rows, width), BF),
        ((images, rows, 3 * width), BF),
        ((images, rows, width), BF),
        ((images, 4, 8, tokens), F32),
    ]
    begin = held is None
    held = () if begin else tuple(held)
    grid = pltpu.PrefetchScalarGridSpec(
        num_scalar_prefetch=1,
        grid=(1,),
        in_specs=[resident(piece.shape) for piece in pieces]
        + [per_image(mod.shape, image)]
        + [resident(w.shape) for w in shared]
        + [pl.BlockSpec(memory_space=pl.ANY)] * len(held),
        out_specs=[per_image(shape, image) for shape, _ in outs],
        scratch_shapes=[pltpu.VMEM((4, tokens + 32, width), F32)] * 2,
    )
    return pl.pallas_call(
        functools.partial(attention_forward_kernel, strips, begin),
        grid_spec=grid,
        out_shape=[out_of(shape, dtype) for shape, dtype in outs],
        input_output_aliases={} if begin else {strips + 6 + at: at for at in range(5)},
        compiler_params=PARAMS,
        cost_estimate=cost(1, 5e9, 8e6),
        name="attention_forward",
    )(rank, *pieces, mod, *shared, *held)


def feed_forward_call(rank, parts, xp, mix, mod, og, weights, moves):
    proj_w, fc1_w, fc1_b, fc2_w, fc2_b, down_w, down_b, conv_f = weights
    images, all_tokens, width = xp.shape
    tokens = moves.shape[1]
    hidden = fc1_w.shape[1]
    padded = tokens + 32
    per = (xp, mix, mod, og)
    shared = (*weights, moves)
    outs = [
        (og.shape[:2] + (down_w.shape[1],), BF),
        (xp.shape, F32),
        ((images, 8, width), F32),
    ]
    sums = [((4 * hidden, width), BF), ((16, hidden), F32)]
    grid = pltpu.PrefetchScalarGridSpec(
        num_scalar_prefetch=1,
        grid=(images,),
        in_specs=[per_image(v.shape) for v in per] + [resident(w.shape) for w in shared],
        out_specs=[per_image(s) for s, _ in outs] + [resident(s) for s, _ in sums],
        scratch_shapes=[
            pltpu.VMEM((4, tokens, width), F32),
            pltpu.VMEM((4, tokens, width), F32),
            pltpu.VMEM((2, 4, padded, CHUNK), BF),
            pltpu.VMEM((2, 4, padded, CHUNK), BF),
            pltpu.VMEM((4, padded, CHUNK), BF),
            pltpu.VMEM((4, padded, CHUNK), BF),
            pltpu.VMEM((all_tokens, width), F32),
            pltpu.VMEM((all_tokens, width), BF),
            pltpu.VMEM((all_tokens, width), BF),
            pltpu.VMEM((2, all_tokens, CHUNK), BF),
            pltpu.VMEM((2, all_tokens, CHUNK), BF),
            pltpu.VMEM((2, all_tokens, CHUNK), BF),
            pltpu.VMEM((width, all_tokens), BF),
            pltpu.VMEM((width, all_tokens), BF),
            pltpu.VMEM((tokens, 4 * width), BF),
            pltpu.VMEM((9, 8, hidden), F32),
            pltpu.VMEM((width, hidden), F32),
            pltpu.VMEM((width, hidden), F32),
            pltpu.VMEM((down_w.shape[1], hidden), F32),
        ],
    )
    return pl.pallas_call(
        functools.partial(feed_forward_kernel, parts=parts),
        grid_spec=grid,
        out_shape=[out_of(s, d) for s, d in outs + sums],
        compiler_params=PARAMS,
        cost_estimate=cost(images, 14e9, 20e6),
        name="feed_forward",
    )(rank, *per, *shared)


def cost(images, flops, moved):
    return pl.CostEstimate(
        flops=int(images * flops), bytes_accessed=int(images * moved), transcendentals=0
    )


def attention_back_call(rank, parts, group, mod, gmid, co, qkv, mix, stat, proj_w, small, before):
    images, all_tokens, width = mix.shape
    first, count = group
    begin, last = before is None, first + count == images
    per = (mod, gmid, co, qkv, mix, stat)
    shared = (proj_w, small) + (() if begin else (before,))
    share = 64 if parts <= 32 else 16
    outs = [((count,) + qkv.shape[1:], BF)]
    sums = [((width, 4 * width), F32)] + ([((share * parts, width), BF)] if last else [])
    grid = pltpu.PrefetchScalarGridSpec(
        num_scalar_prefetch=1,
        grid=(count,),
        in_specs=[per_image(v.shape, first) for v in per] + [resident(w.shape) for w in shared],
        out_specs=[per_image(s) for s, _ in outs] + [resident(s) for s, _ in sums],
        scratch_shapes=[
            pltpu.VMEM((all_tokens, width), BF),
            pltpu.VMEM((all_tokens // 4, width), BF),
        ],
    )
    return pl.pallas_call(
        functools.partial(attention_back_kernel, parts=parts, begin=begin, last=last),
        grid_spec=grid,
        out_shape=[out_of(s, d) for s, d in outs + sums],
        compiler_params=PARAMS,
        cost_estimate=cost(count, 8e9, 10e6),
        name="attention_back",
    )(rank, *per, *shared)


def conv_attn_back_call(rank, strips, first, skip, images, xp, mod, gmid, gqkv, weights, perm_back, moves):
    qkv_w, conv_a = weights
    all_tokens, width = xp.shape[1:]
    tokens = moves.shape[1]
    padded = tokens + 32
    shared = (qkv_w, conv_a, perm_back, moves)
    outs = [((images, all_tokens // strips, width), BF)] * strips + [((images, 8, width), F32)]
    sums = [(16, width)]
    grid = pltpu.PrefetchScalarGridSpec(
        num_scalar_prefetch=1,
        grid=(images,),
        in_specs=[per_image(v.shape, first) for v in (xp, mod, gmid)]
        + [per_image(gqkv.shape, skip)]
        + [resident(w.shape) for w in shared],
        out_specs=[per_image(s) for s, _ in outs] + [resident(s) for s in sums],
        scratch_shapes=[
            pltpu.VMEM((all_tokens, width), F32),
            pltpu.VMEM((4, padded, width), F32),
            pltpu.VMEM((4, padded, width), F32),
            pltpu.VMEM((all_tokens, width), BF),
            pltpu.VMEM((all_tokens, width), F32),
            pltpu.VMEM((9, 8, width), F32),
        ],
    )
    return pl.pallas_call(
        functools.partial(conv_attn_back_kernel, strips),
        grid_spec=grid,
        out_shape=[out_of(s, d) for s, d in outs] + [out_of(s, F32) for s in sums],
        compiler_params=PARAMS,
        cost_estimate=cost(images, 4e9, 8e6),
        name="conv_attn_back",
    )(rank, xp, mod, gmid, gqkv, *shared)


def finish_latents_kernel(strips, rank_ref, *refs):
    out_ref = refs[-1]
    for at in range(strips):
        out_ref[at ^ rank_ref[1], 0] = refs[at][0].astype(F32)


def finish_latents_call(rank, images, first, pieces, held):
    strips = len(pieces)
    count, tokens, width = pieces[0].shape
    shape = (strips, images, tokens, width)
    held = () if held is None else (held,)
    grid = pltpu.PrefetchScalarGridSpec(
        num_scalar_prefetch=1,
        grid=(count,),
        in_specs=[per_image(piece.shape) for piece in pieces]
        + [pl.BlockSpec(memory_space=pl.ANY)] * len(held),
        out_specs=pl.BlockSpec((strips, 1, tokens, width), lambda b, *_: (0, b + first, 0, 0)),
    )
    return pl.pallas_call(
        functools.partial(finish_latents_kernel, strips),
        grid_spec=grid,
        out_shape=out_of(shape, F32),
        input_output_aliases={strips + 1: 0} if held else {},
        compiler_params=PARAMS,
        cost_estimate=cost(count, 0, 3e6),
        name="finish_latents",
    )(rank, *pieces, *held)


def finish_big_call(rows, devices, order, hidden, width):
    count = devices // FINISH_STEPS
    share = rows.shape[0] // devices
    deep = count * share
    def owner(part):
        return sum(((part >> at) & 1) << bit for at, bit in enumerate(reversed(order)))

    return pl.pallas_call(
        finish_big_kernel,
        grid=(FINISH_STEPS,),
        in_specs=[
            pl.BlockSpec((share, width), lambda i, at=at: (owner(i * count + at), 0)) for at in range(count)
        ],
        out_specs=[
            pl.BlockSpec((width, deep), lambda i: (0, jnp.maximum(i - 6, 0))),
            pl.BlockSpec((deep, width), lambda i: (jnp.minimum(i, 1), 0)),
            pl.BlockSpec((deep, width), lambda i: (jnp.clip(i - 2, 0, 3) % 2, jnp.clip(i - 2, 0, 3) // 2)),
        ],
        out_shape=[out_of((width, hidden), F32), out_of((hidden, width), F32), out_of((hidden, 2 * width), F32)],
        compiler_params=PARAMS,
        cost_estimate=cost(1, 0, 15e6),
        name="finish_big",
    )(*[rows] * count)


def finish_rest_call(rank, own, other, share, width, images, features):
    shapes = [
        (width, 3 * width),
        (width, width),
        (3, 3, 4 * width),
        (4 * width,),
        (width,),
        (2 * width,),
        (3, 3, width),
        (features, 6 * width),
        (6 * width,),
    ]
    grid = pltpu.PrefetchScalarGridSpec(
        num_scalar_prefetch=1,
        grid=(1,),
        in_specs=[resident(own.shape), resident(other.shape)],
        out_specs=[resident(shape) for shape in shapes],
    )
    return pl.pallas_call(
        functools.partial(finish_rest_kernel, share=share, images=images, features=features),
        grid_spec=grid,
        out_shape=[out_of(shape, F32) for shape in shapes],
        compiler_params=PARAMS,
        cost_estimate=cost(1, 0, 8e6),
        name="finish_rest",
    )(rank, own, other)


def bit_order(devices, narrow):
    bits, near = devices.bit_length() - 1, narrow.bit_length() - 1
    return [0, *range(near, bits), *range(1, near)]


def stages(order):
    found = [[1 << order[0]]]
    for at in range(1, len(order), 2):
        found.append([1 << bit for bit in order[at : at + 2]])
    return found


def group_masks(group):
    if len(group) == 1:
        return [0, group[0]]
    return [0, group[1], group[0], group[0] | group[1]]


def exchange(values, mask, devices):
    return lax.ppermute(values, AXES, [(i, i ^ mask) for i in range(devices)])


def swap_strips(values, mask):
    count = lax.axis_size("narrow")
    return lax.ppermute(values, "narrow", [(i, i ^ mask) for i in range(count)])


def sent_strips(pieces):
    return [piece if at == 0 else swap_strips(piece, at) for at, piece in enumerate(pieces)]


def scatter_stage(values, group, devices):
    masks = group_masks(group)
    size = values.shape[0] // len(masks)
    total = values[:size].astype(F32)
    for at, mask in enumerate(masks[1:], 1):
        total = total + exchange(values[at * size : (at + 1) * size], mask, devices).astype(F32)
    return total.astype(BF)


def gather_stage(values, group, devices):
    masks = group_masks(group)
    return jnp.concatenate(
        [values] + [exchange(values, mask, devices) for mask in masks[1:]], axis=0
    )


def flat_rank(order):
    index = lax.axis_index("wide") * lax.axis_size("narrow") + lax.axis_index("narrow")
    rank = jnp.zeros((), jnp.int32)
    for bit in order:
        rank = 2 * rank + ((index >> bit) & 1)
    return jnp.stack([rank, lax.axis_index("narrow")])


def shards(
    latents,
    timesteps,
    out_grad,
    ada_weight,
    ada_bias,
    conv_attn,
    qkv_weight,
    proj_weight,
    fc1_weight,
    fc1_bias,
    conv_ffn,
    fc2_weight,
    fc2_bias,
    down_weight,
    down_bias,
):
    images, cols, width = out_grad.shape[0], latents.shape[2], latents.shape[3]
    height = latents.shape[1] * lax.axis_size("narrow")
    hidden = fc1_weight.shape[1]
    devices = lax.axis_size("wide") * lax.axis_size("narrow")
    order = bit_order(devices, lax.axis_size("narrow"))
    rank = flat_rank(order)
    steps = stages(order)
    strips = lax.axis_size("narrow")
    strip_tokens = latents.shape[1] * cols
    place = lax.axis_index("narrow")
    sources = latents.reshape(strips, images, strip_tokens, width)
    own_steps = lax.dynamic_slice_in_dim(timesteps, lax.axis_index("narrow") * images, images)
    half_count = ada_weight.shape[0] // 2
    freq = jnp.exp(-math.log(10000.0) * jnp.arange(half_count, dtype=F32) / half_count)
    angles = own_steps.astype(F32)[:, None] * freq[None, :]
    features = jnp.concatenate([jnp.cos(angles), jnp.sin(angles)], axis=1)
    cond = jax.nn.silu(features).astype(BF)
    mod = jnp.dot(cond, ada_weight, preferred_element_type=F32) + ada_bias.astype(F32)
    mod = jnp.pad(mod.reshape(images, 6, width), ((0, 0), (0, 2), (0, 0)))
    perm, perm_back, moves = token_tables(cols, strip_tokens)
    conv_a = jnp.pad(conv_attn.reshape(9, width).astype(F32), ((0, 7), (0, 0)))
    conv_f = jnp.pad(conv_ffn.reshape(9, hidden), ((0, 7), (0, 0)))
    low = out_grad.reshape(images, height * cols // 4, out_grad.shape[3])
    held = None
    behind = None
    for image in range(images):
        pieces = [
            lax.dynamic_slice(sources, (place ^ at, image, 0, 0), (1, 1, strip_tokens, width)).reshape(
                strip_tokens, width
            )
            for at in range(strips)
        ]
        if behind is not None:
            behind, *pieces = lax.optimization_barrier((behind, *pieces))
            held = attention_forward_call(
                rank, image - 1, images, behind, mod, qkv_weight, conv_a, perm, moves, held
            )
        behind = tuple(
            piece if at == 0 else swap_strips(piece, at) for at, piece in enumerate(pieces)
        )
    xp, co, qkv, mix, stat = attention_forward_call(
        rank, images - 1, images, behind, mod, qkv_weight, conv_a, perm, moves, held
    )
    res, gmid, gmod_two, big, small = feed_forward_call(
        rank,
        devices,
        xp,
        mix,
        mod,
        low,
        (
            proj_weight,
            fc1_weight,
            fc1_bias.astype(F32)[None],
            fc2_weight,
            fc2_bias.astype(F32)[None],
            down_weight,
            down_bias.astype(F32)[None],
            conv_f,
        ),
        moves,
    )
    split = max(images // 2, 1)
    groups = [(0, split)] + ([(split, images - split)] if images > split else [])
    later = [(image, 1) for image in range(split, images)]
    gqkvs = []
    before = None

    def attention_back(group):
        nonlocal before
        gqkv, before, *final = attention_back_call(
            rank, devices, group, mod, gmid, co, qkv, mix, stat, proj_weight, small, before
        )
        gqkvs.append(gqkv)
        return final

    def conv_attn_back(group, skip):
        *made, gmod_one, d_ca = conv_attn_back_call(
            rank, strips, group[0], skip, group[1], xp, mod, gmid, gqkvs[-1], (qkv_weight, conv_a), perm_back, moves
        )
        mods.append(gmod_one)
        convs.append(d_ca)
        return made

    mods, convs = [], []
    big = scatter_stage(big, steps[0], devices)
    mod, big = lax.optimization_barrier((mod, big))
    final = attention_back(groups[0])
    for group in steps[1:-1]:
        big = scatter_stage(big, group, devices)
    mod, big, gqkvs = lax.optimization_barrier((mod, big, gqkvs))
    made = conv_attn_back(groups[0], 0)
    big = scatter_stage(big, steps[-1], devices)
    mod, big, made = lax.optimization_barrier((mod, big, made))
    gathered = lax.all_gather(big, AXES, axis=0, tiled=True)
    outs = [sent_strips(made)]
    for group in groups[1:]:
        final = attention_back(group)
    rest, outs = lax.optimization_barrier((final[0], outs))
    stage = 0
    for at, group in enumerate(later):
        made = conv_attn_back(group, at)
        if stage < len(steps) - 1:
            rest = scatter_stage(rest, steps[stage], devices)
            stage += 1
        mod, rest, made, outs = lax.optimization_barrier((mod, rest, made, outs))
        outs.append(sent_strips(made))
    for group in steps[stage:]:
        rest = scatter_stage(rest, group, devices)
    halves = [groups[0], *later]
    grad_mod = jnp.concatenate([jnp.concatenate(mods, axis=0)[:, :2], gmod_two[:, :4]], axis=1)
    grad_mod = grad_mod.transpose(1, 0, 2).reshape(6 * images, width)
    per_tile = 8 // images
    late = jnp.concatenate(
        [
            sum(convs),
            jnp.pad(grad_mod, ((0, -grad_mod.shape[0] % 8), (0, 0))),
            jnp.pad(
                jnp.concatenate([cond.astype(F32)] * per_tile, axis=0), ((0, 0), (0, width - cond.shape[1]))
            ),
        ],
        axis=0,
    ).astype(BF)
    share = rest.shape[0]
    rest = jnp.concatenate([rest, late], axis=0)
    grad_latents = None
    for at, group in enumerate(steps[:0:-1]):
        rest = gather_stage(rest, group, devices)
        if at == 0:
            rest, outs, gathered = lax.optimization_barrier((rest, outs, gathered))
        if at == len(steps) - 2:
            finished = finish_big_call(gathered, devices, order, hidden, width)
            for (first, count), pieces in zip(halves[:2], outs):
                grad_latents = finish_latents_call(rank, images, first, pieces, grad_latents)
            rest, grad_latents, finished = lax.optimization_barrier((rest, grad_latents, finished))
    grad_fc1, grad_fc2, grad_down = finished
    for (first, count), pieces in zip(halves[2:], outs[2:]):
        grad_latents = finish_latents_call(rank, images, first, pieces, grad_latents)
    rest = rest.reshape(devices // 2, -1, width)
    other = exchange(rest, steps[0][0], devices)
    other, grad_latents = lax.optimization_barrier((other, grad_latents))
    (
        grad_qkv,
        grad_proj,
        grad_conv_ffn,
        grad_fc1b,
        grad_fc2b,
        grad_downb,
        grad_conv_attn,
        grad_ada,
        grad_ada_bias,
    ) = finish_rest_call(rank, rest, other, share, width, images, cond.shape[1])
    return (
        res.reshape(out_grad.shape),
        grad_latents.reshape(latents.shape),
        grad_ada,
        grad_ada_bias,
        grad_conv_attn,
        grad_qkv,
        grad_proj,
        grad_fc1,
        grad_fc1b,
        grad_conv_ffn,
        grad_fc2,
        grad_fc2b,
        grad_down,
        grad_downb,
    )


def solution(mesh):
    strip = P("wide", "narrow", None, None)
    image = P(AXES, None, None, None)
    in_specs = (strip, P("wide"), image) + (P(),) * 12
    out_specs = (image, strip) + (P(),) * 12
    return jax.shard_map(shards, mesh=mesh, in_specs=in_specs, out_specs=out_specs, check_vma=False)
```

```python
import functools
import math

import jax
import jax.numpy as jnp
from jax import lax
from jax.experimental import pallas as pl
from jax.experimental.pallas import tpu as pltpu
from jax.sharding import PartitionSpec as P

HEADS = 6
EPSILON = 1e-06
HIGH = lax.Precision.HIGHEST
BF = jnp.bfloat16
F32 = jnp.float32
NN = ((1,), (0,))
NT = ((1,), (1,))
TN = ((0,), (0,))
LANES = 128
CHUNK = 256
TILE = 64
GELU_A = math.sqrt(2.0 / math.pi)
GELU_B = 0.044715
AXES = ("wide", "narrow")


def mm(left, right, dims=NN):
    return lax.dot_general(left, right, (dims, ((), ())), preferred_element_type=F32)


def col_sum(values):
    return jnp.sum(values, axis=0, keepdims=True)


def row_mean(values):
    return jnp.mean(values, axis=1, keepdims=True)


def normed(values):
    center = values - row_mean(values)
    spread = row_mean(center * center)
    inverse = lax.rsqrt(spread + EPSILON)
    return center * inverse, inverse


def norm_back(grad_normed, normed_values, inverse):
    return inverse * (
        grad_normed - row_mean(grad_normed) - normed_values * row_mean(grad_normed * normed_values)
    )


def tap_source(phase, tap):
    distance = phase + tap - 1
    return distance % 2, distance // 2


def tap_ref(plain, moved, row_phase, col_phase, row_tap, col_tap, cols, start, size, lanes):
    source_row, row_move = tap_source(row_phase, row_tap)
    source_col, col_move = tap_source(col_phase, col_tap)
    held = plain if col_move == 0 else moved
    return held[2 * source_row + source_col, pl.ds(cols + cols * row_move + start, size), lanes]


def fill_planes(plain, moved, plane, col_phase_matrix, values_low, cols, lanes):
    tokens = values_low.shape[0]
    plain[plane, pl.ds(cols, tokens), lanes] = values_low.astype(F32)
    moved[plane, pl.ds(cols, tokens), lanes] = mm(col_phase_matrix, values_low)


def conv_tile(plain, moved, weight, row_phase, col_phase, cols, start, size, lanes, lanes_weight):
    total = None
    for row_tap in range(3):
        for col_tap in range(3):
            window = tap_ref(
                plain, moved, row_phase, col_phase, row_tap, col_tap, cols, start, size, lanes
            )
            part = window * weight[pl.ds(row_tap * 3 + col_tap, 1), lanes_weight]
            total = part if total is None else total + part
    return total


def conv_back_tile(
    plain, moved, weight, inputs, kernel_grad, row_phase, col_phase, cols, start, size, lanes, lanes_weight
):
    total = None
    for row_tap in range(3):
        for col_tap in range(3):
            window = tap_ref(
                plain, moved, row_phase, col_phase, row_tap, col_tap, cols, start, size, lanes
            )
            mirror = (2 - row_tap) * 3 + (2 - col_tap)
            part = window * weight[pl.ds(mirror, 1), lanes_weight]
            total = part if total is None else total + part
            product = jnp.sum((window * inputs).reshape(size // 8, 8, LANES), axis=0)
            kernel_grad[mirror, :, lanes_weight] += product
    return total


def packed(values):
    return values.reshape(values.shape[0] // 8, 8, values.shape[1])


def kernel_rows(weight, lanes):
    return [jnp.broadcast_to(weight[pl.ds(tap, 1), lanes], (8, lanes.size)) for tap in range(9)]


def conv_packed(plain, moved, taps, row_phase, col_phase, cols, start, lanes):
    total = None
    for row_tap in range(3):
        for col_tap in range(3):
            window = packed(
                tap_ref(plain, moved, row_phase, col_phase, row_tap, col_tap, cols, start, TILE, lanes)
            )
            part = window * taps[row_tap * 3 + col_tap]
            total = part if total is None else total + part
    return total


def conv_back_packed(plain, moved, taps, inputs, row_phase, col_phase, cols, start, lanes):
    total = None
    sums = [None] * 9
    for row_tap in range(3):
        for col_tap in range(3):
            window = packed(
                tap_ref(plain, moved, row_phase, col_phase, row_tap, col_tap, cols, start, TILE, lanes)
            )
            mirror = (2 - row_tap) * 3 + (2 - col_tap)
            part = window * taps[mirror]
            total = part if total is None else total + part
            product = window * inputs
            count = product.shape[0]
            while count > 1:
                count //= 2
                product = product[:count] + product[count:]
            sums[mirror] = product[0].astype(F32)
    return total, sums


def column_moved(values, col_phase, cols):
    tokens, lanes = values.shape
    turned = pltpu.roll(values, 1 if col_phase else tokens - 1, 0).reshape(tokens // cols, cols, lanes)
    spot = lax.broadcasted_iota(jnp.int32, (1, cols, lanes), 1)
    edge = 0 if col_phase else cols - 1
    return jnp.where(spot == edge, 0.0, turned).reshape(tokens, lanes)


def fill_packed(plain, moved, plane, values, cols):
    rows = pl.ds(cols, values.shape[0])
    plain[plane, rows, :] = values.astype(BF)
    moved[plane, rows, :] = column_moved(values, plane % 2, cols).astype(BF)


def place_rows(ref, values, first_row, rank, parts):
    share = ref.shape[0] // parts
    step = math.gcd(math.gcd(share, values.shape[0]), first_row)
    for at in range(0, values.shape[0], step):
        part, rest = divmod(first_row + at, share)
        row = pl.multiple_of((part ^ rank) * share + rest, step)
        ref[pl.ds(row, step), :] = values[at : at + step]


def zero_pads(buffer, cols):
    planes, padded, width = buffer.shape
    edge = jnp.zeros((planes, cols, width), buffer.dtype)
    buffer[:, pl.ds(0, cols), :] = edge
    buffer[:, pl.ds(padded - cols, cols), :] = edge


def attention_forward_kernel(strips, begin, rank_ref, *refs):
    pieces, refs = refs[:strips], refs[strips:]
    mod_ref, qkv_w, conv_a, perm, moves = refs[:5]
    refs = refs[5:] if begin else refs[10:]
    xp_ref, co_ref, qkv_ref, mix_ref, stat_ref, plain_h, moved_h = refs
    tokens = moves.shape[1]
    cols = tokens // 16
    width = xp_ref.shape[2]
    quarter = perm.shape[0] // 4
    for ref in (plain_h, moved_h):
        zero_pads(ref, cols)
    shift_one, scale_one = (mod_ref[0, pl.ds(part, 1), :] for part in range(2))

    for at, piece in enumerate(pieces):
        strip = at ^ rank_ref[1]
        moved_piece = mm(perm[...], piece[...]).astype(BF)
        for plane in range(4):
            row = pl.multiple_of(plane * tokens + strip * quarter, quarter)
            xp_ref[0, pl.ds(row, quarter), :] = moved_piece[plane * quarter : (plane + 1) * quarter]

    for plane in range(4):
        unit, _ = normed(xp_ref[0, pl.ds(plane * tokens, tokens), :].astype(F32))
        low = (unit * (1.0 + scale_one) + shift_one).astype(BF)
        fill_planes(plain_h, moved_h, plane, moves[plane % 2], low, cols, pl.ds(0, width))
    for plane in range(4):
        for lane in range(0, width, LANES):
            for start in range(0, tokens, 128):
                lanes = pl.ds(lane, LANES)
                total = conv_tile(
                    plain_h, moved_h, conv_a, plane // 2, plane % 2, cols, start, 128, lanes, lanes
                )
                co_ref[0, pl.ds(plane * tokens + start, 128), lanes] = total.astype(BF)

    head_size = width // HEADS
    factor = head_size ** (-0.5)

    def attend(plane, carry):
        rows = pl.ds(pl.multiple_of(plane * tokens, tokens), tokens)
        qkv_ref[0, rows, :] = mm(co_ref[0, rows, :], qkv_w[...]).astype(BF)
        even = lax.broadcasted_iota(jnp.int32, (tokens, LANES), 1) < head_size
        scores = []
        zero = jnp.zeros((tokens, LANES), BF)
        for pair in range(width // LANES):
            query = qkv_ref[0, rows, pl.ds(pair * LANES, LANES)]
            key = qkv_ref[0, rows, pl.ds(width + pair * LANES, LANES)] * jnp.asarray(factor, BF)
            both = mm(jnp.concatenate([jnp.where(even, key, zero), jnp.where(even, zero, key)], axis=0), query, NT)
            scores += [both[:tokens], both[tokens:]]
        tops = [jnp.max(score, axis=0, keepdims=True) for score in scores]
        grown = [jnp.exp(score - top) for score, top in zip(scores, tops)]
        totals = [col_sum(values) for values in grown]
        probs = [(values * (1.0 / total)).astype(BF) for values, total in zip(grown, totals)]
        for pair in range(width // LANES):
            value_t = qkv_ref[0, rows, pl.ds(2 * width + pair * LANES, LANES)].T
            mixed_t = jnp.concatenate(
                [
                    mm(value_t[half * head_size : (half + 1) * head_size], probs[2 * pair + half])
                    for half in range(2)
                ],
                axis=0,
            )
            mix_ref[0, rows, pl.ds(pair * LANES, LANES)] = mixed_t.astype(BF).T
        for head in range(HEADS):
            stat_ref[0, plane, pl.ds(head, 1), :] = tops[head] + jnp.log(totals[head])
        return carry

    lax.fori_loop(0, 4, attend, 0)


def feed_forward_kernel(
    rank_ref,
    xp_ref,
    mix_ref,
    mod_ref,
    og_ref,
    proj_w,
    fc1_w,
    fc1_b,
    fc2_w,
    fc2_b,
    down_w,
    down_b,
    conv_f,
    moves,
    res_ref,
    gmid_ref,
    gmod_ref,
    big_ref,
    small_ref,
    fout_s,
    ghid_s,
    plain_p,
    moved_p,
    plain_g,
    moved_g,
    attn_s,
    gffn_s,
    hid_s,
    act_s,
    gpre_s,
    gact_s,
    hid_t,
    gffn_t,
    low_s,
    dconv_s,
    fc1_sum,
    fc2_sum,
    down_sum,
    *,
    parts,
):
    image = pl.program_id(0)
    tokens = moves.shape[1]
    cols = tokens // 16
    width = xp_ref.shape[2]
    hidden = fc1_w.shape[1]

    @pl.when(image == 0)
    def _():
        for ref in (fc1_sum, fc2_sum, down_sum, small_ref, dconv_s):
            ref[...] = jnp.zeros(ref.shape, F32)
        hid_t[pl.ds(width, 16), :] = jnp.ones((16, hid_t.shape[1]), BF)
        for ref in (plain_g, moved_g):
            zero_pads(ref, cols)
        for ref in (plain_p, moved_p):
            for slot in range(2):
                zero_pads(ref.at[slot], cols)

    gmod_ref[...] = jnp.zeros(gmod_ref.shape, F32)
    gate_one, shift_two, scale_two, gate_two = (mod_ref[0, pl.ds(part, 1), :] for part in range(2, 6))
    attn_s[...] = mm(mix_ref[0], proj_w[...])

    grad_low = og_ref[0]
    small_ref[pl.ds(10, 1), pl.ds(width, 2 * width)] += col_sum(grad_low.astype(F32))
    grad_all = mm(grad_low, down_w[...], NT)
    for plane in range(4):
        rows = pl.ds(plane * tokens, tokens)
        grad_after = grad_all[:, plane * width : (plane + 1) * width]
        gmid_ref[0, rows, :] = grad_after
        grad_out = (gate_two * grad_after).astype(BF)
        gffn_s[rows, :] = grad_out
        small_ref[pl.ds(10, 1), pl.ds(0, width)] += col_sum(grad_out.astype(F32))
        after = xp_ref[0, rows, :].astype(F32) + gate_one * attn_s[rows, :]
        unit, _ = normed(after)
        hid_s[rows, :] = (unit * (1.0 + scale_two) + shift_two).astype(BF)

    hid_t[pl.ds(0, width), :] = hid_s[...].T
    gffn_t[...] = gffn_s[...].T
    chunks = hidden // CHUNK

    def units_of(chunk):
        return pl.ds(pl.multiple_of(chunk * CHUNK, CHUNK), CHUNK)

    def prepare(chunk, slot):
        units = units_of(chunk)
        pre = mm(hid_s[...], fc1_w[:, units]) + fc1_b[:, units]
        for plane in range(4):
            fill_packed(
                plain_p.at[slot],
                moved_p.at[slot],
                plane,
                pre[plane * tokens : (plane + 1) * tokens],
                cols,
            )
        gact_s[slot] = mm(gffn_s[...], fc2_w[units, :], NT).astype(gact_s.dtype)

    def collect(chunk, slot):
        units = units_of(chunk)
        grad_pre = gpre_s[slot]
        active = act_s[slot]
        sums = mm(hid_t[...], grad_pre)
        fc1_sum[:, units] += sums[:width]
        small_ref[pl.ds(9, 1), units] += sums[width : width + 1]
        fc2_sum[:, units] += mm(gffn_t[...], active)
        out = mm(active, fc2_w[units, :])
        grad_hid = mm(grad_pre, fc1_w[:, units], NT)
        for plane in range(4):
            part = slice(plane * tokens, (plane + 1) * tokens)
            fout_s[plane] += out[part]
            ghid_s[plane] += grad_hid[part]

    def convolve(chunk, slot):
        units = units_of(chunk)
        taps = kernel_rows(conv_f, units)
        chunk_lanes = pl.ds(0, CHUNK)
        plain, moved = plain_p.at[slot], moved_p.at[slot]
        for plane in range(4):
            for start in range(0, tokens, TILE):
                rows = pl.ds(plane * tokens + start, TILE)
                value = conv_packed(plain, moved, taps, plane // 2, plane % 2, cols, start, chunk_lanes)
                value_low = value.reshape(TILE, CHUNK)
                value = value_low.astype(F32)
                square = value * value
                half = 0.5 * jnp.tanh(value * (GELU_A + (GELU_A * GELU_B) * square))
                gate = 0.5 + half
                act_s[slot, rows, :] = (value * gate).astype(BF)
                gate_low = gate.astype(BF)
                bend = (value_low * (0.5 - half).astype(BF)) * (
                    jnp.asarray(2.0 * GELU_A, BF)
                    + (value_low * value_low) * jnp.asarray(6.0 * GELU_A * GELU_B, BF)
                )
                slope = gate_low + gate_low * bend
                plain_g[plane, pl.ds(cols + start, TILE), :] = slope * gact_s[slot, rows, :]
            rows = pl.ds(cols, tokens)
            moved_g[plane, rows, :] = mm(moves[plane % 2], plain_g[plane, rows, :]).astype(BF)
        kernel_grads = None
        for plane in range(4):
            for start in range(0, tokens, TILE):
                inputs = packed(plain[plane, pl.ds(cols + start, TILE), :])
                total, sums = conv_back_packed(
                    plain_g, moved_g, taps, inputs, plane // 2, plane % 2, cols, start, chunk_lanes
                )
                gpre_s[slot, pl.ds(plane * tokens + start, TILE), :] = total.reshape(TILE, CHUNK)
                kernel_grads = (
                    sums if kernel_grads is None else [a + b for a, b in zip(kernel_grads, sums)]
                )
        for tap in range(9):
            dconv_s[tap, :, units] += kernel_grads[tap]

    for ref in (fout_s, ghid_s):
        ref[...] = jnp.zeros(ref.shape, F32)
    for ref in (act_s, gpre_s):
        ref[1] = jnp.zeros(ref.shape[1:], BF)
    prepare(0, 0)

    def feed(step, carry):
        chunk = 2 * step
        prepare(chunk + 1, 1)
        collect(jnp.maximum(chunk - 1, 0), 1)
        convolve(chunk, 0)
        prepare(jnp.minimum(chunk + 2, chunks - 1), 0)
        collect(chunk, 0)
        convolve(chunk + 1, 1)
        return carry

    lax.fori_loop(0, chunks // 2, feed, 0)
    collect(chunks - 1, 1)

    grad_gate_one = grad_shift_two = grad_scale_two = grad_gate_two = jnp.zeros((1, width), F32)
    for plane in range(4):
        rows = pl.ds(plane * tokens, tokens)
        attn = attn_s[rows, :]
        after = xp_ref[0, rows, :].astype(F32) + gate_one * attn
        grad_after = gmid_ref[0, rows, :]
        out = fout_s[plane] + fc2_b[...]
        grad_gate_two += col_sum(out * grad_after)
        low_s[:, pl.ds(plane * width, width)] = (after + gate_two * out).astype(BF)
        grad_hid = ghid_s[plane]
        unit, inverse = normed(after)
        grad_shift_two += col_sum(grad_hid)
        grad_scale_two += col_sum(grad_hid * unit)
        grad_mid = grad_after + norm_back(grad_hid * (1.0 + scale_two), unit, inverse)
        gmid_ref[0, rows, :] = grad_mid
        grad_gate_one += col_sum(attn * grad_mid)
    gmod_ref[0, pl.ds(0, 1), :] = grad_gate_one
    gmod_ref[0, pl.ds(1, 1), :] = grad_shift_two
    gmod_ref[0, pl.ds(2, 1), :] = grad_scale_two
    gmod_ref[0, pl.ds(3, 1), :] = grad_gate_two

    res_ref[0] = (mm(low_s[...], down_w[...]) + down_b[...]).astype(BF)
    grad_low_t = grad_low.T

    def down_weights(chunk, carry):
        units = pl.ds(pl.multiple_of(chunk * CHUNK, CHUNK), CHUNK)
        down_sum[:, units] += mm(grad_low_t, low_s[:, units])
        return carry

    lax.fori_loop(0, low_s.shape[1] // CHUNK, down_weights, 0, unroll=True)

    @pl.when(image == pl.num_programs(0) - 1)
    def _():
        for tap in range(9):
            small_ref[pl.ds(tap, 1), :] = col_sum(dconv_s[tap])

        rank = rank_ref[0]
        for chunk in range(hidden // CHUNK):
            units = pl.ds(chunk * CHUNK, CHUNK)
            place_rows(big_ref, fc2_sum[:, units].T.astype(BF), chunk * CHUNK, rank, parts)
            down = down_sum[:, units].T.astype(BF)
            for half in range(2):
                place_rows(
                    big_ref,
                    down[:, half * width : (half + 1) * width],
                    (1 + half) * hidden + chunk * CHUNK,
                    rank,
                    parts,
                )
        for part in range(hidden // width):
            block = fc1_sum[:, pl.ds(part * width, width)].astype(BF)
            place_rows(big_ref, block, 3 * hidden + part * width, rank, parts)


def attention_back_kernel(
    rank_ref,
    mod_ref,
    gmid_ref,
    co_ref,
    qkv_ref,
    mix_ref,
    stat_ref,
    proj_w,
    small_ref,
    *rest,
    parts,
    begin,
    last,
):
    image = pl.program_id(0)
    width = mix_ref.shape[2]
    tokens = mix_ref.shape[1] // 4
    before_ref = None if begin else rest[0]
    gqkv_ref, sum_ref = rest[0 if begin else 1 :][:2]
    rows_ref = rest[-3] if last else None
    gout_s, gmix_s = rest[-2:]

    @pl.when(image == 0)
    def _():
        sum_ref[...] = jnp.zeros(sum_ref.shape, F32) if begin else before_ref[...]

    gate_one = mod_ref[0, pl.ds(2, 1), :]
    head_size = width // HEADS
    factor = jnp.asarray(head_size ** (-0.5), BF)

    gout_s[...] = (gate_one * gmid_ref[0]).astype(BF)
    gmix_s[...] = mm(gout_s[...], proj_w[...], NT).astype(BF)

    def attend(plane, carry):
        rows = pl.ds(pl.multiple_of(plane * tokens, tokens), tokens)
        even = lax.broadcasted_iota(jnp.int32, (tokens, LANES), 1) < head_size
        zero = jnp.zeros((tokens, LANES), BF)
        for pair in range(width // LANES):
            lane = pair * LANES
            query = qkv_ref[0, rows, pl.ds(lane, LANES)]
            key = qkv_ref[0, rows, pl.ds(width + lane, LANES)] * factor
            value = qkv_ref[0, rows, pl.ds(2 * width + lane, LANES)]
            query_low = query * factor
            key_t = key.T
            grad_mixed = gmix_s[rows, pl.ds(lane, LANES)]

            def heads(values):
                return jnp.concatenate([jnp.where(even, values, zero), jnp.where(even, zero, values)], axis=0)

            def joined(values):
                return jnp.where(even, values[:tokens], values[tokens:])

            scores = mm(heads(key), query, NT)
            grad_probs = mm(heads(value), grad_mixed, NT)
            probs, grad_scores = [], []
            for half in range(2):
                part = slice(half * tokens, (half + 1) * tokens)
                prob = jnp.exp(scores[part] - stat_ref[0, plane, pl.ds(2 * pair + half, 1), :])
                weighted = prob * grad_probs[part]
                probs.append(prob.astype(BF))
                grad_scores.append((weighted - prob * col_sum(weighted)).astype(BF))
            grad_value = joined(mm(jnp.concatenate(probs, axis=0), grad_mixed))
            grad_key = joined(mm(jnp.concatenate(grad_scores, axis=0), query_low))
            grad_query_t = jnp.concatenate(
                [
                    mm(key_t[half * head_size : (half + 1) * head_size], grad_scores[half])
                    for half in range(2)
                ],
                axis=0,
            )
            gqkv_ref[0, rows, pl.ds(lane, LANES)] = grad_query_t.astype(BF).T
            gqkv_ref[0, rows, pl.ds(width + lane, LANES)] = grad_key.astype(BF)
            gqkv_ref[0, rows, pl.ds(2 * width + lane, LANES)] = grad_value.astype(BF)
        return carry

    lax.fori_loop(0, 4, attend, 0, unroll=2)

    sum_ref[:, pl.ds(3 * width, width)] += mm(mix_ref[0].T, gout_s[...])
    conv_t = co_ref[0].T
    for part in range(3):
        lanes = pl.ds(part * width, width)
        sum_ref[:, lanes] += mm(conv_t, gqkv_ref[0, :, lanes])

    if not last:
        return

    @pl.when(image == pl.num_programs(0) - 1)
    def _():
        rank = rank_ref[0]
        rows_ref[...] = jnp.zeros(rows_ref.shape, BF)
        for part in range(4):
            lanes = pl.ds(part * width, width)
            place_rows(rows_ref, sum_ref[:, lanes].astype(BF), part * width, rank, parts)
        for part in range(4):
            lanes = pl.ds(part * width, width)
            place_rows(rows_ref, small_ref[:, lanes].astype(BF), 4 * width + part * 16, rank, parts)


def conv_attn_back_kernel(
    strips,
    rank_ref,
    xp_ref,
    mod_ref,
    gmid_ref,
    gqkv_ref,
    qkv_w,
    conv_a,
    perm_back,
    moves,
    *refs,
):
    pieces, refs = refs[:strips], refs[strips:]
    gmod_ref, d_conv, plain_h, plain_g, moved_g, gout_s, glat_s, dconv_s = refs
    image = pl.program_id(0)
    tokens = moves.shape[1]
    cols = tokens // 16
    width = xp_ref.shape[2]
    quarter = perm_back.shape[0] // 4

    @pl.when(image == 0)
    def _():
        d_conv[...] = jnp.zeros(d_conv.shape, F32)
        dconv_s[...] = jnp.zeros(dconv_s.shape, F32)
        for ref in (plain_g, moved_g):
            zero_pads(ref, cols)

    gmod_ref[...] = jnp.zeros(gmod_ref.shape, F32)
    shift_one, scale_one = (mod_ref[0, pl.ds(part, 1), :] for part in range(2))
    for plane in range(4):
        rows = pl.ds(plane * tokens, tokens)
        grad_conv = mm(gqkv_ref[0, rows, :], qkv_w[...], NT).astype(BF)
        fill_planes(plain_g, moved_g, plane, moves[plane % 2], grad_conv, cols, pl.ds(0, width))
        unit, _ = normed(xp_ref[0, rows, :].astype(F32))
        low = (unit * (1.0 + scale_one) + shift_one).astype(BF)
        plain_h[rows, :] = low.astype(F32)
    for plane in range(4):
        for lane in range(0, width, LANES):
            for start in range(0, tokens, 128):
                lanes = pl.ds(lane, LANES)
                rows = pl.ds(plane * tokens + start, 128)
                total = conv_back_tile(
                    plain_g,
                    moved_g,
                    conv_a,
                    plain_h[rows, lanes],
                    dconv_s,
                    plane // 2,
                    plane % 2,
                    cols,
                    start,
                    128,
                    lanes,
                    lanes,
                )
                glat_s[rows, lanes] = total
    grad_shift = grad_scale = jnp.zeros((1, width), F32)
    for plane in range(4):
        rows = pl.ds(plane * tokens, tokens)
        grad_hid = glat_s[rows, :]
        unit, inverse = normed(xp_ref[0, rows, :].astype(F32))
        grad_shift += col_sum(grad_hid)
        grad_scale += col_sum(grad_hid * unit)
        gout_s[rows, :] = (
            gmid_ref[0, rows, :] + norm_back(grad_hid * (1.0 + scale_one), unit, inverse)
        ).astype(BF)
    gmod_ref[0, pl.ds(0, 1), :] = grad_shift
    gmod_ref[0, pl.ds(1, 1), :] = grad_scale
    for at, piece in enumerate(pieces):
        strip = at ^ rank_ref[1]
        gathered = jnp.concatenate(
            [
                gout_s[pl.ds(pl.multiple_of(plane * tokens + strip * quarter, quarter), quarter), :]
                for plane in range(4)
            ],
            axis=0,
        )
        piece[0] = mm(perm_back[...], gathered).astype(BF)

    @pl.when(image == pl.num_programs(0) - 1)
    def _():
        for tap in range(9):
            d_conv[pl.ds(tap, 1), :] = col_sum(dconv_s[tap])


FINISH_STEPS = 8


def finish_big_kernel(*refs):
    rows, (fc1_ref, fc2_ref, down_ref) = refs[:-3], refs[-3:]
    step = pl.program_id(0)
    share, width = rows[0].shape

    def write(ref, flat):
        for at, rows_ref in enumerate(rows):
            block, row = (0, at * share) if flat else divmod(at * share, width)
            ref[pl.ds(row, share), pl.ds(block * width, width)] = rows_ref[...].astype(F32)

    @pl.when(step < 2)
    def _():
        write(fc2_ref, True)

    @pl.when((step >= 2) & (step < 6))
    def _():
        write(down_ref, True)

    @pl.when(step >= 6)
    def _():
        write(fc1_ref, False)


def finish_rest_kernel(
    rank_ref,
    own_ref,
    other_ref,
    qkv_ref,
    proj_ref,
    conv_ffn_ref,
    fc1b_ref,
    fc2b_ref,
    downb_ref,
    conv_ref,
    ada_ref,
    bias_ref,
    *,
    share,
    images,
    features,
):
    width = proj_ref.shape[0]
    rank = rank_ref[0]
    half = own_ref.shape[0]
    near = rank < half
    for part in range(2 * half):
        at = (part ^ rank) % half
        rows = pl.ds(0, share)
        own, other = own_ref[at, rows, :], other_ref[at, rows, :]
        is_own = near if part < half else ~near
        values = jnp.where(is_own, own.astype(F32), other.astype(F32))
        block, row = divmod(part * share, width)
        if block < 3:
            qkv_ref[pl.ds(row, share), pl.ds(block * width, width)] = values
        elif block == 3:
            proj_ref[pl.ds(row, share), :] = values
        elif block == 4 and row < 64:
            small = min(share, 16)
            for first in range(0, share, small):
                block = (row + first) // 16
                lanes = pl.ds(block * width, width)
                for tap in range(9):
                    conv_ffn_ref[tap // 3, pl.ds(tap % 3, 1), lanes] = values[first + tap : first + tap + 1]
                fc1b_ref[lanes] = values[first + 9]
                if block == 0:
                    fc2b_ref[...] = values[first + 10]
                elif block < 3:
                    downb_ref[pl.ds((block - 1) * width, width)] = values[first + 10]
    conv = jnp.zeros((16, width), F32)
    for ref in (own_ref, other_ref):
        for at in range(half):
            conv += ref[at, pl.ds(share, 16), :].astype(F32)
    for tap in range(9):
        conv_ref[tap // 3, pl.ds(tap % 3, 1), :] = conv[tap : tap + 1]
    per_tile = 8 // images
    tiles = -(-6 // per_tile)

    def tile(index, lanes):
        rows = pl.ds(share + 16 + 8 * index, 8)
        return jnp.concatenate(
            [ref[:, rows, lanes].reshape(8 * half, lanes.size) for ref in (own_ref, other_ref)], axis=0
        )

    cond = tile(tiles, pl.ds(0, features))
    slot = lax.broadcasted_iota(jnp.int32, cond.shape, 0) % 8 // images
    for part in range(6):
        chosen = jnp.where(slot == part % per_tile, cond, jnp.zeros_like(cond))
        ones = jnp.where(slot == part % per_tile, jnp.ones_like(cond), jnp.zeros_like(cond))[:, :LANES]
        grads = tile(part // per_tile, pl.ds(0, width))
        lanes = pl.ds(part * width, width)
        ada_ref[:, lanes] = mm(chosen, grads, TN)
        bias_ref[lanes] = mm(ones, grads, TN)[0]


def per_image(shape, first=0):
    rest = len(shape) - 1
    return pl.BlockSpec((1,) + tuple(shape[1:]), lambda b, *_: (b + first,) + (0,) * rest)


def resident(shape):
    rank = len(shape)
    return pl.BlockSpec(tuple(shape), lambda b, *_: (0,) * rank, pipeline_mode=pl.Buffered(1))


def out_of(shape, dtype):
    return jax.ShapeDtypeStruct(shape, dtype)


PARAMS = pltpu.CompilerParams(
    dimension_semantics=("arbitrary",), vmem_limit_bytes=63 * 1024 * 1024
)


def token_tables(cols, strip):
    half = cols // 2
    spot = jnp.arange(strip)
    from_row, from_col = spot // cols, spot % cols
    target = ((from_row % 2) * 2 + from_col % 2) * (strip // 4) + (from_row // 2) * half + from_col // 2
    perm_back = (target[:, None] == spot[None, :]).astype(BF)
    perm = (spot[:, None] == target[None, :]).astype(BF)
    spot = jnp.arange(half * half)
    ahead = ((spot[None, :] == spot[:, None] + 1) & (spot[:, None] % half != half - 1)).astype(BF)
    behind = ((spot[None, :] == spot[:, None] - 1) & (spot[:, None] % half != 0)).astype(BF)
    return perm, perm_back, jnp.stack([ahead, behind])


def attention_forward_call(rank, image, images, pieces, mod, qkv_w, conv_a, perm, moves, held):
    strips = len(pieces)
    width = pieces[0].shape[1]
    tokens = moves.shape[1]
    shared = (qkv_w, conv_a, perm, moves)
    rows = 4 * tokens
    outs = [
        ((images, rows, width), BF),
        ((images, rows, width), BF),
        ((images, rows, 3 * width), BF),
        ((images, rows, width), BF),
        ((images, 4, 8, tokens), F32),
    ]
    begin = held is None
    held = () if begin else tuple(held)
    grid = pltpu.PrefetchScalarGridSpec(
        num_scalar_prefetch=1,
        grid=(1,),
        in_specs=[resident(piece.shape) for piece in pieces]
        + [per_image(mod.shape, image)]
        + [resident(w.shape) for w in shared]
        + [pl.BlockSpec(memory_space=pl.ANY)] * len(held),
        out_specs=[per_image(shape, image) for shape, _ in outs],
        scratch_shapes=[pltpu.VMEM((4, tokens + 32, width), F32)] * 2,
    )
    return pl.pallas_call(
        functools.partial(attention_forward_kernel, strips, begin),
        grid_spec=grid,
        out_shape=[out_of(shape, dtype) for shape, dtype in outs],
        input_output_aliases={} if begin else {strips + 6 + at: at for at in range(5)},
        compiler_params=PARAMS,
        cost_estimate=cost(1, 5e9, 8e6),
        name="attention_forward",
    )(rank, *pieces, mod, *shared, *held)


def feed_forward_call(rank, parts, xp, mix, mod, og, weights, moves):
    proj_w, fc1_w, fc1_b, fc2_w, fc2_b, down_w, down_b, conv_f = weights
    images, all_tokens, width = xp.shape
    tokens = moves.shape[1]
    hidden = fc1_w.shape[1]
    padded = tokens + 32
    per = (xp, mix, mod, og)
    shared = (*weights, moves)
    outs = [
        (og.shape[:2] + (down_w.shape[1],), BF),
        (xp.shape, F32),
        ((images, 8, width), F32),
    ]
    sums = [((4 * hidden, width), BF), ((16, hidden), F32)]
    grid = pltpu.PrefetchScalarGridSpec(
        num_scalar_prefetch=1,
        grid=(images,),
        in_specs=[per_image(v.shape) for v in per] + [resident(w.shape) for w in shared],
        out_specs=[per_image(s) for s, _ in outs] + [resident(s) for s, _ in sums],
        scratch_shapes=[
            pltpu.VMEM((4, tokens, width), F32),
            pltpu.VMEM((4, tokens, width), F32),
            pltpu.VMEM((2, 4, padded, CHUNK), BF),
            pltpu.VMEM((2, 4, padded, CHUNK), BF),
            pltpu.VMEM((4, padded, CHUNK), BF),
            pltpu.VMEM((4, padded, CHUNK), BF),
            pltpu.VMEM((all_tokens, width), F32),
            pltpu.VMEM((all_tokens, width), BF),
            pltpu.VMEM((all_tokens, width), BF),
            pltpu.VMEM((2, all_tokens, CHUNK), BF),
            pltpu.VMEM((2, all_tokens, CHUNK), BF),
            pltpu.VMEM((2, all_tokens, CHUNK), BF),
            pltpu.VMEM((width + 16, all_tokens), BF),
            pltpu.VMEM((width, all_tokens), BF),
            pltpu.VMEM((tokens, 4 * width), BF),
            pltpu.VMEM((9, 8, hidden), F32),
            pltpu.VMEM((width, hidden), F32),
            pltpu.VMEM((width, hidden), F32),
            pltpu.VMEM((down_w.shape[1], hidden), F32),
        ],
    )
    return pl.pallas_call(
        functools.partial(feed_forward_kernel, parts=parts),
        grid_spec=grid,
        out_shape=[out_of(s, d) for s, d in outs + sums],
        compiler_params=PARAMS,
        cost_estimate=cost(images, 14e9, 20e6),
        name="feed_forward",
    )(rank, *per, *shared)


def cost(images, flops, moved):
    return pl.CostEstimate(
        flops=int(images * flops), bytes_accessed=int(images * moved), transcendentals=0
    )


def attention_back_call(rank, parts, group, mod, gmid, co, qkv, mix, stat, proj_w, small, before):
    images, all_tokens, width = mix.shape
    first, count = group
    begin, last = before is None, first + count == images
    per = (mod, gmid, co, qkv, mix, stat)
    shared = (proj_w, small) + (() if begin else (before,))
    share = 64 if parts <= 32 else 16
    outs = [((count,) + qkv.shape[1:], BF)]
    sums = [((width, 4 * width), F32)] + ([((share * parts, width), BF)] if last else [])
    grid = pltpu.PrefetchScalarGridSpec(
        num_scalar_prefetch=1,
        grid=(count,),
        in_specs=[per_image(v.shape, first) for v in per] + [resident(w.shape) for w in shared],
        out_specs=[per_image(s) for s, _ in outs] + [resident(s) for s, _ in sums],
        scratch_shapes=[
            pltpu.VMEM((all_tokens, width), BF),
            pltpu.VMEM((all_tokens, width), BF),
        ],
    )
    return pl.pallas_call(
        functools.partial(attention_back_kernel, parts=parts, begin=begin, last=last),
        grid_spec=grid,
        out_shape=[out_of(s, d) for s, d in outs + sums],
        compiler_params=PARAMS,
        cost_estimate=cost(count, 8e9, 10e6),
        name="attention_back",
    )(rank, *per, *shared)


def conv_attn_back_call(rank, strips, first, skip, images, xp, mod, gmid, gqkv, weights, perm_back, moves):
    qkv_w, conv_a = weights
    all_tokens, width = xp.shape[1:]
    tokens = moves.shape[1]
    padded = tokens + 32
    shared = (qkv_w, conv_a, perm_back, moves)
    outs = [((images, all_tokens // strips, width), BF)] * strips + [((images, 8, width), F32)]
    sums = [(16, width)]
    grid = pltpu.PrefetchScalarGridSpec(
        num_scalar_prefetch=1,
        grid=(images,),
        in_specs=[per_image(v.shape, first) for v in (xp, mod, gmid)]
        + [per_image(gqkv.shape, skip)]
        + [resident(w.shape) for w in shared],
        out_specs=[per_image(s) for s, _ in outs] + [resident(s) for s in sums],
        scratch_shapes=[
            pltpu.VMEM((all_tokens, width), F32),
            pltpu.VMEM((4, padded, width), F32),
            pltpu.VMEM((4, padded, width), F32),
            pltpu.VMEM((all_tokens, width), BF),
            pltpu.VMEM((all_tokens, width), F32),
            pltpu.VMEM((9, 8, width), F32),
        ],
    )
    return pl.pallas_call(
        functools.partial(conv_attn_back_kernel, strips),
        grid_spec=grid,
        out_shape=[out_of(s, d) for s, d in outs] + [out_of(s, F32) for s in sums],
        compiler_params=PARAMS,
        cost_estimate=cost(images, 4e9, 8e6),
        name="conv_attn_back",
    )(rank, xp, mod, gmid, gqkv, *shared)


def finish_latents_kernel(strips, rank_ref, *refs):
    out_ref = refs[-1]
    for at in range(strips):
        out_ref[at ^ rank_ref[1], 0] = refs[at][0].astype(F32)


def finish_latents_call(rank, images, first, pieces, held):
    strips = len(pieces)
    count, tokens, width = pieces[0].shape
    shape = (strips, images, tokens, width)
    held = () if held is None else (held,)
    grid = pltpu.PrefetchScalarGridSpec(
        num_scalar_prefetch=1,
        grid=(count,),
        in_specs=[per_image(piece.shape) for piece in pieces]
        + [pl.BlockSpec(memory_space=pl.ANY)] * len(held),
        out_specs=pl.BlockSpec((strips, 1, tokens, width), lambda b, *_: (0, b + first, 0, 0)),
    )
    return pl.pallas_call(
        functools.partial(finish_latents_kernel, strips),
        grid_spec=grid,
        out_shape=out_of(shape, F32),
        input_output_aliases={strips + 1: 0} if held else {},
        compiler_params=PARAMS,
        cost_estimate=cost(count, 0, 3e6),
        name="finish_latents",
    )(rank, *pieces, *held)


def finish_big_call(rows, devices, order, hidden, width):
    count = devices // FINISH_STEPS
    share = rows.shape[0] // devices
    deep = count * share
    def owner(part):
        return sum(((part >> at) & 1) << bit for at, bit in enumerate(reversed(order)))

    return pl.pallas_call(
        finish_big_kernel,
        grid=(FINISH_STEPS,),
        in_specs=[
            pl.BlockSpec((share, width), lambda i, at=at: (owner(i * count + at), 0)) for at in range(count)
        ],
        out_specs=[
            pl.BlockSpec((width, deep), lambda i: (0, jnp.maximum(i - 6, 0))),
            pl.BlockSpec((deep, width), lambda i: (jnp.minimum(i, 1), 0)),
            pl.BlockSpec((deep, width), lambda i: (jnp.clip(i - 2, 0, 3) % 2, jnp.clip(i - 2, 0, 3) // 2)),
        ],
        out_shape=[out_of((width, hidden), F32), out_of((hidden, width), F32), out_of((hidden, 2 * width), F32)],
        compiler_params=PARAMS,
        cost_estimate=cost(1, 0, 15e6),
        name="finish_big",
    )(*[rows] * count)


def finish_rest_call(rank, own, other, share, width, images, features):
    shapes = [
        (width, 3 * width),
        (width, width),
        (3, 3, 4 * width),
        (4 * width,),
        (width,),
        (2 * width,),
        (3, 3, width),
        (features, 6 * width),
        (6 * width,),
    ]
    grid = pltpu.PrefetchScalarGridSpec(
        num_scalar_prefetch=1,
        grid=(1,),
        in_specs=[resident(own.shape), resident(other.shape)],
        out_specs=[resident(shape) for shape in shapes],
    )
    return pl.pallas_call(
        functools.partial(finish_rest_kernel, share=share, images=images, features=features),
        grid_spec=grid,
        out_shape=[out_of(shape, F32) for shape in shapes],
        compiler_params=PARAMS,
        cost_estimate=cost(1, 0, 8e6),
        name="finish_rest",
    )(rank, own, other)


def bit_order(devices, narrow):
    bits, near = devices.bit_length() - 1, narrow.bit_length() - 1
    return [0, *range(near, bits), *range(1, near)]


def stages(order):
    found = [[1 << order[0]]]
    for at in range(1, len(order), 2):
        found.append([1 << bit for bit in order[at : at + 2]])
    return found


def group_masks(group):
    if len(group) == 1:
        return [0, group[0]]
    return [0, group[1], group[0], group[0] | group[1]]


def exchange(values, mask, devices):
    return lax.ppermute(values, AXES, [(i, i ^ mask) for i in range(devices)])


def swap_strips(values, mask):
    count = lax.axis_size("narrow")
    return lax.ppermute(values, "narrow", [(i, i ^ mask) for i in range(count)])


def sent_strips(pieces):
    return [piece if at == 0 else swap_strips(piece, at) for at, piece in enumerate(pieces)]


def scatter_stage(values, group, devices):
    masks = group_masks(group)
    size = values.shape[0] // len(masks)
    total = values[:size].astype(F32)
    for at, mask in enumerate(masks[1:], 1):
        total = total + exchange(values[at * size : (at + 1) * size], mask, devices).astype(F32)
    return total.astype(BF)


def gather_stage(values, group, devices):
    masks = group_masks(group)
    return jnp.concatenate(
        [values] + [exchange(values, mask, devices) for mask in masks[1:]], axis=0
    )


def flat_rank(order):
    index = lax.axis_index("wide") * lax.axis_size("narrow") + lax.axis_index("narrow")
    rank = jnp.zeros((), jnp.int32)
    for bit in order:
        rank = 2 * rank + ((index >> bit) & 1)
    return jnp.stack([rank, lax.axis_index("narrow")])


def shards(
    latents,
    timesteps,
    out_grad,
    ada_weight,
    ada_bias,
    conv_attn,
    qkv_weight,
    proj_weight,
    fc1_weight,
    fc1_bias,
    conv_ffn,
    fc2_weight,
    fc2_bias,
    down_weight,
    down_bias,
):
    images, cols, width = out_grad.shape[0], latents.shape[2], latents.shape[3]
    height = latents.shape[1] * lax.axis_size("narrow")
    hidden = fc1_weight.shape[1]
    devices = lax.axis_size("wide") * lax.axis_size("narrow")
    order = bit_order(devices, lax.axis_size("narrow"))
    rank = flat_rank(order)
    steps = stages(order)
    strips = lax.axis_size("narrow")
    strip_tokens = latents.shape[1] * cols
    place = lax.axis_index("narrow")
    sources = latents.reshape(strips, images, strip_tokens, width)
    own_steps = lax.dynamic_slice_in_dim(timesteps, lax.axis_index("narrow") * images, images)
    half_count = ada_weight.shape[0] // 2
    freq = jnp.exp(-math.log(10000.0) * jnp.arange(half_count, dtype=F32) / half_count)
    angles = own_steps.astype(F32)[:, None] * freq[None, :]
    features = jnp.concatenate([jnp.cos(angles), jnp.sin(angles)], axis=1)
    cond = jax.nn.silu(features).astype(BF)
    mod = jnp.dot(cond, ada_weight, preferred_element_type=F32) + ada_bias.astype(F32)
    mod = jnp.pad(mod.reshape(images, 6, width), ((0, 0), (0, 2), (0, 0)))
    perm, perm_back, moves = token_tables(cols, strip_tokens)
    conv_a = jnp.pad(conv_attn.reshape(9, width).astype(F32), ((0, 7), (0, 0)))
    conv_f = jnp.pad(conv_ffn.reshape(9, hidden), ((0, 7), (0, 0)))
    low = out_grad.reshape(images, height * cols // 4, out_grad.shape[3])
    held = None
    behind = None
    for image in range(images):
        pieces = [
            lax.dynamic_slice(sources, (place ^ at, image, 0, 0), (1, 1, strip_tokens, width)).reshape(
                strip_tokens, width
            )
            for at in range(strips)
        ]
        if behind is not None:
            behind, *pieces = lax.optimization_barrier((behind, *pieces))
            held = attention_forward_call(
                rank, image - 1, images, behind, mod, qkv_weight, conv_a, perm, moves, held
            )
        behind = tuple(
            piece if at == 0 else swap_strips(piece, at) for at, piece in enumerate(pieces)
        )
    xp, co, qkv, mix, stat = attention_forward_call(
        rank, images - 1, images, behind, mod, qkv_weight, conv_a, perm, moves, held
    )
    res, gmid, gmod_two, big, small = feed_forward_call(
        rank,
        devices,
        xp,
        mix,
        mod,
        low,
        (
            proj_weight,
            fc1_weight,
            fc1_bias.astype(F32)[None],
            fc2_weight,
            fc2_bias.astype(F32)[None],
            down_weight,
            down_bias.astype(F32)[None],
            conv_f,
        ),
        moves,
    )
    split = max(images // 2, 1)
    groups = [(0, split)] + ([(split, images - split)] if images > split else [])
    later = [(image, 1) for image in range(split, images)]
    gqkvs = []
    before = None

    def attention_back(group):
        nonlocal before
        gqkv, before, *final = attention_back_call(
            rank, devices, group, mod, gmid, co, qkv, mix, stat, proj_weight, small, before
        )
        gqkvs.append(gqkv)
        return final

    def conv_attn_back(group, skip):
        *made, gmod_one, d_ca = conv_attn_back_call(
            rank, strips, group[0], skip, group[1], xp, mod, gmid, gqkvs[-1], (qkv_weight, conv_a), perm_back, moves
        )
        mods.append(gmod_one)
        convs.append(d_ca)
        return made

    mods, convs = [], []
    big = scatter_stage(big, steps[0], devices)
    mod, big = lax.optimization_barrier((mod, big))
    final = attention_back(groups[0])
    for group in steps[1:-1]:
        big = scatter_stage(big, group, devices)
    mod, big, gqkvs = lax.optimization_barrier((mod, big, gqkvs))
    made = conv_attn_back(groups[0], 0)
    big = scatter_stage(big, steps[-1], devices)
    mod, big, made = lax.optimization_barrier((mod, big, made))
    gathered = lax.all_gather(big, AXES, axis=0, tiled=True)
    outs = [sent_strips(made)]
    for group in groups[1:]:
        final = attention_back(group)
    rest, outs = lax.optimization_barrier((final[0], outs))
    stage = 0
    for at, group in enumerate(later):
        made = conv_attn_back(group, at)
        if stage < len(steps) - 1:
            rest = scatter_stage(rest, steps[stage], devices)
            stage += 1
        mod, rest, made, outs = lax.optimization_barrier((mod, rest, made, outs))
        outs.append(sent_strips(made))
    for group in steps[stage:]:
        rest = scatter_stage(rest, group, devices)
    halves = [groups[0], *later]
    grad_mod = jnp.concatenate([jnp.concatenate(mods, axis=0)[:, :2], gmod_two[:, :4]], axis=1)
    grad_mod = grad_mod.transpose(1, 0, 2).reshape(6 * images, width)
    per_tile = 8 // images
    late = jnp.concatenate(
        [
            sum(convs),
            jnp.pad(grad_mod, ((0, -grad_mod.shape[0] % 8), (0, 0))),
            jnp.pad(
                jnp.concatenate([cond.astype(F32)] * per_tile, axis=0), ((0, 0), (0, width - cond.shape[1]))
            ),
        ],
        axis=0,
    ).astype(BF)
    share = rest.shape[0]
    rest = jnp.concatenate([rest, late], axis=0)
    grad_latents = None
    for at, group in enumerate(steps[:0:-1]):
        rest = gather_stage(rest, group, devices)
        if at == 0:
            rest, outs, gathered = lax.optimization_barrier((rest, outs, gathered))
        if at == len(steps) - 2:
            finished = finish_big_call(gathered, devices, order, hidden, width)
            for (first, count), pieces in zip(halves[:2], outs):
                grad_latents = finish_latents_call(rank, images, first, pieces, grad_latents)
            rest, grad_latents, finished = lax.optimization_barrier((rest, grad_latents, finished))
    grad_fc1, grad_fc2, grad_down = finished
    for (first, count), pieces in zip(halves[2:], outs[2:]):
        grad_latents = finish_latents_call(rank, images, first, pieces, grad_latents)
    rest = rest.reshape(devices // 2, -1, width)
    other = exchange(rest, steps[0][0], devices)
    other, grad_latents = lax.optimization_barrier((other, grad_latents))
    (
        grad_qkv,
        grad_proj,
        grad_conv_ffn,
        grad_fc1b,
        grad_fc2b,
        grad_downb,
        grad_conv_attn,
        grad_ada,
        grad_ada_bias,
    ) = finish_rest_call(rank, rest, other, share, width, images, cond.shape[1])
    return (
        res.reshape(out_grad.shape),
        grad_latents.reshape(latents.shape),
        grad_ada,
        grad_ada_bias,
        grad_conv_attn,
        grad_qkv,
        grad_proj,
        grad_fc1,
        grad_fc1b,
        grad_conv_ffn,
        grad_fc2,
        grad_fc2b,
        grad_down,
        grad_downb,
    )


def solution(mesh):
    strip = P("wide", "narrow", None, None)
    image = P(AXES, None, None, None)
    in_specs = (strip, P("wide"), image) + (P(),) * 12
    out_specs = (image, strip) + (P(),) * 12
    return jax.shard_map(shards, mesh=mesh, in_specs=in_specs, out_specs=out_specs, check_vma=False)
```

```python
import functools
import math

import jax
import jax.numpy as jnp
from jax import lax
from jax.experimental import pallas as pl
from jax.experimental.pallas import tpu as pltpu
from jax.sharding import PartitionSpec as P

HEADS = 6
EPSILON = 1e-06
HIGH = lax.Precision.HIGHEST
BF = jnp.bfloat16
F32 = jnp.float32
NN = ((1,), (0,))
NT = ((1,), (1,))
TN = ((0,), (0,))
LANES = 128
CHUNK = 256
TILE = 64
GELU_A = math.sqrt(2.0 / math.pi)
GELU_B = 0.044715
AXES = ("wide", "narrow")


def mm(left, right, dims=NN):
    return lax.dot_general(left, right, (dims, ((), ())), preferred_element_type=F32)


def col_sum(values):
    return jnp.sum(values, axis=0, keepdims=True)


def rows_of(*rows):
    blank = jnp.zeros((8 - len(rows), rows[0].shape[1]), F32)
    return jnp.concatenate([*rows, blank], axis=0).astype(BF)


def row_mean(values):
    return jnp.mean(values, axis=1, keepdims=True)


def normed(values):
    center = values - row_mean(values)
    spread = row_mean(center * center)
    inverse = lax.rsqrt(spread + EPSILON)
    return center * inverse, inverse


def norm_back(grad_normed, normed_values, inverse):
    return inverse * (
        grad_normed - row_mean(grad_normed) - normed_values * row_mean(grad_normed * normed_values)
    )


def tap_source(phase, tap):
    distance = phase + tap - 1
    return distance % 2, distance // 2


def tap_ref(plain, moved, row_phase, col_phase, row_tap, col_tap, cols, start, size, lanes):
    source_row, row_move = tap_source(row_phase, row_tap)
    source_col, col_move = tap_source(col_phase, col_tap)
    held = plain if col_move == 0 else moved
    return held[2 * source_row + source_col, pl.ds(cols + cols * row_move + start, size), lanes]


def fill_planes(plain, moved, plane, col_phase_matrix, values_low, cols, lanes):
    tokens = values_low.shape[0]
    plain[plane, pl.ds(cols, tokens), lanes] = values_low.astype(F32)
    moved[plane, pl.ds(cols, tokens), lanes] = mm(col_phase_matrix, values_low)


def conv_tile(plain, moved, weight, row_phase, col_phase, cols, start, size, lanes, lanes_weight):
    total = None
    for row_tap in range(3):
        for col_tap in range(3):
            window = tap_ref(
                plain, moved, row_phase, col_phase, row_tap, col_tap, cols, start, size, lanes
            )
            part = window * weight[pl.ds(row_tap * 3 + col_tap, 1), lanes_weight]
            total = part if total is None else total + part
    return total


def conv_back_tile(
    plain, moved, weight, inputs, kernel_grad, row_phase, col_phase, cols, start, size, lanes, lanes_weight
):
    total = None
    for row_tap in range(3):
        for col_tap in range(3):
            window = tap_ref(
                plain, moved, row_phase, col_phase, row_tap, col_tap, cols, start, size, lanes
            )
            mirror = (2 - row_tap) * 3 + (2 - col_tap)
            part = window * weight[pl.ds(mirror, 1), lanes_weight]
            total = part if total is None else total + part
            product = jnp.sum((window * inputs).reshape(size // 8, 8, LANES), axis=0)
            kernel_grad[mirror, :, lanes_weight] += product
    return total


def packed(values):
    return values.reshape(values.shape[0] // 8, 8, values.shape[1])


def kernel_rows(weight, lanes):
    return [jnp.broadcast_to(weight[pl.ds(tap, 1), lanes], (8, lanes.size)) for tap in range(9)]


def conv_packed(plain, moved, taps, row_phase, col_phase, cols, start, lanes):
    total = None
    for row_tap in range(3):
        for col_tap in range(3):
            window = packed(
                tap_ref(plain, moved, row_phase, col_phase, row_tap, col_tap, cols, start, TILE, lanes)
            )
            part = window * taps[row_tap * 3 + col_tap]
            total = part if total is None else total + part
    return total


def conv_back_packed(plain, moved, taps, inputs, row_phase, col_phase, cols, start, lanes):
    total = None
    sums = [None] * 9
    for row_tap in range(3):
        for col_tap in range(3):
            window = packed(
                tap_ref(plain, moved, row_phase, col_phase, row_tap, col_tap, cols, start, TILE, lanes)
            )
            mirror = (2 - row_tap) * 3 + (2 - col_tap)
            part = window * taps[mirror]
            total = part if total is None else total + part
            product = window * inputs
            count = product.shape[0]
            while count > 1:
                count //= 2
                product = product[:count] + product[count:]
            sums[mirror] = product[0].astype(F32)
    return total, sums


def column_moved(values, col_phase, cols):
    tokens, lanes = values.shape
    turned = pltpu.roll(values, 1 if col_phase else tokens - 1, 0).reshape(tokens // cols, cols, lanes)
    spot = lax.broadcasted_iota(jnp.int32, (1, cols, lanes), 1)
    edge = 0 if col_phase else cols - 1
    return jnp.where(spot == edge, 0.0, turned).reshape(tokens, lanes)


def fill_packed(plain, moved, plane, values, cols):
    rows = pl.ds(cols, values.shape[0])
    plain[plane, rows, :] = values.astype(BF)
    moved[plane, rows, :] = column_moved(values, plane % 2, cols).astype(BF)


def place_rows(ref, values, first_row, rank, parts):
    share = ref.shape[0] // parts
    step = math.gcd(math.gcd(share, values.shape[0]), first_row)
    for at in range(0, values.shape[0], step):
        part, rest = divmod(first_row + at, share)
        row = pl.multiple_of((part ^ rank) * share + rest, step)
        ref[pl.ds(row, step), :] = values[at : at + step]


def zero_pads(buffer, cols):
    planes, padded, width = buffer.shape
    edge = jnp.zeros((planes, cols, width), buffer.dtype)
    buffer[:, pl.ds(0, cols), :] = edge
    buffer[:, pl.ds(padded - cols, cols), :] = edge


def attention_forward_kernel(strips, begin, rank_ref, *refs):
    pieces, refs = refs[:strips], refs[strips:]
    mod_ref, qkv_w, conv_a, perm, moves = refs[:5]
    refs = refs[5:] if begin else refs[10:]
    xp_ref, co_ref, qkv_ref, mix_ref, stat_ref, plain_h, moved_h = refs
    tokens = moves.shape[1]
    cols = tokens // 16
    width = xp_ref.shape[2]
    quarter = perm.shape[0] // 4
    for ref in (plain_h, moved_h):
        zero_pads(ref, cols)
    shift_one, scale_one = (mod_ref[0, pl.ds(part, 1), :] for part in range(2))

    for at, piece in enumerate(pieces):
        strip = at ^ rank_ref[1]
        moved_piece = mm(perm[...], piece[...]).astype(BF)
        for plane in range(4):
            row = pl.multiple_of(plane * tokens + strip * quarter, quarter)
            xp_ref[0, pl.ds(row, quarter), :] = moved_piece[plane * quarter : (plane + 1) * quarter]

    for plane in range(4):
        unit, _ = normed(xp_ref[0, pl.ds(plane * tokens, tokens), :].astype(F32))
        low = (unit * (1.0 + scale_one) + shift_one).astype(BF)
        fill_planes(plain_h, moved_h, plane, moves[plane % 2], low, cols, pl.ds(0, width))
    for plane in range(4):
        for lane in range(0, width, LANES):
            for start in range(0, tokens, 128):
                lanes = pl.ds(lane, LANES)
                total = conv_tile(
                    plain_h, moved_h, conv_a, plane // 2, plane % 2, cols, start, 128, lanes, lanes
                )
                co_ref[0, pl.ds(plane * tokens + start, 128), lanes] = total.astype(BF)

    head_size = width // HEADS
    factor = head_size ** (-0.5)

    def attend(plane, carry):
        rows = pl.ds(pl.multiple_of(plane * tokens, tokens), tokens)
        qkv_ref[0, rows, :] = mm(co_ref[0, rows, :], qkv_w[...]).astype(BF)
        even = lax.broadcasted_iota(jnp.int32, (tokens, LANES), 1) < head_size
        scores = []
        zero = jnp.zeros((tokens, LANES), BF)
        for pair in range(width // LANES):
            query = qkv_ref[0, rows, pl.ds(pair * LANES, LANES)]
            key = qkv_ref[0, rows, pl.ds(width + pair * LANES, LANES)] * jnp.asarray(factor, BF)
            both = mm(jnp.concatenate([jnp.where(even, key, zero), jnp.where(even, zero, key)], axis=0), query, NT)
            scores += [both[:tokens], both[tokens:]]
        tops = [jnp.max(score, axis=0, keepdims=True) for score in scores]
        grown = [jnp.exp(score - top) for score, top in zip(scores, tops)]
        totals = [col_sum(values) for values in grown]
        probs = [(values * (1.0 / total)).astype(BF) for values, total in zip(grown, totals)]
        for pair in range(width // LANES):
            value_t = qkv_ref[0, rows, pl.ds(2 * width + pair * LANES, LANES)].T
            mixed_t = jnp.concatenate(
                [
                    mm(value_t[half * head_size : (half + 1) * head_size], probs[2 * pair + half])
                    for half in range(2)
                ],
                axis=0,
            )
            mix_ref[0, rows, pl.ds(pair * LANES, LANES)] = mixed_t.astype(BF).T
        for head in range(HEADS):
            stat_ref[0, plane, pl.ds(head, 1), :] = tops[head] + jnp.log(totals[head])
        return carry

    lax.fori_loop(0, 4, attend, 0)


def feed_forward_kernel(
    rank_ref,
    xp_ref,
    mix_ref,
    mod_ref,
    og_ref,
    proj_w,
    fc1_w,
    fc1_b,
    fc2_w,
    fc2_b,
    down_w,
    down_b,
    conv_f,
    moves,
    res_ref,
    gmid_ref,
    gmod_ref,
    big_ref,
    small_ref,
    fout_s,
    ghid_s,
    plain_p,
    moved_p,
    plain_g,
    moved_g,
    attn_s,
    gffn_s,
    hid_s,
    act_s,
    gpre_s,
    gact_s,
    hid_t,
    gffn_t,
    low_s,
    dconv_s,
    fc1_sum,
    fc2_sum,
    down_sum,
    *,
    parts,
):
    image = pl.program_id(0)
    tokens = moves.shape[1]
    cols = tokens // 16
    width = xp_ref.shape[2]
    hidden = fc1_w.shape[1]

    @pl.when(image == 0)
    def _():
        for ref in (fc1_sum, fc2_sum, down_sum, small_ref, dconv_s):
            ref[...] = jnp.zeros(ref.shape, F32)
        hid_t[pl.ds(width, 16), :] = jnp.ones((16, hid_t.shape[1]), BF)
        for ref in (plain_g, moved_g):
            zero_pads(ref, cols)
        for ref in (plain_p, moved_p):
            for slot in range(2):
                zero_pads(ref.at[slot], cols)

    gate_one, shift_two, scale_two, gate_two = (mod_ref[0, pl.ds(part, 1), :] for part in range(2, 6))
    attn_s[...] = mm(mix_ref[0], proj_w[...])

    grad_low = og_ref[0]
    small_ref[pl.ds(10, 1), pl.ds(width, 2 * width)] += col_sum(grad_low.astype(F32))
    grad_all = mm(grad_low, down_w[...], NT)
    for plane in range(4):
        rows = pl.ds(plane * tokens, tokens)
        grad_after = grad_all[:, plane * width : (plane + 1) * width]
        gmid_ref[0, rows, :] = grad_after
        grad_out = (gate_two * grad_after).astype(BF)
        gffn_s[rows, :] = grad_out
        small_ref[pl.ds(10, 1), pl.ds(0, width)] += col_sum(grad_out.astype(F32))
        after = xp_ref[0, rows, :].astype(F32) + gate_one * attn_s[rows, :]
        unit, _ = normed(after)
        hid_s[rows, :] = (unit * (1.0 + scale_two) + shift_two).astype(BF)

    hid_t[pl.ds(0, width), :] = hid_s[...].T
    gffn_t[...] = gffn_s[...].T
    chunks = hidden // CHUNK

    def units_of(chunk):
        return pl.ds(pl.multiple_of(chunk * CHUNK, CHUNK), CHUNK)

    def prepare(chunk, slot):
        units = units_of(chunk)
        pre = mm(hid_s[...], fc1_w[:, units]) + fc1_b[:, units]
        for plane in range(4):
            fill_packed(
                plain_p.at[slot],
                moved_p.at[slot],
                plane,
                pre[plane * tokens : (plane + 1) * tokens],
                cols,
            )
        gact_s[slot] = mm(gffn_s[...], fc2_w[units, :], NT).astype(gact_s.dtype)

    def collect(chunk, slot):
        units = units_of(chunk)
        grad_pre = gpre_s[slot]
        active = act_s[slot]
        sums = mm(hid_t[...], grad_pre)
        fc1_sum[:, units] += sums[:width]
        small_ref[pl.ds(9, 1), units] += sums[width : width + 1]
        fc2_sum[:, units] += mm(gffn_t[...], active)
        out = mm(active, fc2_w[units, :])
        grad_hid = mm(grad_pre, fc1_w[:, units], NT)
        for plane in range(4):
            part = slice(plane * tokens, (plane + 1) * tokens)
            fout_s[plane] += out[part]
            ghid_s[plane] += grad_hid[part]

    def convolve(chunk, slot):
        units = units_of(chunk)
        taps = kernel_rows(conv_f, units)
        chunk_lanes = pl.ds(0, CHUNK)
        plain, moved = plain_p.at[slot], moved_p.at[slot]
        for plane in range(4):
            for start in range(0, tokens, TILE):
                rows = pl.ds(plane * tokens + start, TILE)
                value = conv_packed(plain, moved, taps, plane // 2, plane % 2, cols, start, chunk_lanes)
                value_low = value.reshape(TILE, CHUNK)
                value = value_low.astype(F32)
                square = value * value
                half = 0.5 * jnp.tanh(value * (GELU_A + (GELU_A * GELU_B) * square))
                gate = 0.5 + half
                act_s[slot, rows, :] = (value * gate).astype(BF)
                gate_low = gate.astype(BF)
                bend = (value_low * (0.5 - half).astype(BF)) * (
                    jnp.asarray(2.0 * GELU_A, BF)
                    + (value_low * value_low) * jnp.asarray(6.0 * GELU_A * GELU_B, BF)
                )
                slope = gate_low + gate_low * bend
                plain_g[plane, pl.ds(cols + start, TILE), :] = slope * gact_s[slot, rows, :]
            rows = pl.ds(cols, tokens)
            moved_g[plane, rows, :] = mm(moves[plane % 2], plain_g[plane, rows, :]).astype(BF)
        kernel_grads = None
        for plane in range(4):
            for start in range(0, tokens, TILE):
                inputs = packed(plain[plane, pl.ds(cols + start, TILE), :])
                total, sums = conv_back_packed(
                    plain_g, moved_g, taps, inputs, plane // 2, plane % 2, cols, start, chunk_lanes
                )
                gpre_s[slot, pl.ds(plane * tokens + start, TILE), :] = total.reshape(TILE, CHUNK)
                kernel_grads = (
                    sums if kernel_grads is None else [a + b for a, b in zip(kernel_grads, sums)]
                )
        for tap in range(9):
            dconv_s[tap, :, units] += kernel_grads[tap]

    for ref in (fout_s, ghid_s):
        ref[...] = jnp.zeros(ref.shape, F32)
    for ref in (act_s, gpre_s):
        ref[1] = jnp.zeros(ref.shape[1:], BF)
    prepare(0, 0)

    def feed(step, carry):
        chunk = 2 * step
        prepare(chunk + 1, 1)
        collect(jnp.maximum(chunk - 1, 0), 1)
        convolve(chunk, 0)
        prepare(jnp.minimum(chunk + 2, chunks - 1), 0)
        collect(chunk, 0)
        convolve(chunk + 1, 1)
        return carry

    lax.fori_loop(0, chunks // 2, feed, 0)
    collect(chunks - 1, 1)

    grad_gate_one = grad_shift_two = grad_scale_two = grad_gate_two = jnp.zeros((1, width), F32)
    for plane in range(4):
        rows = pl.ds(plane * tokens, tokens)
        attn = attn_s[rows, :]
        after = xp_ref[0, rows, :].astype(F32) + gate_one * attn
        grad_after = gmid_ref[0, rows, :]
        out = fout_s[plane] + fc2_b[...]
        grad_gate_two += col_sum(out * grad_after)
        low_s[:, pl.ds(plane * width, width)] = (after + gate_two * out).astype(BF)
        grad_hid = ghid_s[plane]
        unit, inverse = normed(after)
        grad_shift_two += col_sum(grad_hid)
        grad_scale_two += col_sum(grad_hid * unit)
        grad_mid = grad_after + norm_back(grad_hid * (1.0 + scale_two), unit, inverse)
        gmid_ref[0, rows, :] = grad_mid
        grad_gate_one += col_sum(attn * grad_mid)
    gmod_ref[0] = rows_of(grad_gate_one, grad_shift_two, grad_scale_two, grad_gate_two)

    res_ref[0] = (mm(low_s[...], down_w[...]) + down_b[...]).astype(BF)
    grad_low_t = grad_low.T

    def down_weights(chunk, carry):
        units = pl.ds(pl.multiple_of(chunk * CHUNK, CHUNK), CHUNK)
        down_sum[:, units] += mm(grad_low_t, low_s[:, units])
        return carry

    lax.fori_loop(0, low_s.shape[1] // CHUNK, down_weights, 0, unroll=True)

    @pl.when(image == pl.num_programs(0) - 1)
    def _():
        for tap in range(9):
            small_ref[pl.ds(tap, 1), :] = col_sum(dconv_s[tap])

        rank = rank_ref[0]
        for chunk in range(hidden // CHUNK):
            units = pl.ds(chunk * CHUNK, CHUNK)
            place_rows(big_ref, fc2_sum[:, units].T.astype(BF), chunk * CHUNK, rank, parts)
            down = down_sum[:, units].T.astype(BF)
            for half in range(2):
                place_rows(
                    big_ref,
                    down[:, half * width : (half + 1) * width],
                    (1 + half) * hidden + chunk * CHUNK,
                    rank,
                    parts,
                )
        for part in range(hidden // width):
            block = fc1_sum[:, pl.ds(part * width, width)].astype(BF)
            place_rows(big_ref, block, 3 * hidden + part * width, rank, parts)


def attention_back_kernel(
    rank_ref,
    mod_ref,
    gmid_ref,
    co_ref,
    qkv_ref,
    mix_ref,
    stat_ref,
    proj_w,
    small_ref,
    *rest,
    parts,
    begin,
    last,
):
    image = pl.program_id(0)
    width = mix_ref.shape[2]
    tokens = mix_ref.shape[1] // 4
    before_ref = None if begin else rest[0]
    gqkv_ref, sum_ref = rest[0 if begin else 1 :][:2]
    rows_ref = rest[-3] if last else None
    gout_s, gmix_s = rest[-2:]

    @pl.when(image == 0)
    def _():
        sum_ref[...] = jnp.zeros(sum_ref.shape, F32) if begin else before_ref[...]

    gate_one = mod_ref[0, pl.ds(2, 1), :]
    head_size = width // HEADS
    factor = jnp.asarray(head_size ** (-0.5), BF)

    gout_s[...] = (gate_one * gmid_ref[0]).astype(BF)
    gmix_s[...] = mm(gout_s[...], proj_w[...], NT).astype(BF)

    def attend(plane, carry):
        rows = pl.ds(pl.multiple_of(plane * tokens, tokens), tokens)
        even = lax.broadcasted_iota(jnp.int32, (tokens, LANES), 1) < head_size
        zero = jnp.zeros((tokens, LANES), BF)
        for pair in range(width // LANES):
            lane = pair * LANES
            query = qkv_ref[0, rows, pl.ds(lane, LANES)]
            key = qkv_ref[0, rows, pl.ds(width + lane, LANES)] * factor
            value = qkv_ref[0, rows, pl.ds(2 * width + lane, LANES)]
            query_low = query * factor
            key_t = key.T
            grad_mixed = gmix_s[rows, pl.ds(lane, LANES)]

            def heads(values):
                return jnp.concatenate([jnp.where(even, values, zero), jnp.where(even, zero, values)], axis=0)

            def joined(values):
                return jnp.where(even, values[:tokens], values[tokens:])

            scores = mm(heads(key), query, NT)
            grad_probs = mm(heads(value), grad_mixed, NT)
            probs, grad_scores = [], []
            for half in range(2):
                part = slice(half * tokens, (half + 1) * tokens)
                prob = jnp.exp(scores[part] - stat_ref[0, plane, pl.ds(2 * pair + half, 1), :])
                weighted = prob * grad_probs[part]
                probs.append(prob.astype(BF))
                grad_scores.append((weighted - prob * col_sum(weighted)).astype(BF))
            grad_value = joined(mm(jnp.concatenate(probs, axis=0), grad_mixed))
            grad_key = joined(mm(jnp.concatenate(grad_scores, axis=0), query_low))
            grad_query_t = jnp.concatenate(
                [
                    mm(key_t[half * head_size : (half + 1) * head_size], grad_scores[half])
                    for half in range(2)
                ],
                axis=0,
            )
            gqkv_ref[0, rows, pl.ds(lane, LANES)] = grad_query_t.astype(BF).T
            gqkv_ref[0, rows, pl.ds(width + lane, LANES)] = grad_key.astype(BF)
            gqkv_ref[0, rows, pl.ds(2 * width + lane, LANES)] = grad_value.astype(BF)
        return carry

    lax.fori_loop(0, 4, attend, 0, unroll=2)

    sum_ref[:, pl.ds(3 * width, width)] += mm(mix_ref[0].T, gout_s[...])
    conv_t = co_ref[0].T
    for part in range(3):
        lanes = pl.ds(part * width, width)
        sum_ref[:, lanes] += mm(conv_t, gqkv_ref[0, :, lanes])

    if not last:
        return

    @pl.when(image == pl.num_programs(0) - 1)
    def _():
        rank = rank_ref[0]
        rows_ref[...] = jnp.zeros(rows_ref.shape, BF)
        for part in range(4):
            lanes = pl.ds(part * width, width)
            place_rows(rows_ref, sum_ref[:, lanes].astype(BF), part * width, rank, parts)
        for part in range(4):
            lanes = pl.ds(part * width, width)
            place_rows(rows_ref, small_ref[:, lanes].astype(BF), 4 * width + part * 16, rank, parts)


def conv_attn_back_kernel(
    strips,
    rank_ref,
    xp_ref,
    mod_ref,
    gmid_ref,
    gqkv_ref,
    qkv_w,
    conv_a,
    perm_back,
    moves,
    *refs,
):
    pieces, refs = refs[:strips], refs[strips:]
    gmod_ref, d_conv, plain_h, plain_g, moved_g, gout_s, glat_s, dconv_s = refs
    image = pl.program_id(0)
    tokens = moves.shape[1]
    cols = tokens // 16
    width = xp_ref.shape[2]
    quarter = perm_back.shape[0] // 4

    @pl.when(image == 0)
    def _():
        d_conv[...] = jnp.zeros(d_conv.shape, F32)
        dconv_s[...] = jnp.zeros(dconv_s.shape, F32)
        for ref in (plain_g, moved_g):
            zero_pads(ref, cols)

    shift_one, scale_one = (mod_ref[0, pl.ds(part, 1), :] for part in range(2))
    for plane in range(4):
        rows = pl.ds(plane * tokens, tokens)
        grad_conv = mm(gqkv_ref[0, rows, :], qkv_w[...], NT).astype(BF)
        fill_planes(plain_g, moved_g, plane, moves[plane % 2], grad_conv, cols, pl.ds(0, width))
        unit, _ = normed(xp_ref[0, rows, :].astype(F32))
        low = (unit * (1.0 + scale_one) + shift_one).astype(BF)
        plain_h[rows, :] = low.astype(F32)
    for plane in range(4):
        for lane in range(0, width, LANES):
            for start in range(0, tokens, 128):
                lanes = pl.ds(lane, LANES)
                rows = pl.ds(plane * tokens + start, 128)
                total = conv_back_tile(
                    plain_g,
                    moved_g,
                    conv_a,
                    plain_h[rows, lanes],
                    dconv_s,
                    plane // 2,
                    plane % 2,
                    cols,
                    start,
                    128,
                    lanes,
                    lanes,
                )
                glat_s[rows, lanes] = total
    grad_shift = grad_scale = jnp.zeros((1, width), F32)
    for plane in range(4):
        rows = pl.ds(plane * tokens, tokens)
        grad_hid = glat_s[rows, :]
        unit, inverse = normed(xp_ref[0, rows, :].astype(F32))
        grad_shift += col_sum(grad_hid)
        grad_scale += col_sum(grad_hid * unit)
        gout_s[rows, :] = (
            gmid_ref[0, rows, :] + norm_back(grad_hid * (1.0 + scale_one), unit, inverse)
        ).astype(BF)
    gmod_ref[0] = rows_of(grad_shift, grad_scale)
    for at, piece in enumerate(pieces):
        strip = at ^ rank_ref[1]
        gathered = jnp.concatenate(
            [
                gout_s[pl.ds(pl.multiple_of(plane * tokens + strip * quarter, quarter), quarter), :]
                for plane in range(4)
            ],
            axis=0,
        )
        piece[0] = mm(perm_back[...], gathered).astype(BF)

    @pl.when(image == pl.num_programs(0) - 1)
    def _():
        for tap in range(9):
            d_conv[pl.ds(tap, 1), :] = col_sum(dconv_s[tap])


FINISH_STEPS = 8


def finish_big_kernel(*refs):
    rows, (fc1_ref, fc2_ref, down_ref) = refs[:-3], refs[-3:]
    step = pl.program_id(0)
    share, width = rows[0].shape

    def write(ref, flat):
        for at, rows_ref in enumerate(rows):
            block, row = (0, at * share) if flat else divmod(at * share, width)
            ref[pl.ds(row, share), pl.ds(block * width, width)] = rows_ref[...].astype(F32)

    @pl.when(step < 2)
    def _():
        write(fc2_ref, True)

    @pl.when((step >= 2) & (step < 6))
    def _():
        write(down_ref, True)

    @pl.when(step >= 6)
    def _():
        write(fc1_ref, False)


def finish_rest_kernel(
    rank_ref,
    own_ref,
    other_ref,
    qkv_ref,
    proj_ref,
    conv_ffn_ref,
    fc1b_ref,
    fc2b_ref,
    downb_ref,
    conv_ref,
    ada_ref,
    bias_ref,
    *,
    share,
    images,
    features,
):
    width = proj_ref.shape[0]
    rank = rank_ref[0]
    half = own_ref.shape[0]
    near = rank < half
    for part in range(2 * half):
        at = (part ^ rank) % half
        rows = pl.ds(0, share)
        own, other = own_ref[at, rows, :], other_ref[at, rows, :]
        is_own = near if part < half else ~near
        values = jnp.where(is_own, own.astype(F32), other.astype(F32))
        block, row = divmod(part * share, width)
        if block < 3:
            qkv_ref[pl.ds(row, share), pl.ds(block * width, width)] = values
        elif block == 3:
            proj_ref[pl.ds(row, share), :] = values
        elif block == 4 and row < 64:
            small = min(share, 16)
            for first in range(0, share, small):
                block = (row + first) // 16
                lanes = pl.ds(block * width, width)
                for tap in range(9):
                    conv_ffn_ref[tap // 3, pl.ds(tap % 3, 1), lanes] = values[first + tap : first + tap + 1]
                fc1b_ref[lanes] = values[first + 9]
                if block == 0:
                    fc2b_ref[...] = values[first + 10]
                elif block < 3:
                    downb_ref[pl.ds((block - 1) * width, width)] = values[first + 10]
    conv = jnp.zeros((16, width), F32)
    for ref in (own_ref, other_ref):
        for at in range(half):
            conv += ref[at, pl.ds(share, 16), :].astype(F32)
    for tap in range(9):
        conv_ref[tap // 3, pl.ds(tap % 3, 1), :] = conv[tap : tap + 1]
    per_tile = 8 // images
    tiles = -(-6 // per_tile)

    def tile(index, lanes):
        rows = pl.ds(share + 16 + 8 * index, 8)
        return jnp.concatenate(
            [ref[:, rows, lanes].reshape(8 * half, lanes.size) for ref in (own_ref, other_ref)], axis=0
        )

    cond = tile(tiles, pl.ds(0, features))
    slot = lax.broadcasted_iota(jnp.int32, cond.shape, 0) % 8 // images
    for part in range(6):
        chosen = jnp.where(slot == part % per_tile, cond, jnp.zeros_like(cond))
        ones = jnp.where(slot == part % per_tile, jnp.ones_like(cond), jnp.zeros_like(cond))[:, :LANES]
        grads = tile(part // per_tile, pl.ds(0, width))
        lanes = pl.ds(part * width, width)
        ada_ref[:, lanes] = mm(chosen, grads, TN)
        bias_ref[lanes] = mm(ones, grads, TN)[0]


def per_image(shape, first=0):
    rest = len(shape) - 1
    return pl.BlockSpec((1,) + tuple(shape[1:]), lambda b, *_: (b + first,) + (0,) * rest)


def resident(shape):
    rank = len(shape)
    return pl.BlockSpec(tuple(shape), lambda b, *_: (0,) * rank, pipeline_mode=pl.Buffered(1))


def out_of(shape, dtype):
    return jax.ShapeDtypeStruct(shape, dtype)


PARAMS = pltpu.CompilerParams(
    dimension_semantics=("arbitrary",), vmem_limit_bytes=63 * 1024 * 1024
)


def token_tables(cols, strip):
    half = cols // 2
    spot = jnp.arange(strip)
    from_row, from_col = spot // cols, spot % cols
    target = ((from_row % 2) * 2 + from_col % 2) * (strip // 4) + (from_row // 2) * half + from_col // 2
    perm_back = (target[:, None] == spot[None, :]).astype(BF)
    perm = (spot[:, None] == target[None, :]).astype(BF)
    spot = jnp.arange(half * half)
    ahead = ((spot[None, :] == spot[:, None] + 1) & (spot[:, None] % half != half - 1)).astype(BF)
    behind = ((spot[None, :] == spot[:, None] - 1) & (spot[:, None] % half != 0)).astype(BF)
    return perm, perm_back, jnp.stack([ahead, behind])


def attention_forward_call(rank, image, images, pieces, mod, qkv_w, conv_a, perm, moves, held):
    strips = len(pieces)
    width = pieces[0].shape[1]
    tokens = moves.shape[1]
    shared = (qkv_w, conv_a, perm, moves)
    rows = 4 * tokens
    outs = [
        ((images, rows, width), BF),
        ((images, rows, width), BF),
        ((images, rows, 3 * width), BF),
        ((images, rows, width), BF),
        ((images, 4, 8, tokens), F32),
    ]
    begin = held is None
    held = () if begin else tuple(held)
    grid = pltpu.PrefetchScalarGridSpec(
        num_scalar_prefetch=1,
        grid=(1,),
        in_specs=[resident(piece.shape) for piece in pieces]
        + [per_image(mod.shape, image)]
        + [resident(w.shape) for w in shared]
        + [pl.BlockSpec(memory_space=pl.ANY)] * len(held),
        out_specs=[per_image(shape, image) for shape, _ in outs],
        scratch_shapes=[pltpu.VMEM((4, tokens + 32, width), F32)] * 2,
    )
    return pl.pallas_call(
        functools.partial(attention_forward_kernel, strips, begin),
        grid_spec=grid,
        out_shape=[out_of(shape, dtype) for shape, dtype in outs],
        input_output_aliases={} if begin else {strips + 6 + at: at for at in range(5)},
        compiler_params=PARAMS,
        cost_estimate=cost(1, 5e9, 8e6),
        name="attention_forward",
    )(rank, *pieces, mod, *shared, *held)


def feed_forward_call(rank, parts, xp, mix, mod, og, weights, moves):
    proj_w, fc1_w, fc1_b, fc2_w, fc2_b, down_w, down_b, conv_f = weights
    images, all_tokens, width = xp.shape
    tokens = moves.shape[1]
    hidden = fc1_w.shape[1]
    padded = tokens + 32
    per = (xp, mix, mod, og)
    shared = (*weights, moves)
    outs = [
        (og.shape[:2] + (down_w.shape[1],), BF),
        (xp.shape, F32),
        ((images, 8, width), BF),
    ]
    sums = [((4 * hidden, width), BF), ((16, hidden), F32)]
    grid = pltpu.PrefetchScalarGridSpec(
        num_scalar_prefetch=1,
        grid=(images,),
        in_specs=[per_image(v.shape) for v in per] + [resident(w.shape) for w in shared],
        out_specs=[per_image(s) for s, _ in outs] + [resident(s) for s, _ in sums],
        scratch_shapes=[
            pltpu.VMEM((4, tokens, width), F32),
            pltpu.VMEM((4, tokens, width), F32),
            pltpu.VMEM((2, 4, padded, CHUNK), BF),
            pltpu.VMEM((2, 4, padded, CHUNK), BF),
            pltpu.VMEM((4, padded, CHUNK), BF),
            pltpu.VMEM((4, padded, CHUNK), BF),
            pltpu.VMEM((all_tokens, width), F32),
            pltpu.VMEM((all_tokens, width), BF),
            pltpu.VMEM((all_tokens, width), BF),
            pltpu.VMEM((2, all_tokens, CHUNK), BF),
            pltpu.VMEM((2, all_tokens, CHUNK), BF),
            pltpu.VMEM((2, all_tokens, CHUNK), BF),
            pltpu.VMEM((width + 16, all_tokens), BF),
            pltpu.VMEM((width, all_tokens), BF),
            pltpu.VMEM((tokens, 4 * width), BF),
            pltpu.VMEM((9, 8, hidden), F32),
            pltpu.VMEM((width, hidden), F32),
            pltpu.VMEM((width, hidden), F32),
            pltpu.VMEM((down_w.shape[1], hidden), F32),
        ],
    )
    return pl.pallas_call(
        functools.partial(feed_forward_kernel, parts=parts),
        grid_spec=grid,
        out_shape=[out_of(s, d) for s, d in outs + sums],
        compiler_params=PARAMS,
        cost_estimate=cost(images, 14e9, 20e6),
        name="feed_forward",
    )(rank, *per, *shared)


def cost(images, flops, moved):
    return pl.CostEstimate(
        flops=int(images * flops), bytes_accessed=int(images * moved), transcendentals=0
    )


def attention_back_call(rank, parts, group, mod, gmid, co, qkv, mix, stat, proj_w, small, before):
    images, all_tokens, width = mix.shape
    first, count = group
    begin, last = before is None, first + count == images
    per = (mod, gmid, co, qkv, mix, stat)
    shared = (proj_w, small) + (() if begin else (before,))
    share = 64 if parts <= 32 else 16
    outs = [((count,) + qkv.shape[1:], BF)]
    sums = [((width, 4 * width), F32)] + ([((share * parts, width), BF)] if last else [])
    grid = pltpu.PrefetchScalarGridSpec(
        num_scalar_prefetch=1,
        grid=(count,),
        in_specs=[per_image(v.shape, first) for v in per] + [resident(w.shape) for w in shared],
        out_specs=[per_image(s) for s, _ in outs] + [resident(s) for s, _ in sums],
        scratch_shapes=[
            pltpu.VMEM((all_tokens, width), BF),
            pltpu.VMEM((all_tokens, width), BF),
        ],
    )
    return pl.pallas_call(
        functools.partial(attention_back_kernel, parts=parts, begin=begin, last=last),
        grid_spec=grid,
        out_shape=[out_of(s, d) for s, d in outs + sums],
        compiler_params=PARAMS,
        cost_estimate=cost(count, 8e9, 10e6),
        name="attention_back",
    )(rank, *per, *shared)


def conv_attn_back_call(rank, strips, first, skip, images, xp, mod, gmid, gqkv, weights, perm_back, moves):
    qkv_w, conv_a = weights
    all_tokens, width = xp.shape[1:]
    tokens = moves.shape[1]
    padded = tokens + 32
    shared = (qkv_w, conv_a, perm_back, moves)
    outs = [((images, all_tokens // strips, width), BF)] * strips + [((images, 8, width), BF)]
    sums = [(16, width)]
    grid = pltpu.PrefetchScalarGridSpec(
        num_scalar_prefetch=1,
        grid=(images,),
        in_specs=[per_image(v.shape, first) for v in (xp, mod, gmid)]
        + [per_image(gqkv.shape, skip)]
        + [resident(w.shape) for w in shared],
        out_specs=[per_image(s) for s, _ in outs] + [resident(s) for s in sums],
        scratch_shapes=[
            pltpu.VMEM((all_tokens, width), F32),
            pltpu.VMEM((4, padded, width), F32),
            pltpu.VMEM((4, padded, width), F32),
            pltpu.VMEM((all_tokens, width), BF),
            pltpu.VMEM((all_tokens, width), F32),
            pltpu.VMEM((9, 8, width), F32),
        ],
    )
    return pl.pallas_call(
        functools.partial(conv_attn_back_kernel, strips),
        grid_spec=grid,
        out_shape=[out_of(s, d) for s, d in outs] + [out_of(s, F32) for s in sums],
        compiler_params=PARAMS,
        cost_estimate=cost(images, 4e9, 8e6),
        name="conv_attn_back",
    )(rank, xp, mod, gmid, gqkv, *shared)


def finish_latents_kernel(strips, rank_ref, *refs):
    out_ref = refs[-1]
    for at in range(strips):
        out_ref[at ^ rank_ref[1], 0] = refs[at][0].astype(F32)


def finish_latents_call(rank, images, first, pieces, held):
    strips = len(pieces)
    count, tokens, width = pieces[0].shape
    shape = (strips, images, tokens, width)
    held = () if held is None else (held,)
    grid = pltpu.PrefetchScalarGridSpec(
        num_scalar_prefetch=1,
        grid=(count,),
        in_specs=[per_image(piece.shape) for piece in pieces]
        + [pl.BlockSpec(memory_space=pl.ANY)] * len(held),
        out_specs=pl.BlockSpec((strips, 1, tokens, width), lambda b, *_: (0, b + first, 0, 0)),
    )
    return pl.pallas_call(
        functools.partial(finish_latents_kernel, strips),
        grid_spec=grid,
        out_shape=out_of(shape, F32),
        input_output_aliases={strips + 1: 0} if held else {},
        compiler_params=PARAMS,
        cost_estimate=cost(count, 0, 3e6),
        name="finish_latents",
    )(rank, *pieces, *held)


def finish_big_call(rows, devices, order, hidden, width):
    count = devices // FINISH_STEPS
    share = rows.shape[0] // devices
    deep = count * share
    def owner(part):
        return sum(((part >> at) & 1) << bit for at, bit in enumerate(reversed(order)))

    return pl.pallas_call(
        finish_big_kernel,
        grid=(FINISH_STEPS,),
        in_specs=[
            pl.BlockSpec((share, width), lambda i, at=at: (owner(i * count + at), 0)) for at in range(count)
        ],
        out_specs=[
            pl.BlockSpec((width, deep), lambda i: (0, jnp.maximum(i - 6, 0))),
            pl.BlockSpec((deep, width), lambda i: (jnp.minimum(i, 1), 0)),
            pl.BlockSpec((deep, width), lambda i: (jnp.clip(i - 2, 0, 3) % 2, jnp.clip(i - 2, 0, 3) // 2)),
        ],
        out_shape=[out_of((width, hidden), F32), out_of((hidden, width), F32), out_of((hidden, 2 * width), F32)],
        compiler_params=PARAMS,
        cost_estimate=cost(1, 0, 15e6),
        name="finish_big",
    )(*[rows] * count)


def finish_rest_call(rank, own, other, share, width, images, features):
    shapes = [
        (width, 3 * width),
        (width, width),
        (3, 3, 4 * width),
        (4 * width,),
        (width,),
        (2 * width,),
        (3, 3, width),
        (features, 6 * width),
        (6 * width,),
    ]
    grid = pltpu.PrefetchScalarGridSpec(
        num_scalar_prefetch=1,
        grid=(1,),
        in_specs=[resident(own.shape), resident(other.shape)],
        out_specs=[resident(shape) for shape in shapes],
    )
    return pl.pallas_call(
        functools.partial(finish_rest_kernel, share=share, images=images, features=features),
        grid_spec=grid,
        out_shape=[out_of(shape, F32) for shape in shapes],
        compiler_params=PARAMS,
        cost_estimate=cost(1, 0, 8e6),
        name="finish_rest",
    )(rank, own, other)


def bit_order(devices, narrow):
    bits, near = devices.bit_length() - 1, narrow.bit_length() - 1
    return [0, *range(near, bits), *range(1, near)]


def stages(order):
    found = [[1 << order[0]]]
    for at in range(1, len(order), 2):
        found.append([1 << bit for bit in order[at : at + 2]])
    return found


def group_masks(group):
    if len(group) == 1:
        return [0, group[0]]
    return [0, group[1], group[0], group[0] | group[1]]


def exchange(values, mask, devices):
    return lax.ppermute(values, AXES, [(i, i ^ mask) for i in range(devices)])


def swap_strips(values, mask):
    count = lax.axis_size("narrow")
    return lax.ppermute(values, "narrow", [(i, i ^ mask) for i in range(count)])


def sent_strips(pieces):
    return [piece if at == 0 else swap_strips(piece, at) for at, piece in enumerate(pieces)]


def scatter_stage(values, group, devices):
    masks = group_masks(group)
    size = values.shape[0] // len(masks)
    total = values[:size].astype(F32)
    for at, mask in enumerate(masks[1:], 1):
        total = total + exchange(values[at * size : (at + 1) * size], mask, devices).astype(F32)
    return total.astype(BF)


def gather_stage(values, group, devices):
    masks = group_masks(group)
    return jnp.concatenate(
        [values] + [exchange(values, mask, devices) for mask in masks[1:]], axis=0
    )


def flat_rank(order):
    index = lax.axis_index("wide") * lax.axis_size("narrow") + lax.axis_index("narrow")
    rank = jnp.zeros((), jnp.int32)
    for bit in order:
        rank = 2 * rank + ((index >> bit) & 1)
    return jnp.stack([rank, lax.axis_index("narrow")])


def shards(
    latents,
    timesteps,
    out_grad,
    ada_weight,
    ada_bias,
    conv_attn,
    qkv_weight,
    proj_weight,
    fc1_weight,
    fc1_bias,
    conv_ffn,
    fc2_weight,
    fc2_bias,
    down_weight,
    down_bias,
):
    images, cols, width = out_grad.shape[0], latents.shape[2], latents.shape[3]
    height = latents.shape[1] * lax.axis_size("narrow")
    hidden = fc1_weight.shape[1]
    devices = lax.axis_size("wide") * lax.axis_size("narrow")
    order = bit_order(devices, lax.axis_size("narrow"))
    rank = flat_rank(order)
    steps = stages(order)
    strips = lax.axis_size("narrow")
    strip_tokens = latents.shape[1] * cols
    place = lax.axis_index("narrow")
    sources = latents.reshape(strips, images, strip_tokens, width)
    own_steps = lax.dynamic_slice_in_dim(timesteps, lax.axis_index("narrow") * images, images)
    half_count = ada_weight.shape[0] // 2
    freq = jnp.exp(-math.log(10000.0) * jnp.arange(half_count, dtype=F32) / half_count)
    angles = own_steps.astype(F32)[:, None] * freq[None, :]
    features = jnp.concatenate([jnp.cos(angles), jnp.sin(angles)], axis=1)
    cond = jax.nn.silu(features).astype(BF)
    mod = jnp.dot(cond, ada_weight, preferred_element_type=F32) + ada_bias.astype(F32)
    mod = jnp.pad(mod.reshape(images, 6, width), ((0, 0), (0, 2), (0, 0)))
    perm, perm_back, moves = token_tables(cols, strip_tokens)
    conv_a = jnp.pad(conv_attn.reshape(9, width).astype(F32), ((0, 7), (0, 0)))
    conv_f = jnp.pad(conv_ffn.reshape(9, hidden), ((0, 7), (0, 0)))
    low = out_grad.reshape(images, height * cols // 4, out_grad.shape[3])
    held = None
    behind = None
    for image in range(images):
        pieces = [
            lax.dynamic_slice(sources, (place ^ at, image, 0, 0), (1, 1, strip_tokens, width)).reshape(
                strip_tokens, width
            )
            for at in range(strips)
        ]
        if behind is not None:
            behind, *pieces = lax.optimization_barrier((behind, *pieces))
            held = attention_forward_call(
                rank, image - 1, images, behind, mod, qkv_weight, conv_a, perm, moves, held
            )
        behind = tuple(
            piece if at == 0 else swap_strips(piece, at) for at, piece in enumerate(pieces)
        )
    xp, co, qkv, mix, stat = attention_forward_call(
        rank, images - 1, images, behind, mod, qkv_weight, conv_a, perm, moves, held
    )
    res, gmid, gmod_two, big, small = feed_forward_call(
        rank,
        devices,
        xp,
        mix,
        mod,
        low,
        (
            proj_weight,
            fc1_weight,
            fc1_bias.astype(F32)[None],
            fc2_weight,
            fc2_bias.astype(F32)[None],
            down_weight,
            down_bias.astype(F32)[None],
            conv_f,
        ),
        moves,
    )
    split = max(images // 2, 1)
    groups = [(0, split)] + ([(split, images - split)] if images > split else [])
    later = [(image, 1) for image in range(split, images)]
    gqkvs = []
    before = None

    def attention_back(group):
        nonlocal before
        gqkv, before, *final = attention_back_call(
            rank, devices, group, mod, gmid, co, qkv, mix, stat, proj_weight, small, before
        )
        gqkvs.append(gqkv)
        return final

    def conv_attn_back(group, skip):
        *made, gmod_one, d_ca = conv_attn_back_call(
            rank, strips, group[0], skip, group[1], xp, mod, gmid, gqkvs[-1], (qkv_weight, conv_a), perm_back, moves
        )
        mods.append(gmod_one)
        convs.append(d_ca)
        return made

    mods, convs = [], []
    big = scatter_stage(big, steps[0], devices)
    mod, big = lax.optimization_barrier((mod, big))
    final = attention_back(groups[0])
    for group in steps[1:-1]:
        big = scatter_stage(big, group, devices)
    mod, big, gqkvs = lax.optimization_barrier((mod, big, gqkvs))
    made = conv_attn_back(groups[0], 0)
    big = scatter_stage(big, steps[-1], devices)
    mod, big, made = lax.optimization_barrier((mod, big, made))
    gathered = lax.all_gather(big, AXES, axis=0, tiled=True)
    outs = [sent_strips(made)]
    for group in groups[1:]:
        final = attention_back(group)
    rest, outs = lax.optimization_barrier((final[0], outs))
    stage = 0
    for at, group in enumerate(later):
        made = conv_attn_back(group, at)
        if stage < len(steps) - 1:
            rest = scatter_stage(rest, steps[stage], devices)
            stage += 1
        mod, rest, made, outs = lax.optimization_barrier((mod, rest, made, outs))
        outs.append(sent_strips(made))
    for group in steps[stage:]:
        rest = scatter_stage(rest, group, devices)
    halves = [groups[0], *later]
    grad_mod = jnp.concatenate([jnp.concatenate(mods, axis=0)[:, :2], gmod_two[:, :4]], axis=1)
    grad_mod = grad_mod.transpose(1, 0, 2).reshape(6 * images, width)
    per_tile = 8 // images
    late = jnp.concatenate(
        [
            sum(convs).astype(BF),
            jnp.pad(grad_mod, ((0, -grad_mod.shape[0] % 8), (0, 0))),
            jnp.pad(
                jnp.concatenate([cond] * per_tile, axis=0), ((0, 0), (0, width - cond.shape[1]))
            ),
        ],
        axis=0,
    )
    share = rest.shape[0]
    rest = jnp.concatenate([rest, late], axis=0)
    grad_latents = None
    for at, group in enumerate(steps[:0:-1]):
        rest = gather_stage(rest, group, devices)
        if at == 0:
            rest, outs, gathered = lax.optimization_barrier((rest, outs, gathered))
        if at == len(steps) - 2:
            finished = finish_big_call(gathered, devices, order, hidden, width)
            for (first, count), pieces in zip(halves[:2], outs):
                grad_latents = finish_latents_call(rank, images, first, pieces, grad_latents)
            rest, grad_latents, finished = lax.optimization_barrier((rest, grad_latents, finished))
    grad_fc1, grad_fc2, grad_down = finished
    for (first, count), pieces in zip(halves[2:], outs[2:]):
        grad_latents = finish_latents_call(rank, images, first, pieces, grad_latents)
    rest = rest.reshape(devices // 2, -1, width)
    other = exchange(rest, steps[0][0], devices)
    other, grad_latents = lax.optimization_barrier((other, grad_latents))
    (
        grad_qkv,
        grad_proj,
        grad_conv_ffn,
        grad_fc1b,
        grad_fc2b,
        grad_downb,
        grad_conv_attn,
        grad_ada,
        grad_ada_bias,
    ) = finish_rest_call(rank, rest, other, share, width, images, cond.shape[1])
    return (
        res.reshape(out_grad.shape),
        grad_latents.reshape(latents.shape),
        grad_ada,
        grad_ada_bias,
        grad_conv_attn,
        grad_qkv,
        grad_proj,
        grad_fc1,
        grad_fc1b,
        grad_conv_ffn,
        grad_fc2,
        grad_fc2b,
        grad_down,
        grad_downb,
    )


def solution(mesh):
    strip = P("wide", "narrow", None, None)
    image = P(AXES, None, None, None)
    in_specs = (strip, P("wide"), image) + (P(),) * 12
    out_specs = (image, strip) + (P(),) * 12
    return jax.shard_map(shards, mesh=mesh, in_specs=in_specs, out_specs=out_specs, check_vma=False)
```
